32 devices in a mesh: wide: 8 (over z, x), narrow: 4 (over y, core).
Axes of the slice: x: 2, y: 2, z: 4, core: 2. Of those that a mesh axis runs over, the one named last changes fastest.
Arguments:
- tokens: bfloat16 [32, 512, 768], P(('wide', 'narrow')), may hold values from -6 to 6
- lengths: int32 [32, 2], P(('wide', 'narrow')), may hold values from 8 to 504, as said below
- buckets: int32 [1023], replicated, may hold values from 0 to 255
- query_weight: bfloat16 [768, 768], P(('wide', 'narrow')), may hold values from -0.21875 to 0.21875
- query_bias: bfloat16 [768], P(('wide', 'narrow')), may hold values from -3 to 3
- key_weight: bfloat16 [768, 768], P(('wide', 'narrow')), may hold values from -0.21875 to 0.21875
- key_bias: bfloat16 [768], P(('wide', 'narrow')), may hold values from -3 to 3
- value_weight: bfloat16 [768, 768], P(('wide', 'narrow')), may hold values from -0.21875 to 0.21875
- value_bias: bfloat16 [768], P(('wide', 'narrow')), may hold values from -3 to 3
- output_weight: bfloat16 [768, 768], P(('wide', 'narrow')), may hold values from -0.875 to 0.875
- output_bias: bfloat16 [768], P(('wide', 'narrow')), may hold values from -3 to 3
- relative_table: bfloat16 [256, 768], P(('wide', 'narrow')), may hold values from -6 to 6
- first_gain: bfloat16 [768], P(('wide', 'narrow')), may hold values from 0.5 to 1.5
- first_shift: bfloat16 [768], P(('wide', 'narrow')), may hold values from -3 to 3
- inner_weight: bfloat16 [768, 3072], P(('wide', 'narrow')), may hold values from -0.21875 to 0.21875
- inner_bias: bfloat16 [3072], P(('wide', 'narrow')), may hold values from -3 to 3
- outer_weight: bfloat16 [3072, 768], P(('wide', 'narrow')), may hold values from -0.109375 to 0.109375
- outer_bias: bfloat16 [768], P(('wide', 'narrow')), may hold values from -3 to 3
- second_gain: bfloat16 [768], P(('wide', 'narrow')), may hold values from 0.5 to 1.5
- second_shift: bfloat16 [768], P(('wide', 'narrow')), may hold values from -3 to 3
- cotangent: bfloat16 [32, 512, 768], P(('wide', 'narrow')), may hold values from -6 to 6
Outputs:
- layer_out: bfloat16 [32, 512, 768], P(('wide', 'narrow'))
- tokens_grad: float32 [32, 512, 768], P(('wide', 'narrow'))
- query_weight_grad: float32 [768, 768], P(('wide', 'narrow'))
- query_bias_grad: float32 [768], P(('wide', 'narrow'))
- key_weight_grad: float32 [768, 768], P(('wide', 'narrow'))
- key_bias_grad: float32 [768], P(('wide', 'narrow'))
- value_weight_grad: float32 [768, 768], P(('wide', 'narrow'))
- value_bias_grad: float32 [768], P(('wide', 'narrow'))
- output_weight_grad: float32 [768, 768], P(('wide', 'narrow'))
- output_bias_grad: float32 [768], P(('wide', 'narrow'))
- relative_table_grad: float32 [256, 768], P(('wide', 'narrow'))
- first_gain_grad: float32 [768], P(('wide', 'narrow'))
- first_shift_grad: float32 [768], P(('wide', 'narrow'))
- inner_weight_grad: float32 [768, 3072], P(('wide', 'narrow'))
- inner_bias_grad: float32 [3072], P(('wide', 'narrow'))
- outer_weight_grad: float32 [3072, 768], P(('wide', 'narrow'))
- outer_bias_grad: float32 [768], P(('wide', 'narrow'))
- second_gain_grad: float32 [768], P(('wide', 'narrow'))
- second_shift_grad: float32 [768], P(('wide', 'narrow'))
The draws below stay inside these ranges and needn't reach their ends.
Inputs may be any that keep to these rules, and one draw needn't show every extreme that they name: lengths[p, 0] is pair p's query length, 8 to 64; lengths[p, 1] is its passage length, 112 or more; the two sum to at most 512, and to exactly 512 in some pair of every draw, whose query length is 8.
All inputs are finite; a program needn't handle non-finite values.
Results may differ from the reference program's by a relative error of at most 0.025.
Values may be sent and summed in bfloat16 or wider, within the bound.
No kernel may reach another device: no remote copies, remote signals or barrier semaphores. Data moves between devices by JAX's collectives and lax.ppermute only.
A program may use at most 256 MiB of HBM per device.

```python
import math
import jax
import jax.numpy as jnp
from jax import lax

D = 768
HD = 64
FF = 3072
NB = 256
L = 512
PAIRS = 32


def draw_lengths(key, part):
    query_seed, divisor_seed, factor_seed, chosen_seed = jax.random.split(jax.random.fold_in(key, 11), 4)
    query_len = jax.random.randint(query_seed, (PAIRS,), 8, L // 8 + 1)
    chosen = jax.random.randint(chosen_seed, (), 0, PAIRS)
    is_chosen = jnp.arange(PAIRS) == chosen
    query_len = jnp.where(is_chosen, 8, query_len)
    free_room = L - query_len
    divisor = 1 + jax.random.randint(divisor_seed, (PAIRS,), 0, 4) * jax.random.randint(factor_seed, (PAIRS,), 0, 2)
    passage = jnp.maximum(free_room // divisor, 1)
    passage = jnp.where(is_chosen, free_room, passage)
    return jnp.stack([query_len, passage], axis=1).astype(jnp.int32)


def set_ends(result, rng, low, largest):
    spot = [jax.random.randint(jax.random.fold_in(rng, axis), (), 0, length) for axis, length in enumerate(result.shape)]
    longest = result.shape.index(max(result.shape))
    neighbour = spot[:longest] + [(spot[longest] + 1) % result.shape[longest]] + spot[longest + 1:]
    return result.at[tuple(spot)].set(low).at[tuple(neighbour)].set(largest)


def spiked(entries, rng, source, target, blocks, factor):
    owner, partner = [(jnp.arange(entries.shape[axis_at]) // (entries.shape[axis_at] // blocks)).reshape([-1 if axis == axis_at else 1 for axis in range(entries.ndim)]) for axis_at in (source, target)]
    chosen = jax.random.permutation(rng, blocks)[partner]
    strong = (owner == chosen) | (owner == (partner + blocks // 2) % blocks)
    return jnp.where(strong, factor * entries, entries)


def block_scale(stream_key, extent, pieces, low, top_value):
    def one(position, blocks):
        heights = jax.random.uniform(jax.random.fold_in(jax.random.fold_in(stream_key, 6), position), (blocks,), jnp.float32, low / len(pieces), top_value / len(pieces))
        return jnp.repeat(jnp.exp(heights), extent[position] // blocks).reshape((-1,) + (1,) * (len(extent) - position - 1))

    level = one(*pieces[0])
    for cut in pieces[1:]:
        level = level * one(*cut)
    return level


def bell_draw(key, shape, width, limit, cuts=(), held_as=jnp.bfloat16):
    factor_of = block_scale(key, shape, cuts, -0.22, 0.18) if cuts else 1.0
    array = jax.random.normal(key, shape, jnp.float32) * width * factor_of
    return jnp.minimum(jnp.maximum(array, -limit), limit).astype(held_as)


def noise_with(key, shape, deviation, reach, pieces, heavy, dtype=jnp.bfloat16):
    entries = deviation * jax.random.normal(key, shape, jnp.float32)
    if pieces:
        entries = entries * block_scale(key, shape, pieces, -0.22, 0.18)
    return jnp.clip(spiked(entries, jax.random.fold_in(key, 3), *heavy), -reach, reach).astype(dtype)


def setup_inputs(seed: int = 0) -> dict:
    arg_keys = jax.random.split(jax.random.key(seed), 22)
    tokens = noise_with(arg_keys[0], (PAIRS, L, D), 1.0, 6.0, ((0, 32),), (0, 2, 32, 2.75))
    lengths = draw_lengths(jax.random.fold_in(arg_keys[21], 71), 0)
    buckets = set_ends(jax.random.randint(arg_keys[2], (2 * L - 1,), 0, NB), jax.random.fold_in(arg_keys[2], 1), 0, NB - 1).astype(jnp.int32)
    query_weight = bell_draw(arg_keys[3], (D, D), D ** -0.5, 0.21875, ((0, 32),))
    query_bias = bell_draw(arg_keys[4], (D,), 0.5, 3.0, ((0, 32),))
    key_weight = bell_draw(arg_keys[5], (D, D), D ** -0.5, 0.21875, ((0, 32),))
    key_bias = bell_draw(arg_keys[6], (D,), 0.5, 3.0, ((0, 32),))
    value_weight = bell_draw(arg_keys[7], (D, D), D ** -0.5, 0.21875, ((0, 32),))
    value_bias = bell_draw(arg_keys[8], (D,), 0.5, 3.0, ((0, 32),))
    output_weight = bell_draw(arg_keys[9], (D, D), (D // 16) ** -0.5, 0.875, ((0, 32),))
    output_bias = bell_draw(arg_keys[10], (D,), 0.5, 3.0, ((0, 32),))
    relative_table = bell_draw(arg_keys[11], (NB, D), 1.0, 6.0, ((0, 32),))
    first_gain = jnp.clip(1.0 + 0.1 * jax.random.normal(arg_keys[12], (D,), jnp.float32), 0.5, 1.5).astype(jnp.bfloat16)
    first_shift = bell_draw(arg_keys[13], (D,), 0.5, 3.0, ((0, 32),))
    inner_weight = bell_draw(arg_keys[14], (D, FF), D ** -0.5, 0.21875, ((0, 32),))
    inner_bias = bell_draw(arg_keys[15], (FF,), 0.5, 3.0, ((0, 32),))
    outer_weight = bell_draw(arg_keys[16], (FF, D), FF ** -0.5, 0.109375, ((0, 32),))
    outer_bias = bell_draw(arg_keys[17], (D,), 0.5, 3.0, ((0, 32),))
    second_gain = jnp.clip(1.0 + 0.1 * jax.random.normal(arg_keys[18], (D,), jnp.float32), 0.5, 1.5).astype(jnp.bfloat16)
    second_shift = bell_draw(arg_keys[19], (D,), 0.5, 3.0, ((0, 32),))
    cotangent = bell_draw(arg_keys[20], (PAIRS, L, D), 1.0, 6.0, ((0, 32),))
    return dict(tokens=tokens, lengths=lengths, buckets=buckets, query_weight=query_weight, query_bias=query_bias, key_weight=key_weight, key_bias=key_bias, value_weight=value_weight, value_bias=value_bias, output_weight=output_weight, output_bias=output_bias, relative_table=relative_table, first_gain=first_gain, first_shift=first_shift, inner_weight=inner_weight, inner_bias=inner_bias, outer_weight=outer_weight, outer_bias=outer_bias, second_gain=second_gain, second_shift=second_shift, cotangent=cotangent)


EPSILON = 1e-05
MASKED = -1000000000.0

@jax.custom_vjp
def low(v):
    return lax.optimization_barrier(v.astype(jnp.bfloat16)).astype(jnp.float32)

@jax.custom_vjp
def low_back(v):
    return v

def low_keep(v):
    return (low(v), None)

def low_pass(kept, grad):
    return (grad,)

def back_keep(v):
    return (v, None)

def back_low(kept, grad):
    return (low(grad),)
low.defvjp(low_keep, low_pass)
low_back.defvjp(back_keep, back_low)

def shifted_scores(scores, sequence_rows):
    leading = scores.shape[:-2]
    span_width = 2 * sequence_rows - 1
    padded = jnp.pad(scores, [(0, 0)] * len(leading) + [(0, 0), (0, 1)])
    flattened = padded.reshape(leading + (2 * sequence_rows * sequence_rows,))
    flattened = flattened[..., sequence_rows - 1:sequence_rows - 1 + sequence_rows * span_width]
    return flattened.reshape(leading + (sequence_rows, span_width))[..., :sequence_rows]

def project(row_block, matrix, vector):
    return jnp.dot(row_block, matrix, precision=lax.Precision.HIGHEST) + vector

def normalize(hidden, gain_vec, shift_vec):
    centered = hidden - lax.optimization_barrier(jnp.mean(hidden, axis=-1, keepdims=True))
    inverse = lax.rsqrt(lax.optimization_barrier(jnp.mean(centered * centered, axis=-1, keepdims=True)) + EPSILON)
    return centered * inverse * gain_vec + shift_vec

def forward(tokens_float, params, lengths, buckets):
    query_mat, query_vec, key_mat, key_vec, value_mat, value_vec, output_mat, output_vec, table_all, gain_one, shift_one, inner_mat, inner_vec, outer_mat, outer_vec, gain_two, shift_two = params
    pair_count, sequence_rows, model_width = tokens_float.shape
    head_count = model_width // HD
    score_scale = (3.0 * HD) ** (-0.5)
    highest_precision_setting = lax.Precision.HIGHEST
    flat_tokens = tokens_float.reshape(-1, model_width)
    head_shape = (pair_count, sequence_rows, head_count, HD)
    query_rows = low_back(low(project(flat_tokens, query_mat, query_vec))).reshape(head_shape)
    key_rows = low_back(low(project(flat_tokens, key_mat, key_vec))).reshape(head_shape)
    value_rows = low_back(low(project(flat_tokens, value_mat, value_vec))).reshape(head_shape)
    pos_query = low(project(table_all, query_mat, query_vec))
    pos_key = low(project(table_all, key_mat, key_vec))
    reversed_buckets = buckets[::-1]
    onehot = (reversed_buckets[:, None] == jnp.arange(table_all.shape[0])[None, :]).astype(jnp.float32)
    key_reversed = jnp.dot(onehot, pos_key, precision=highest_precision_setting).reshape(-1, head_count, HD)
    query_reversed = jnp.dot(onehot, pos_query, precision=highest_precision_setting).reshape(-1, head_count, HD)
    totals = lengths[:, 0] + lengths[:, 1]

    def attend_one(query_sequence, key_sequence, value_seq, row_total):
        direct = jnp.einsum('ihd,jhd->hij', query_sequence, key_sequence, precision=highest_precision_setting)
        content_scores = shifted_scores(jnp.einsum('qbx,ubx->bqu', query_sequence, key_reversed, precision=highest_precision_setting), sequence_rows)
        position_scores = jnp.swapaxes(shifted_scores(jnp.einsum('ten,xen->etx', key_sequence, query_reversed, precision=highest_precision_setting), sequence_rows), 1, 2)
        raw_scores = low_back(direct + content_scores + position_scores)
        valid_keys = jnp.arange(sequence_rows) < row_total
        scores = jnp.where(valid_keys[None, None, :], raw_scores * score_scale, MASKED)
        attention = low(jax.nn.softmax(scores, axis=-1))
        return low_back(low(jnp.einsum('hij,jhd->ihd', attention, value_seq, precision=highest_precision_setting)))

    def attend_group(carried, inputs):
        return (carried, jax.vmap(attend_one)(*inputs))
    group_size = math.gcd(pair_count, 4)
    grouped = tuple((member.reshape((pair_count // group_size, group_size) + member.shape[1:]) for member in (query_rows, key_rows, value_rows, totals)))
    unused_carry, context = lax.scan(jax.checkpoint(attend_group), jnp.float32(0.0), grouped)
    context = context.reshape(-1, model_width)
    attended = low_back(project(context, output_mat, output_vec))
    first_out = normalize(flat_tokens + attended, gain_one, shift_one)
    inner_pre = low_back(project(low(first_out), inner_mat, inner_vec))
    activated = low(jax.nn.gelu(inner_pre, approximate=False))
    outer_out = low_back(project(activated, outer_mat, outer_vec))
    second_out = normalize(first_out + outer_out, gain_two, shift_two)
    return second_out.reshape(pair_count, sequence_rows, model_width)

def reference(tokens, lengths, buckets, query_weight, query_bias, key_weight, key_bias, value_weight, value_bias, output_weight, output_bias, relative_table, first_gain, first_shift, inner_weight, inner_bias, outer_weight, outer_bias, second_gain, second_shift, cotangent):
    params = tuple((member.astype(jnp.float32) for member in (query_weight, query_bias, key_weight, key_bias, value_weight, value_bias, output_weight, output_bias, relative_table, first_gain, first_shift, inner_weight, inner_bias, outer_weight, outer_bias, second_gain, second_shift)))
    tokens_float = tokens.astype(jnp.float32)

    def forward_fn(tokens_in, params_in):
        return forward(tokens_in, params_in, lengths, buckets)
    layer_out, pullback = jax.vjp(forward_fn, tokens_float, params)
    tokens_grad, param_grads = pullback(cotangent.astype(jnp.float32))
    return (layer_out.astype(jnp.bfloat16), tokens_grad, param_grads[0], param_grads[1], param_grads[2], param_grads[3], param_grads[4], param_grads[5], param_grads[6], param_grads[7], param_grads[8], param_grads[9], param_grads[10], param_grads[11], param_grads[12], param_grads[13], param_grads[14], param_grads[15], param_grads[16])
```

```python
import jax
import jax.numpy as jnp
import numpy as np
from jax import lax
from jax.experimental import pallas as pl
from jax.experimental.pallas import tpu as pltpu
from jax.sharding import PartitionSpec as P

HD = 64
EPSILON = 1e-05
MASKED = -1000000000.0
AXES = ("wide", "narrow")
BF = jnp.bfloat16
F32 = jnp.float32
NT = (((1,), (1,)), ((), ()))
NN = (((1,), (0,)), ((), ()))
TN = (((0,), (0,)), ((), ()))


def dot(left, right, dims):
    return lax.dot_general(left, right, dims, preferred_element_type=F32)


def attend_kernel(tot_ref, q_ref, k_ref, v_ref, kr_ref, qr_ref, c_ref, p_ref, t_ref, *, rows, tile):
    span = rows + tile
    scale = (3.0 * HD) ** (-0.5)
    lane = lax.broadcasted_iota(jnp.int32, (1, 128), 1)
    valid = lax.broadcasted_iota(jnp.int32, (1, rows), 1) < tot_ref[0]

    def skewed(grid_scores):
        return pltpu.roll(grid_scores, span - (tile - 1), 1, stride=1, stride_axis=0)[:, :rows]

    for head in range(2):
        mine = (lane >= head * HD) & (lane < (head + 1) * HD)
        q = jnp.where(mine, q_ref[...], 0).astype(BF)
        k = jnp.where(mine, k_ref[...], 0).astype(BF)
        for b in range(rows // tile):
            sl = slice(b * tile, (b + 1) * tile)
            low = rows - tile - b * tile
            t_ref[sl, :] = skewed(dot(k[sl], qr_ref[low : low + span, :], NT))
        for b in range(rows // tile):
            sl = slice(b * tile, (b + 1) * tile)
            low = rows - tile - b * tile
            raw = (
                dot(q[sl], k_ref[...], NT)
                + skewed(dot(q[sl], kr_ref[low : low + span, :], NT))
                + t_ref[:, sl].T
            )
            scores = jnp.where(valid, raw * scale, MASKED)
            top = jnp.max(scores, axis=-1, keepdims=True)
            expd = jnp.exp(scores - top)
            probs = (expd * (1.0 / jnp.sum(expd, axis=-1, keepdims=True))).astype(BF)
            p_ref[head, sl, :] = probs
            ctx = dot(probs, v_ref[...], NN).astype(BF)
            if head == 0:
                c_ref[sl, :] = ctx
            else:
                c_ref[sl, :] = jnp.where(mine, ctx, c_ref[sl, :])


def attend(total, q, k, v, kr, qr):
    rows, width = q.shape
    groups = width // 128
    cols = lambda r: pl.BlockSpec((r, 128), lambda p: (0, p))
    return pl.pallas_call(
        lambda *refs: attend_kernel(*refs, rows=rows, tile=rows),
        grid=(groups,),
        in_specs=[pl.BlockSpec(memory_space=pltpu.SMEM)]
        + [cols(rows)] * 3
        + [cols(2 * rows)] * 2,
        out_specs=[cols(rows), pl.BlockSpec((2, rows, rows), lambda p: (p, 0, 0))],
        out_shape=[
            jax.ShapeDtypeStruct((rows, width), BF),
            jax.ShapeDtypeStruct((2 * groups, rows, rows), BF),
        ],
        scratch_shapes=[pltpu.VMEM((rows, rows), F32)],
        name="attend",
    )(total, q, k, v, kr, qr)


def attend_back_kernel(
    q_ref, k_ref, v_ref, kr_ref, qr_ref, dc_ref, p_ref,
    dq_ref, dk_ref, dv_ref, dkr_ref, dqr_ref, ds_ref, dvt_ref, *, rows, tile,
):
    span = rows + tile
    scale = (3.0 * HD) ** (-0.5)
    lane = lax.broadcasted_iota(jnp.int32, (1, 128), 1)
    flip = (
        lax.broadcasted_iota(jnp.int32, (tile, tile), 0)
        + lax.broadcasted_iota(jnp.int32, (tile, tile), 1)
        == tile - 1
    ).astype(BF)
    dkr_ref[...] = jnp.zeros_like(dkr_ref)
    dqr_ref[...] = jnp.zeros_like(dqr_ref)
    zeros = jnp.zeros((tile, tile), F32)

    def unskewed(flipped):
        wide = jnp.concatenate([flipped, zeros], axis=1)
        return pltpu.roll(wide, 0, 1, stride=1, stride_axis=0).astype(BF)

    for head in range(2):
        mine = (lane >= head * HD) & (lane < (head + 1) * HD)
        only = lambda ref: jnp.where(mine, ref[...], 0).astype(BF)
        q, k, dc = only(q_ref), only(k_ref), only(dc_ref)
        dct = dc.astype(F32).T.astype(BF)
        dvt = jnp.zeros((128, rows), F32)
        for b in range(rows // tile):
            sl = slice(b * tile, (b + 1) * tile)
            low = rows - tile - b * tile
            dp = dot(dc[sl], v_ref[...], NT)
            pb = p_ref[head, sl, :]
            p = pb.astype(F32)
            pdp = p * dp
            delta = jnp.sum(pdp, axis=-1, keepdims=True)
            ds = ((pdp - p * delta) * scale).astype(BF)
            ds_ref[sl, :] = ds
            dvt = dvt + dot(dct[:, sl], pb, NN)
            d = unskewed(dot(flip, ds, NN))
            qt = dot(flip, q[sl], NN).T.astype(BF)
            dq = dot(ds, k_ref[...], NN) + dot(
                flip, dot(d, kr_ref[low : low + span, :], NN).astype(BF), NN
            )
            if head == 0:
                dq_ref[sl, :] = dq.astype(BF)
            else:
                dq_ref[sl, :] = jnp.where(mine, dq.astype(BF), dq_ref[sl, :])
            dkr_ref[:, low : low + span] += dot(qt, d, NN)
        if head == 0:
            dvt_ref[...] = dvt
        else:
            dv_ref[...] = (dvt_ref[...] + dvt).T.astype(BF)
        for b in range(rows // tile):
            sl = slice(b * tile, (b + 1) * tile)
            low = rows - tile - b * tile
            dst = dot(flip, ds_ref[:, sl], NT)
            d = unskewed(dst)
            dk = dot(dst.astype(BF), q_ref[...], NN) + dot(d, qr_ref[low : low + span, :], NN)
            dk = dot(flip, dk.astype(BF), NN).astype(BF)
            if head == 0:
                dk_ref[sl, :] = dk
            else:
                dk_ref[sl, :] = jnp.where(mine, dk, dk_ref[sl, :])
            kt = dot(flip, k[sl], NN).T.astype(BF)
            dqr_ref[:, low : low + span] += dot(kt, d, NN)


def attend_back(q, k, v, kr, qr, dc, probs):
    rows, width = q.shape
    groups = width // 128
    cols = lambda r: pl.BlockSpec((r, 128), lambda p: (0, p))
    turned = pl.BlockSpec((128, 2 * rows), lambda p: (p, 0))
    return pl.pallas_call(
        lambda *refs: attend_back_kernel(*refs, rows=rows, tile=rows // 2),
        grid=(groups,),
        in_specs=[cols(rows)] * 3
        + [cols(2 * rows)] * 2
        + [cols(rows), pl.BlockSpec((2, rows, rows), lambda p: (p, 0, 0))],
        out_specs=[cols(rows)] * 3 + [turned] * 2,
        out_shape=[jax.ShapeDtypeStruct((rows, width), BF)] * 3
        + [jax.ShapeDtypeStruct((width, 2 * rows), F32)] * 2,
        scratch_shapes=[pltpu.VMEM((rows, rows), BF), pltpu.VMEM((128, rows), F32)],
        name="attend_back",
    )(q, k, v, kr, qr, dc, probs)


def gather_rows(block):
    return lax.all_gather(block, AXES, axis=0, tiled=False)


def xor_permute(block, mask, count):
    return lax.ppermute(block, AXES, [(d, d ^ mask) for d in range(count)])


def scatter_sum(blocks, counts, order):
    count = counts[0] * counts[1]
    bits = count.bit_length() - 1
    if counts != (8, 4):
        return lax.psum_scatter(blocks.astype(F32), AXES, scatter_dimension=0, tiled=False)
    me = lax.axis_index("wide") * counts[1] + lax.axis_index("narrow")
    left = list(range(bits - 1, -1, -1))
    value = blocks.reshape((2,) * bits + blocks.shape[1:])
    for position, bit in enumerate(order):
        axis = left.index(bit)
        left.pop(axis)
        own = (me >> bit) & 1
        sent = lax.dynamic_index_in_dim(value, 1 - own, axis, keepdims=False)
        kept = lax.dynamic_index_in_dim(value, own, axis, keepdims=False)
        got = xor_permute(sent, 1 << bit, count)
        value = kept.astype(F32) + got.astype(F32)
        if position + 1 < bits:
            value = value.astype(BF)
    return value


def normalize(hidden, gain_vec, shift_vec):
    centered = hidden - jnp.mean(hidden, axis=-1, keepdims=True)
    inverse = lax.rsqrt(jnp.mean(centered * centered, axis=-1, keepdims=True) + EPSILON)
    normed = centered * inverse
    return (normed * gain_vec + shift_vec, normed, inverse)


def normalize_back(upstream, normed, inverse, gain_vec):
    scaled = upstream * gain_vec
    return inverse * (
        scaled
        - jnp.mean(scaled, axis=-1, keepdims=True)
        - normed * jnp.mean(scaled * normed, axis=-1, keepdims=True)
    )


def gelu_slope(inner_pre):
    return (
        0.5 * (1.0 + lax.erf(inner_pre * 0.7071067811865476))
        + inner_pre * jnp.exp(-0.5 * inner_pre * inner_pre) * 0.3989422804014327
    )


def make_body(counts):
    count = counts[0] * counts[1]

    def body(
        tokens, lengths, buckets,
        query_weight, query_bias, key_weight, key_bias, value_weight, value_bias,
        output_weight, output_bias, relative_table, first_gain, first_shift,
        inner_weight, inner_bias, outer_weight, outer_bias, second_gain, second_shift,
        cotangent,
    ):
        pair_count, rows, width = tokens.shape
        assert pair_count == 1
        own = query_weight.shape[0]
        own_table = relative_table.shape[0]
        fan = inner_weight.shape[1] // width
        own_outer = outer_weight.shape[0]
        vectors = (
            query_bias, key_bias, value_bias, output_bias, first_gain, first_shift,
            outer_bias, second_gain, second_shift, inner_bias,
        )
        sizes = [v.shape[0] for v in vectors]
        vector_row = jnp.concatenate(vectors)
        vector_row = jnp.pad(vector_row, (0, width - vector_row.shape[0])).reshape(1, width)

        def pad8(block):
            return jnp.pad(block, ((0, -block.shape[0] % 8), (0, 0)))

        first_pack = pad8(
            jnp.concatenate([query_weight, key_weight, value_weight, relative_table, vector_row])
        )
        second_pack = jnp.concatenate(
            [output_weight]
            + [inner_weight[:, f * width : (f + 1) * width] for f in range(fan)]
            + [outer_weight]
        )
        first_all = gather_rows(first_pack)
        second_pack, first_all = lax.optimization_barrier((second_pack, first_all))
        second_all = gather_rows(second_pack)
        whole = lambda packed, lo, n: packed[:, lo : lo + n].reshape(count * n, width)
        query_mat = whole(first_all, 0, own)
        key_mat = whole(first_all, own, own)
        value_mat = whole(first_all, 2 * own, own)
        table_all = whole(first_all, 3 * own, own_table)
        vec_all = first_all[:, 3 * own + own_table].astype(F32)
        vecs, at = [], 0
        for size in sizes:
            vecs.append(vec_all[:, at : at + size].reshape(-1))
            at += size
        (query_vec, key_vec, value_vec, output_vec, gain_one, shift_one, outer_vec, gain_two,
         shift_two, inner_vec) = vecs
        output_mat = whole(second_all, 0, own)
        inner_mats = [whole(second_all, (1 + f) * own, own) for f in range(fan)]
        outer_mat = whole(second_all, (1 + fan) * own, own_outer)

        flat = tokens.reshape(rows, width)
        project = lambda a, m, v: dot(a, m, NN) + v
        q = project(flat, query_mat, query_vec).astype(BF)
        k = project(flat, key_mat, key_vec).astype(BF)
        v = project(flat, value_mat, value_vec).astype(BF)
        pos_query = project(table_all, query_mat, query_vec).astype(BF)
        pos_key = project(table_all, key_mat, key_vec).astype(BF)
        reversed_buckets = jnp.pad(buckets[::-1], (0, 1), constant_values=-1)
        onehot = (reversed_buckets[:, None] == jnp.arange(table_all.shape[0])[None, :]).astype(BF)
        kr = dot(onehot, pos_key, NN).astype(BF)
        qr = dot(onehot, pos_query, NN).astype(BF)
        total = lengths[:, 0] + lengths[:, 1]
        context, probs = attend(total, q, k, v, kr, qr)

        attended = project(context, output_mat, output_vec)
        first_out, first_normed, first_inverse = normalize(
            flat.astype(F32) + attended, gain_one, shift_one
        )
        first_low = first_out.astype(BF)
        inner_pre = [
            project(first_low, inner_mats[f], inner_vec[f * width : (f + 1) * width])
            for f in range(fan)
        ]
        activated = [jax.nn.gelu(x, approximate=False).astype(BF) for x in inner_pre]
        outer_mats = [outer_mat[f * width : (f + 1) * width] for f in range(fan)]
        outer_out = outer_vec + sum(dot(activated[f], outer_mats[f], NN) for f in range(fan))
        second_out, second_normed, second_inverse = normalize(
            first_out + outer_out, gain_two, shift_two
        )
        layer_out = second_out.astype(BF).reshape(pair_count, rows, width)

        upstream = cotangent.reshape(rows, width).astype(F32)
        second_gain_grad = jnp.sum(upstream * second_normed, axis=0)
        second_shift_grad = jnp.sum(upstream, axis=0)
        second_grad = normalize_back(upstream, second_normed, second_inverse, gain_two)
        outer_grad = second_grad.astype(BF)
        outer_bias_grad = jnp.sum(outer_grad.astype(F32), axis=0)
        outer_weight_grad = jnp.concatenate(
            [dot(activated[f], outer_grad, TN).astype(BF) for f in range(fan)]
        )
        inner_grad = [
            (dot(outer_grad, outer_mats[f], NT) * gelu_slope(inner_pre[f])).astype(BF)
            for f in range(fan)
        ]
        inner_bias_grad = jnp.concatenate([jnp.sum(g.astype(F32), axis=0) for g in inner_grad])
        inner_weight_grad = [dot(first_low, g, TN).astype(BF) for g in inner_grad]
        first_total = second_grad + sum(
            dot(inner_grad[f], inner_mats[f], NT) for f in range(fan)
        )
        first_gain_grad = jnp.sum(first_total * first_normed, axis=0)
        first_shift_grad = jnp.sum(first_total, axis=0)
        first_grad = normalize_back(first_total, first_normed, first_inverse, gain_one)
        attended_grad = first_grad.astype(BF)
        output_bias_grad = jnp.sum(attended_grad.astype(F32), axis=0)
        output_weight_grad = dot(context, attended_grad, TN).astype(BF)
        context_grad = dot(attended_grad, output_mat, NT).astype(BF)

        split = lambda grad: grad.reshape(count, grad.shape[0] // count, width)
        outer_sum = scatter_sum(split(outer_weight_grad), counts, (0, 1, 2, 3, 4))
        inner_sum = scatter_sum(
            jnp.concatenate([split(g) for g in inner_weight_grad] + [split(output_weight_grad)], 1),
            counts, (0, 2, 1, 3, 4),
        )

        dq, dk, dv, dkr, dqr = attend_back(q, k, v, kr, qr, context_grad, probs)
        pos_key_grad = dot(onehot, dkr.astype(BF), (((0,), (1,)), ((), ())))
        pos_query_grad = dot(onehot, dqr.astype(BF), (((0,), (1,)), ((), ())))
        pos_key_low = pos_key_grad.astype(BF)
        pos_query_low = pos_query_grad.astype(BF)
        query_weight_grad = dot(flat, dq, TN) + dot(table_all, pos_query_low, TN)
        key_weight_grad = dot(flat, dk, TN) + dot(table_all, pos_key_low, TN)
        value_weight_grad = dot(flat, dv, TN)
        column = lambda a: jnp.sum(a.astype(F32), axis=0)
        query_bias_grad = column(dq) + column(pos_query_grad)
        key_bias_grad = column(dk) + column(pos_key_grad)
        value_bias_grad = column(dv)
        table_grad = dot(pos_query_low, query_mat, NT) + dot(pos_key_low, key_mat, NT)
        tokens_grad = (
            first_grad + dot(dq, query_mat, NT) + dot(dk, key_mat, NT) + dot(dv, value_mat, NT)
        )

        vector_grads = [
            query_bias_grad, key_bias_grad, value_bias_grad, output_bias_grad, first_gain_grad,
            first_shift_grad, outer_bias_grad, second_gain_grad, second_shift_grad, inner_bias_grad,
        ]
        vector_block = jnp.concatenate([g.reshape(count, -1) for g in vector_grads], axis=1)
        vector_block = jnp.pad(vector_block, ((0, 0), (0, width - vector_block.shape[1])))
        last = jnp.concatenate(
            [split(g.astype(BF)) for g in (query_weight_grad, key_weight_grad, value_weight_grad, table_grad)]
            + [vector_block.astype(BF).reshape(count, 1, width)],
            axis=1,
        )
        last = jnp.pad(last, ((0, 0), (0, -last.shape[1] % 8), (0, 0)))
        last_sum = scatter_sum(last, counts, (0, 1, 2, 3, 4))

        inner_out = jnp.concatenate([inner_sum[f * own : (f + 1) * own] for f in range(fan)], axis=1)
        output_out = inner_sum[fan * own : (fan + 1) * own]
        vector_sum = last_sum[3 * own + own_table]
        vec_out, at = [], 0
        for size in sizes:
            vec_out.append(vector_sum[at : at + size])
            at += size
        (qb, kb, vb, ob, g1, s1, outb, g2, s2, inb) = vec_out
        return (
            layer_out, tokens_grad.reshape(pair_count, rows, width),
            last_sum[:own], qb, last_sum[own : 2 * own], kb, last_sum[2 * own : 3 * own], vb,
            output_out, ob, last_sum[3 * own : 3 * own + own_table], g1, s1,
            inner_out, inb, outer_sum, outb, g2, s2,
        )

    return body


def solution(mesh):
    counts = (mesh.shape["wide"], mesh.shape["narrow"])
    rows3, rows2, rows1 = P(AXES, None, None), P(AXES, None), P(AXES)
    params = (
        rows2, rows1, rows2, rows1, rows2, rows1, rows2, rows1, rows2, rows1, rows1,
        rows2, rows1, rows2, rows1, rows1, rows1,
    )
    return jax.shard_map(
        make_body(counts),
        mesh=mesh,
        in_specs=(rows3, rows2, P()) + params + (rows3,),
        out_specs=(rows3, rows3) + params,
        check_vma=False,
    )
```

```python
import jax
import jax.numpy as jnp
from jax import lax
from jax.experimental import pallas as pl
from jax.experimental.pallas import tpu as pltpu
from jax.sharding import PartitionSpec as P

HD = 64
EPSILON = 1e-05
MASKED = -1000000000.0
AXES = ("wide", "narrow")
BF = jnp.bfloat16
F32 = jnp.float32
NT = (((1,), (1,)), ((), ()))
NN = (((1,), (0,)), ((), ()))
TN = (((0,), (0,)), ((), ()))


def dot(left, right, dims):
    return lax.dot_general(left, right, dims, preferred_element_type=F32)


def attend_kernel(tot_ref, q_ref, k_ref, v_ref, kr_ref, qr_ref, c_ref, p_ref, t_ref, *, rows, tile):
    span = rows + tile
    scale = (3.0 * HD) ** (-0.5)
    lane = lax.broadcasted_iota(jnp.int32, (1, 128), 1)
    valid = lax.broadcasted_iota(jnp.int32, (1, rows), 1) < tot_ref[0]

    def skewed(grid_scores):
        return pltpu.roll(grid_scores, span - (tile - 1), 1, stride=1, stride_axis=0)[:, :rows]

    for head in range(2):
        mine = (lane >= head * HD) & (lane < (head + 1) * HD)
        q = jnp.where(mine, q_ref[...], 0).astype(BF)
        k = jnp.where(mine, k_ref[...], 0).astype(BF)
        for b in range(rows // tile):
            sl = slice(b * tile, (b + 1) * tile)
            low = rows - tile - b * tile
            t_ref[sl, :] = skewed(dot(k[sl], qr_ref[low : low + span, :], NT))
        for b in range(rows // tile):
            sl = slice(b * tile, (b + 1) * tile)
            low = rows - tile - b * tile
            raw = (
                dot(q[sl], k_ref[...], NT)
                + skewed(dot(q[sl], kr_ref[low : low + span, :], NT))
                + t_ref[:, sl].T
            )
            scores = jnp.where(valid, raw * scale, MASKED)
            top = jnp.max(scores, axis=-1, keepdims=True)
            expd = jnp.exp(scores - top)
            probs = (expd * (1.0 / jnp.sum(expd, axis=-1, keepdims=True))).astype(BF)
            p_ref[head, sl, :] = probs
            ctx = dot(probs, v_ref[...], NN).astype(BF)
            if head == 0:
                c_ref[sl, :] = ctx
            else:
                c_ref[sl, :] = jnp.where(mine, ctx, c_ref[sl, :])


def attend(total, q, k, v, kr, qr):
    rows, width = q.shape
    groups = width // 128
    cols = lambda r: pl.BlockSpec((r, 128), lambda p: (0, p))
    return pl.pallas_call(
        lambda *refs: attend_kernel(*refs, rows=rows, tile=rows),
        grid=(groups,),
        in_specs=[pl.BlockSpec(memory_space=pltpu.SMEM)]
        + [cols(rows)] * 3
        + [cols(2 * rows)] * 2,
        out_specs=[cols(rows), pl.BlockSpec((2, rows, rows), lambda p: (p, 0, 0))],
        out_shape=[
            jax.ShapeDtypeStruct((rows, width), BF),
            jax.ShapeDtypeStruct((2 * groups, rows, rows), BF),
        ],
        scratch_shapes=[pltpu.VMEM((rows, rows), F32)],
        cost_estimate=pl.CostEstimate(
            flops=25 << 30, bytes_accessed=12 << 20, transcendentals=12 * rows * rows
        ),
        name="attend",
    )(total, q, k, v, kr, qr)


def attend_back_kernel(
    q_ref, k_ref, v_ref, kr_ref, qr_ref, dc_ref, p_ref, *refs, rows, tile,
):
    d_ref, dpos_ref, ds_ref, dvt_ref = refs[-4:]
    dq_ref, dk_ref, dv_ref = d_ref.at[0], d_ref.at[1], d_ref.at[2]
    dqr_ref, dkr_ref = dpos_ref.at[0], dpos_ref.at[1]
    span = rows + tile
    scale = (3.0 * HD) ** (-0.5)
    lane = lax.broadcasted_iota(jnp.int32, (1, 128), 1)
    flip = (
        lax.broadcasted_iota(jnp.int32, (tile, tile), 0)
        + lax.broadcasted_iota(jnp.int32, (tile, tile), 1)
        == tile - 1
    ).astype(BF)
    dkr_ref[...] = jnp.zeros_like(dkr_ref)
    dqr_ref[...] = jnp.zeros_like(dqr_ref)
    zeros = jnp.zeros((tile, tile), F32)

    def unskewed(flipped):
        wide = jnp.concatenate([flipped, zeros], axis=1)
        return pltpu.roll(wide, 0, 1, stride=1, stride_axis=0).astype(BF)

    for head in range(2):
        mine = (lane >= head * HD) & (lane < (head + 1) * HD)
        only = lambda ref: jnp.where(mine, ref[...], 0).astype(BF)
        q, k, dc = only(q_ref), only(k_ref), only(dc_ref)
        dct = dc.astype(F32).T.astype(BF)
        dvt = jnp.zeros((128, rows), F32)
        for b in range(rows // tile):
            sl = slice(b * tile, (b + 1) * tile)
            low = rows - tile - b * tile
            dp = dot(dc[sl], v_ref[...], NT)
            pb = p_ref[head, sl, :]
            p = pb.astype(F32)
            pdp = p * dp
            delta = jnp.sum(pdp, axis=-1, keepdims=True)
            ds = ((pdp - p * delta) * scale).astype(BF)
            ds_ref[sl, :] = ds
            dvt = dvt + dot(dct[:, sl], pb, NN)
            d = unskewed(dot(flip, ds, NN))
            qt = dot(flip, q[sl], NN).T.astype(BF)
            dq = dot(ds, k_ref[...], NN) + dot(
                flip, dot(d, kr_ref[low : low + span, :], NN).astype(BF), NN
            )
            if head == 0:
                dq_ref[sl, :] = dq.astype(BF)
            else:
                dq_ref[sl, :] = jnp.where(mine, dq.astype(BF), dq_ref[sl, :])
            dkr_ref[:, low : low + span] += dot(qt, d, NN)
        if head == 0:
            dvt_ref[...] = dvt
        else:
            dv_ref[...] = (dvt_ref[...] + dvt).T.astype(BF)
        for b in range(rows // tile):
            sl = slice(b * tile, (b + 1) * tile)
            low = rows - tile - b * tile
            dst = dot(flip, ds_ref[:, sl], NT)
            d = unskewed(dst)
            dk = dot(dst.astype(BF), q_ref[...], NN) + dot(d, qr_ref[low : low + span, :], NN)
            dk = dot(flip, dk.astype(BF), NN).astype(BF)
            if head == 0:
                dk_ref[sl, :] = dk
            else:
                dk_ref[sl, :] = jnp.where(mine, dk, dk_ref[sl, :])
            kt = dot(flip, k[sl], NN).T.astype(BF)
            dqr_ref[:, low : low + span] += dot(kt, d, NN)


def attend_back(q, k, v, kr, qr, dc, probs, first, groups, before):
    rows, width = q.shape
    cols = lambda r: pl.BlockSpec((r, 128), lambda p: (0, first + p))
    skip = [pl.BlockSpec(memory_space=pl.ANY)] * len(before)
    share = groups / (width // 128)
    return pl.pallas_call(
        lambda *refs: attend_back_kernel(*refs, rows=rows, tile=rows // 2),
        grid=(groups,),
        in_specs=[cols(rows)] * 3
        + [cols(2 * rows)] * 2
        + [cols(rows), pl.BlockSpec((2, rows, rows), lambda p: (first + p, 0, 0))]
        + skip,
        out_specs=[
            pl.BlockSpec((3, rows, 128), lambda p: (0, 0, first + p)),
            pl.BlockSpec((2, 128, 2 * rows), lambda p: (0, first + p, 0)),
        ],
        out_shape=[
            jax.ShapeDtypeStruct((3, rows, width), BF),
            jax.ShapeDtypeStruct((2, width, 2 * rows), F32),
        ],
        scratch_shapes=[pltpu.VMEM((rows, rows), BF), pltpu.VMEM((128, rows), F32)],
        input_output_aliases={7 + i: i for i in range(len(before))},
        cost_estimate=pl.CostEstimate(
            flops=int(42e9 * share), bytes_accessed=int(18e6 * share), transcendentals=0
        ),
        name="attend_back",
    )(q, k, v, kr, qr, dc, probs, *before)


STRIPES = 32
VECTORS = 10


def cost(flops, moved, transcendentals=0):
    return pl.CostEstimate(flops=flops, bytes_accessed=moved, transcendentals=transcendentals)


def big(**extra):
    return pltpu.CompilerParams(vmem_limit_bytes=60 << 20, **extra)


def stripe_marks(width, dtype):
    part = width // STRIPES
    column = lax.broadcasted_iota(jnp.int32, (STRIPES, width), 1)
    stripe = lax.broadcasted_iota(jnp.int32, (STRIPES, width), 0)
    owner = (column >= stripe * part) & (column < stripe * part + part)
    place = lax.broadcasted_iota(jnp.int32, (128, width), 0)
    spot = (lax.broadcasted_iota(jnp.int32, (128, width), 1) % part == place).astype(dtype)
    return owner, spot


def project_kernel(wq_ref, wk_ref, wv_ref, table_ref, vec_ref, x_ref, bucket_ref,
                   q_ref, k_ref, v_ref, kr_ref, qr_ref, vecs_ref, onehot_ref, *, fan):
    step = pl.program_id(0)
    width = x_ref.shape[1]
    span = q_ref.shape[1]
    buckets = onehot_ref.shape[1]

    @pl.when(step == 0)
    def _():
        index = lax.broadcasted_iota(jnp.int32, onehot_ref.shape, 1)
        onehot_ref[...] = (bucket_ref[...] == index).astype(F32).astype(BF)
        owner, spot = stripe_marks(width, BF)
        vecs_ref[...] = jnp.zeros_like(vecs_ref)

        def spread(block, marks, mine):
            return jnp.sum(jnp.where(mine, dot(block, marks, NN), 0.0), axis=0, keepdims=True)

        for i in range(VECTORS - 1):
            lanes = slice(0, 128) if i < 8 else slice(128, 256)
            vecs_ref[i : i + 1, :] = spread(vec_ref[:, i % 8, lanes], spot, owner)
        block = vec_ref[:, (VECTORS - 1) % 8, 128:256]
        part = width * fan // STRIPES
        for f in range(fan):
            column = lax.broadcasted_iota(jnp.int32, (STRIPES, width), 1) + f * width
            stripe = lax.broadcasted_iota(jnp.int32, (STRIPES, width), 0)
            mine = (column >= stripe * part) & (column < stripe * part + part)
            place = lax.broadcasted_iota(jnp.int32, (128, width), 0)
            marks = lax.broadcasted_iota(jnp.int32, (128, width), 1) + f * width
            marks = (marks % part == place).astype(BF)
            row = VECTORS - 1 + f
            vecs_ref[row : row + 1, :] = spread(block, marks, mine)

    x = x_ref[...]
    table = table_ref.reshape(buckets, width)[...]
    columns = pl.ds(pl.multiple_of(step * span, 128), span)
    bias = [vecs_ref[i : i + 1, columns] for i in range(3)]
    mats = [ref.reshape(width, span)[...] for ref in (wq_ref, wk_ref, wv_ref)]
    for i, out in enumerate((q_ref, k_ref, v_ref)):
        out[...] = (dot(x, mats[i], NN) + bias[i]).astype(BF)
    for i, out in ((0, qr_ref), (1, kr_ref)):
        pos = (dot(table, mats[i], NN) + bias[i]).astype(BF)
        out[...] = dot(onehot_ref[...], pos, NN).astype(BF)


def project_all(packed, x, bucket_column, fan):
    rows, width = x.shape
    part = width // STRIPES
    span = 256
    weight = lambda i: pl.BlockSpec((STRIPES, part, span), lambda p: (0, i, p))
    buckets = 8 * STRIPES
    whole = lambda shape: pl.BlockSpec(shape, lambda p: (0,) * len(shape))
    cols = lambda r: pl.BlockSpec((r, span), lambda p: (0, p))
    out = lambda r: jax.ShapeDtypeStruct((r, width), BF)
    return pl.pallas_call(
        lambda *refs: project_kernel(*refs, fan=fan),
        grid=(width // span,),
        in_specs=[weight(0), weight(1), weight(2),
                  pl.BlockSpec((STRIPES, 8, width), lambda p: (0, 3 * part // 8, 0)),
                  pl.BlockSpec((STRIPES, 8, width), lambda p: (0, 3 * part // 8 + 1, 0)),
                  whole((rows, width)), whole((2 * rows, 1))],
        out_specs=[cols(rows)] * 3 + [cols(2 * rows)] * 2 + [whole((16, width))],
        out_shape=[out(rows)] * 3 + [out(2 * rows)] * 2 + [jax.ShapeDtypeStruct((16, width), F32)],
        scratch_shapes=[pltpu.VMEM((2 * rows, buckets), BF)],
        compiler_params=big(),
        cost_estimate=cost(4 << 30, 12 << 20),
        name="project",
    )(packed, packed, packed, packed, packed, x, bucket_column)


def normal_parts(hidden):
    centered = hidden - jnp.mean(hidden, axis=-1, keepdims=True)
    inverse = lax.rsqrt(jnp.mean(centered * centered, axis=-1, keepdims=True) + EPSILON)
    return centered * inverse, inverse


def normal_back(upstream, normed, inverse, gain):
    scaled = upstream * gain
    return inverse * (
        scaled
        - jnp.mean(scaled, axis=-1, keepdims=True)
        - normed * jnp.mean(scaled * normed, axis=-1, keepdims=True)
    )


def forward_kernel(ctx_ref, x_ref, cot_ref, vecs_ref, wo_ref, wi_ref, w2_ref,
                   act_ref, slope_ref, out_ref, og_ref, sg_ref, n1_ref, inv_ref, low_ref, vg_ref,
                   first_ref, acc_ref, *, fan):
    step = pl.program_id(0)
    rows, width = x_ref.shape
    vec = lambda i: vecs_ref[i : i + 1, :]

    @pl.when(step == 0)
    def _():
        attended = dot(ctx_ref[...], wo_ref.reshape(width, width)[...], NN) + vec(3)
        normed, inverse = normal_parts(x_ref[...].astype(F32) + attended)
        n1_ref[...] = normed
        inv_ref[...] = jnp.broadcast_to(inverse, inv_ref.shape)
        first = normed * vec(4) + vec(5)
        first_ref[...] = first
        low_ref[...] = first.astype(BF)
        acc_ref[...] = first + vec(6)

    pre = dot(low_ref[...], wi_ref.reshape(width, width)[...], NN) + vecs_ref[pl.ds(9 + step, 1), :]
    half = 0.5 + 0.5 * lax.erf(pre * 0.7071067811865476)
    act = (pre * half).astype(BF)
    act_ref[...] = act
    slope_ref[...] = (half + pre * (jnp.exp(-0.5 * pre * pre) * 0.3989422804014327)).astype(BF)
    acc_ref[...] += dot(act, w2_ref.reshape(width, width)[...], NN)

    @pl.when(step == fan - 1)
    def _():
        normed, inverse = normal_parts(acc_ref[...])
        out_ref[...] = (normed * vec(7) + vec(8)).astype(BF)
        upstream = cot_ref[...].astype(F32)
        column = lambda a: jnp.sum(a, axis=0, keepdims=True)
        sg = normal_back(upstream, normed, inverse, vec(7))
        sg_ref[...] = sg
        og = sg.astype(BF)
        og_ref[...] = og
        vg_ref[...] = jnp.zeros_like(vg_ref)
        vg_ref[0:1, :] = column(upstream * normed)
        vg_ref[1:2, :] = column(upstream)
        vg_ref[2:3, :] = column(og.astype(F32))


def feed_forward(ctx, x, cot, vecs, packed, fan):
    rows, width = x.shape
    part = width // STRIPES
    whole = lambda shape: pl.BlockSpec(shape, lambda f: (0,) * len(shape))
    chunk = pl.BlockSpec((rows, width), lambda f: (0, f))
    full = whole((rows, width))
    shape = jax.ShapeDtypeStruct
    return pl.pallas_call(
        lambda *refs: forward_kernel(*refs, fan=fan),
        grid=(fan,),
        in_specs=[full, full, full, whole((16, width)),
                  pl.BlockSpec((STRIPES, part, width), lambda f: (0, 2 * fan, 0)),
                  pl.BlockSpec((STRIPES, part, width), lambda f: (0, fan + f, 0)),
                  pl.BlockSpec((STRIPES // fan, part * fan, width), lambda f: (f, 0, 0))],
        out_specs=[chunk, chunk, full, full, full, full, whole((rows, 128)), full, whole((8, width))],
        out_shape=[shape((rows, fan * width), BF), shape((rows, fan * width), BF),
                   shape((rows, width), BF), shape((rows, width), BF), shape((rows, width), F32),
                   shape((rows, width), F32), shape((rows, 128), F32), shape((rows, width), BF),
                   shape((8, width), F32)],
        scratch_shapes=[pltpu.VMEM((rows, width), F32)] * 2,
        compiler_params=big(),
        cost_estimate=cost(12 << 30, 24 << 20),
        name="feed_forward",
    )(ctx, x, cot, vecs, packed, packed, packed)


def halves(grad, own, part):
    blocks = grad.reshape((grad.shape[0] // (2 * part), 2, part, grad.shape[1]))
    even, odd = blocks[:, 0], blocks[:, 1]
    return jnp.where(own == 0, even, odd).astype(BF), jnp.where(own == 0, odd, even).astype(BF)


def outer_grad_kernel(own_ref, act_ref, og_ref, keep_ref, send_ref):
    grad = dot(act_ref[...], og_ref[...], TN)
    keep_ref[...], send_ref[...] = halves(grad, own_ref[0], keep_ref.shape[1])


def outer_grads(own, act, og, fan):
    rows, width = og.shape
    part = width // STRIPES * fan
    block = pl.BlockSpec((STRIPES // 2 // fan, part, width), lambda f: (f, 0, 0))
    half = jax.ShapeDtypeStruct((STRIPES // 2, part, width), BF)
    return pl.pallas_call(
        outer_grad_kernel,
        grid=(fan,),
        in_specs=[pl.BlockSpec(memory_space=pltpu.SMEM),
                  pl.BlockSpec((rows, width), lambda f: (0, f)),
                  pl.BlockSpec((rows, width), lambda f: (0, 0))],
        out_specs=[block, block],
        out_shape=[half, half],
        compiler_params=big(),
        cost_estimate=cost(3 << 30, 9 << 20),
        name="outer_grads",
    )(own, act, og)


def backward_kernel(own_ref, og_ref, sg_ref, n1_ref, inv_ref, low_ref, ctx_ref, vecs_ref, slope_ref,
                    w2_ref, wi_ref, wo_ref, keep_ref, send_ref, cg_ref, fg_ref, vg_ref,
                    acc_ref, lowt_ref, *, fan):
    step = pl.program_id(0)
    rows, width = og_ref.shape
    part = width // STRIPES
    column = lambda a: jnp.sum(a, axis=0, keepdims=True)

    @pl.when(step == 0)
    def _():
        acc_ref[...] = sg_ref[...]
        lowt_ref[...] = low_ref[...].T
        vg_ref[...] = jnp.zeros_like(vg_ref)

    @pl.when(step < fan)
    def _():
        ig = dot(og_ref[...], w2_ref.reshape(width, width)[...], NT) * slope_ref[...].astype(F32)
        ig = ig.astype(BF)
        acc_ref[...] += dot(ig, wi_ref.reshape(width, width)[...], NT)
        vg_ref[pl.ds(step, 1), :] = column(ig.astype(F32))
        keep_ref[...], send_ref[...] = halves(dot(lowt_ref[...], ig, NN), own_ref[0], part)

    @pl.when(step == fan)
    def _():
        total = acc_ref[...]
        normed = n1_ref[...]
        vg_ref[4:5, :] = column(total * normed)
        vg_ref[5:6, :] = column(total)
        fg = normal_back(total, normed, inv_ref[:, 0:1], vecs_ref[4:5, :])
        fg_ref[...] = fg
        ag = fg.astype(BF)
        vg_ref[6:7, :] = column(ag.astype(F32))
        cg_ref[...] = dot(ag, wo_ref.reshape(width, width)[...], NT).astype(BF)
        keep_ref[...], send_ref[...] = halves(dot(ctx_ref[...], ag, TN), own_ref[0], part)


def feed_back(own, og, sg, n1, inv, low, ctx, vecs, slope, packed, fan):
    rows, width = og.shape
    part = width // STRIPES
    whole = lambda shape: pl.BlockSpec(shape, lambda f: (0,) * len(shape))
    full = whole((rows, width))
    last = lambda f: jnp.minimum(f, fan - 1)
    block = pl.BlockSpec((STRIPES // 2, part, width), lambda f: (0, f, 0))
    shape = jax.ShapeDtypeStruct
    half = shape((STRIPES // 2, part * (fan + 1), width), BF)
    return pl.pallas_call(
        lambda *refs: backward_kernel(*refs, fan=fan),
        grid=(fan + 1,),
        in_specs=[pl.BlockSpec(memory_space=pltpu.SMEM), full, full, full, whole((rows, 128)), full, full,
                  whole((16, width)), pl.BlockSpec((rows, width), lambda f: (0, last(f))),
                  pl.BlockSpec((STRIPES // fan, part * fan, width), lambda f: (last(f), 0, 0)),
                  pl.BlockSpec((STRIPES, part, width), lambda f: (0, fan + last(f), 0)),
                  pl.BlockSpec((STRIPES, part, width), lambda f: (0, 2 * fan, 0))],
        out_specs=[block, block, full, full, whole((8, width))],
        out_shape=[half, half, shape((rows, width), BF), shape((rows, width), F32), shape((8, width), F32)],
        scratch_shapes=[pltpu.VMEM((rows, width), F32), pltpu.VMEM((width, rows), BF)],
        compiler_params=big(),
        cost_estimate=cost(14 << 30, 26 << 20),
        name="feed_back",
    )(own, og, sg, n1, inv, low, ctx, vecs, slope, packed, packed, packed)


def project_back_kernel(own_ref, d_ref, dpos_ref, w_ref, table_ref, x_ref, fg_ref, vg1_ref, vg2_ref,
                        bucket_ref, keep_ref, send_ref, tg_ref,
                        xt_ref, tt_ref, onehot_ref, pos_ref, vec_ref, tab_ref, bias_ref, *, fan):
    step = pl.program_id(0)
    rows, width = x_ref.shape
    buckets = onehot_ref.shape[1]
    part = width // STRIPES
    own = own_ref[0]
    column = lambda a: jnp.sum(a, axis=0, keepdims=True)

    @pl.when(step == 0)
    def _():
        xt_ref[...] = x_ref[...].T
        tt_ref[...] = table_ref.reshape(buckets, width)[...].T
        index = lax.broadcasted_iota(jnp.int32, onehot_ref.shape, 1)
        onehot_ref[...] = (bucket_ref[...] == index).astype(F32).astype(BF)
        tg_ref[...] = fg_ref[...]
        tab_ref[...] = jnp.zeros_like(tab_ref)

    @pl.when(step < 3)
    def _():
        d = d_ref[0]
        w = w_ref.reshape(width, width)[...]
        tg_ref[...] += dot(d, w, NT)
        pos_ref[...] = jnp.zeros_like(pos_ref)

        @pl.when(step < 2)
        def _():
            turned = dot(dpos_ref[0].astype(BF), onehot_ref[...], NN)
            pos_ref[...] = turned.T
            tab_ref[...] += dot(pos_ref[...].astype(BF), w, NT)

        bias_ref[pl.ds(step, 1), :] = column(d.astype(F32)) + column(pos_ref[...])
        grad = dot(xt_ref[...], d, NN) + dot(tt_ref[...], pos_ref[...].astype(BF), NN)
        keep_ref[...], send_ref[...] = halves(grad, own, part)

    @pl.when(step == 3)
    def _():
        vec_ref[...] = jnp.zeros_like(vec_ref)
        owner, spot = stripe_marks(width, BF)

        def cut(row, marks, mine):
            return dot(jnp.where(mine, jnp.broadcast_to(row, mine.shape), 0.0).astype(BF), marks, NT)

        grads = [bias_ref[0:1, :], bias_ref[1:2, :], bias_ref[2:3, :], vg2_ref[6:7, :], vg2_ref[4:5, :],
                 vg2_ref[5:6, :], vg1_ref[2:3, :], vg1_ref[0:1, :], vg1_ref[1:2, :]]
        for i, row in enumerate(grads):
            lanes = slice(0, 128) if i < 8 else slice(128, 256)
            vec_ref[:, i % 8, lanes] = cut(row, spot, owner)
        broad = width * fan // STRIPES
        total = jnp.zeros((STRIPES, 128), F32)
        for f in range(fan):
            column_at = lax.broadcasted_iota(jnp.int32, (STRIPES, width), 1) + f * width
            stripe = lax.broadcasted_iota(jnp.int32, (STRIPES, width), 0)
            mine = (column_at >= stripe * broad) & (column_at < stripe * broad + broad)
            place = lax.broadcasted_iota(jnp.int32, (128, width), 0)
            marks = lax.broadcasted_iota(jnp.int32, (128, width), 1) + f * width
            total += cut(vg2_ref[f : f + 1, :], (marks % broad == place).astype(BF), mine)
        vec_ref[:, (VECTORS - 1) % 8, 128:256] = total
        blocks = tab_ref[...].reshape((STRIPES // 2, 2, 8, width))
        vectors = vec_ref[...].reshape((STRIPES // 2, 2, 8, width))
        zero = jnp.zeros((STRIPES // 2, part - 16, width), BF)
        for out, pick in ((keep_ref, own == 0), (send_ref, own != 0)):
            out[:, 0:8] = jnp.where(pick, blocks[:, 0], blocks[:, 1]).astype(BF)
            out[:, 8:16] = jnp.where(pick, vectors[:, 0], vectors[:, 1]).astype(BF)
            out[:, 16:part] = zero


def project_back(own, d, dpos, packed, x, fg, vg1, vg2, bucket_column, fan):
    rows, width = x.shape
    part = width // STRIPES
    buckets = 8 * STRIPES
    whole = lambda shape: pl.BlockSpec(shape, lambda g: (0,) * len(shape))
    block = pl.BlockSpec((STRIPES // 2, part, width), lambda g: (0, g, 0))
    shape = jax.ShapeDtypeStruct
    half = shape((STRIPES // 2, part * 4, width), BF)
    return pl.pallas_call(
        lambda *refs: project_back_kernel(*refs, fan=fan),
        grid=(4,),
        in_specs=[pl.BlockSpec(memory_space=pltpu.SMEM),
                  pl.BlockSpec((1, rows, width), lambda g: (jnp.minimum(g, 2), 0, 0)),
                  pl.BlockSpec((1, width, 2 * rows), lambda g: (jnp.minimum(g, 1), 0, 0)),
                  pl.BlockSpec((STRIPES, part, width), lambda g: (0, jnp.minimum(g, 2), 0)),
                  pl.BlockSpec((STRIPES, 8, width), lambda g: (0, 3 * part // 8, 0)),
                  whole((rows, width)), whole((rows, width)), whole((8, width)), whole((8, width)),
                  whole((2 * rows, 1))],
        out_specs=[block, block, whole((rows, width))],
        out_shape=[half, half, shape((rows, width), F32)],
        scratch_shapes=[pltpu.VMEM((width, rows), BF), pltpu.VMEM((width, buckets), BF),
                        pltpu.VMEM((2 * rows, buckets), BF), pltpu.VMEM((buckets, width), F32),
                        pltpu.VMEM((STRIPES, 8, width), F32), pltpu.VMEM((buckets, width), F32),
                        pltpu.VMEM((8, width), F32)],
        compiler_params=big(),
        cost_estimate=cost(6 << 30, 20 << 20),
        name="project_back",
    )(own, d, dpos, packed, packed, x, fg, vg1, vg2, bucket_column)


def hop_kernel(bits_ref, keep_a, keep_b, got_a, got_b, keep_ref, send_ref):
    keep_ref[...] = (keep_a[...].astype(F32) + got_a[...].astype(F32)).astype(BF)
    send_ref[...] = (keep_b[...].astype(F32) + got_b[...].astype(F32)).astype(BF)


def hop(own, keep, got, low_bits):
    count, rows, width = keep.shape

    def at(flip):
        def index(i, own_ref):
            bit = own_ref[0] if not flip else 1 - own_ref[0]
            high = (i >> low_bits) << (low_bits + 1)
            return (high | (bit << low_bits) | (i & ((1 << low_bits) - 1)), 0, 0)
        return pl.BlockSpec((1, rows, width), index)

    out = pl.BlockSpec((1, rows, width), lambda i, own_ref: (i, 0, 0))
    half = jax.ShapeDtypeStruct((count // 2, rows, width), BF)
    return pl.pallas_call(
        hop_kernel,
        grid_spec=pltpu.PrefetchScalarGridSpec(
            num_scalar_prefetch=1,
            grid=(count // 2,),
            in_specs=[at(False), at(True), at(False), at(True)],
            out_specs=[out, out],
        ),
        out_shape=[half, half],
        compiler_params=big(),
        cost_estimate=cost(keep.size, 6 * keep.size),
        name="hop",
    )(own, keep, keep, got, got)


def gather_rows(block):
    return lax.all_gather(block, AXES, axis=0, tiled=False)


def xor_permute(block, mask, count):
    return lax.ppermute(block, AXES, [(d, d ^ mask) for d in range(count)])


class Scatter:
    def __init__(self, keep, send, count, bits, own):
        self.keep, self.count, self.bits, self.own = keep, count, list(bits), own
        self.left = [4, 3, 2, 1]
        self.sent = send
        self.got = xor_permute(send, 1, count)

    def step(self, after=None):
        bit = self.bits.pop(0)
        low_bits = len(self.left) - 1 - self.left.index(bit)
        self.left.remove(bit)
        got = self.got if after is None else tie(self.got, after)
        self.keep, self.sent = hop(self.own[bit], self.keep, got, low_bits)
        self.got = xor_permute(self.sent, 1 << bit, self.count)

    def finish(self):
        while self.bits:
            self.step()
        return self.keep[0].astype(F32) + self.got[0].astype(F32)


def tie(value, other):
    return lax.optimization_barrier((value, other))[0]


def scatter_plain(keep, send, parts, count):
    blocks = jnp.stack([keep, send], axis=1).reshape((STRIPES,) + keep.shape[1:])
    sums, at = [], 0
    for part in parts:
        whole = blocks[:, at : at + part]
        rows = STRIPES * part
        flat = whole.reshape(count, rows // count, whole.shape[2])
        sums.append(lax.psum_scatter(flat.astype(F32), AXES, scatter_dimension=0, tiled=False))
        at += part
    return sums


def make_body(counts):
    count = counts[0] * counts[1]
    direct = counts == (8, 4)

    def body(
        tokens, lengths, buckets,
        query_weight, query_bias, key_weight, key_bias, value_weight, value_bias,
        output_weight, output_bias, relative_table, first_gain, first_shift,
        inner_weight, inner_bias, outer_weight, outer_bias, second_gain, second_shift,
        cotangent,
    ):
        rows, width = tokens.shape[1:]
        fan = inner_weight.shape[1] // width
        vectors = (
            query_bias, key_bias, value_bias, output_bias, first_gain, first_shift,
            outer_bias, second_gain, second_shift, inner_bias,
        )
        first_mats = (query_weight, key_weight, value_weight, relative_table)
        second_mats = [outer_weight]
        second_mats += [inner_weight[:, f * width : (f + 1) * width] for f in range(fan)]
        second_mats += [output_weight]

        def vector_rows(pieces):
            lead = pieces[0].shape[:-1]
            tile = jnp.zeros(lead + (8, width), BF)
            for i, piece in enumerate(pieces):
                lane = 0 if i < 8 else 128
                tile = tile.at[..., i % 8, lane : lane + piece.shape[-1]].set(piece)
            return tile

        if direct:
            first_all = gather_rows(jnp.concatenate(first_mats + (vector_rows(vectors),)))
            second_all = gather_rows(jnp.concatenate(second_mats))
        else:
            whole = lambda block: lax.all_gather(block, AXES, axis=0, tiled=True)
            striped = lambda block: whole(block).reshape(STRIPES, -1, width)
            spread = [whole(v).reshape(STRIPES, -1) for v in vectors]
            first_all = jnp.concatenate(
                [striped(m) for m in first_mats] + [vector_rows(spread)], axis=1
            )
            second_all = jnp.concatenate([striped(m) for m in second_mats], axis=1)

        me = lax.axis_index("wide") * counts[1] + lax.axis_index("narrow")
        own = [((me >> bit) & 1).astype(jnp.int32).reshape(1) for bit in range(5)]
        if not direct:
            own = [jnp.zeros((1,), jnp.int32)] * 5
        flat = tokens.reshape(rows, width)
        bucket_column = jnp.pad(buckets[::-1], (0, 1), constant_values=-1).reshape(-1, 1)
        q, k, v, kr, qr, vecs = project_all(first_all, flat, bucket_column, fan)
        total = lengths[0, 0:1] + lengths[0, 1:2]
        context, probs = attend(total, q, k, v, kr, qr)
        cot = cotangent.reshape(rows, width)
        act, slope, layer_out, og, sg, n1, inv, low, vg1 = feed_forward(
            context, flat, cot, vecs, second_all, fan
        )
        outer_keep, outer_send = outer_grads(own[0], act, og, fan)
        og = tie(og, outer_send)
        inner_keep, inner_send, context_grad, fg, vg2 = feed_back(
            own[0], og, sg, n1, inv, low, context, vecs, slope, second_all, fan
        )
        groups = width // 128
        third = groups // 3
        back = lambda dc, i, before: attend_back(
            q, k, v, kr, qr, dc, probs, i * third, third, before
        )
        if direct:
            outer = Scatter(outer_keep, outer_send, count, (1, 2, 3, 4), own)
            outer.step(context_grad)
            inner = Scatter(inner_keep, inner_send, count, (2, 1, 3, 4), own)
            grads = back(tie(context_grad, outer.sent), 0, ())
            inner.step(grads[0])
            grads = back(tie(context_grad, inner.sent), 1, grads)
            outer.step(grads[0])
            grads = back(tie(context_grad, outer.sent), 2, grads)
            inner.step(grads[0])
            d, dpos = tie(tuple(grads), inner.sent)
        else:
            grads = ()
            for i in range(3):
                grads = back(context_grad, i, grads)
            d, dpos = grads
        last_keep, last_send, tokens_grad = project_back(
            own[0], d, dpos, first_all, flat, fg, vg1, vg2, bucket_column, fan
        )

        part = width // STRIPES
        if direct:
            last = Scatter(last_keep, last_send, count, (1, 2, 3, 4), own)
            outer_out, inner_sum, last_sum = outer.finish(), inner.finish(), last.finish()
            inner_parts = [inner_sum[f * part : (f + 1) * part] for f in range(fan + 1)]
            query_out, key_out, value_out = [last_sum[i * part : (i + 1) * part] for i in range(3)]
            table_out = last_sum[3 * part : 3 * part + 8]
            tile = last_sum[3 * part + 8 : 3 * part + 16]
            pieces = [
                tile[i % 8, (0 if i < 8 else 128) :][: piece.shape[0]]
                for i, piece in enumerate(vectors)
            ]
        else:
            (outer_out,) = scatter_plain(outer_keep, outer_send, (fan * part,), count)
            inner_parts = scatter_plain(inner_keep, inner_send, (part,) * (fan + 1), count)
            query_out, key_out, value_out, table_out, _ = scatter_plain(
                last_keep, last_send, (part,) * 3 + (8, part - 8), count
            )
            blocks = jnp.stack([last_keep, last_send], axis=1).reshape(STRIPES, -1, width)
            tile = blocks[:, 3 * part + 8 : 3 * part + 16].astype(F32)
            pieces = []
            for i, piece in enumerate(vectors):
                lane = 0 if i < 8 else 128
                length = piece.shape[0] * count // STRIPES
                line = tile[:, i % 8, lane : lane + length].reshape(-1)
                pieces.append(lax.psum_scatter(line, AXES, scatter_dimension=0, tiled=True))
        inner_out = jnp.concatenate(inner_parts[:fan], axis=1)
        output_out = inner_parts[fan]
        (qb, kb, vb, ob, g1, s1, outb, g2, s2, inb) = pieces
        return (
            layer_out.reshape(tokens.shape), tokens_grad.reshape(tokens.shape),
            query_out, qb, key_out, kb, value_out, vb, output_out, ob, table_out, g1, s1,
            inner_out, inb, outer_out, outb, g2, s2,
        )

    return body


def solution(mesh):
    counts = (mesh.shape["wide"], mesh.shape["narrow"])
    rows3, rows2, rows1 = P(AXES, None, None), P(AXES, None), P(AXES)
    params = (
        rows2, rows1, rows2, rows1, rows2, rows1, rows2, rows1, rows2, rows1, rows1,
        rows2, rows1, rows2, rows1, rows1, rows1,
    )
    return jax.shard_map(
        make_body(counts),
        mesh=mesh,
        in_specs=(rows3, rows2, P()) + params + (rows3,),
        out_specs=(rows3, rows3) + params,
        check_vma=False,
    )
```

```python
import jax
import jax.numpy as jnp
from jax import lax
from jax.experimental import pallas as pl
from jax.experimental.pallas import tpu as pltpu
from jax.sharding import PartitionSpec as P

HD = 64
EPSILON = 1e-05
MASKED = -1000000000.0
AXES = ("wide", "narrow")
BF = jnp.bfloat16
F32 = jnp.float32
NT = (((1,), (1,)), ((), ()))
NN = (((1,), (0,)), ((), ()))
TN = (((0,), (0,)), ((), ()))


def dot(left, right, dims):
    return lax.dot_general(left, right, dims, preferred_element_type=F32)


def attend_kernel(tot_ref, q_ref, k_ref, v_ref, kr_ref, qr_ref, c_ref, p_ref, t_ref, *, rows, tile):
    span = rows + tile
    scale = (3.0 * HD) ** (-0.5)
    lane = lax.broadcasted_iota(jnp.int32, (1, 128), 1)
    valid = lax.broadcasted_iota(jnp.int32, (1, rows), 1) < tot_ref[0]

    def skewed(grid_scores):
        return pltpu.roll(grid_scores, span - (tile - 1), 1, stride=1, stride_axis=0)[:, :rows]

    for head in range(2):
        mine = (lane >= head * HD) & (lane < (head + 1) * HD)
        q = jnp.where(mine, q_ref[...], 0).astype(BF)
        k = jnp.where(mine, k_ref[...], 0).astype(BF)
        for b in range(rows // tile):
            sl = slice(b * tile, (b + 1) * tile)
            low = rows - tile - b * tile
            t_ref[sl, :] = skewed(dot(k[sl], qr_ref[low : low + span, :], NT))
        for b in range(rows // tile):
            sl = slice(b * tile, (b + 1) * tile)
            low = rows - tile - b * tile
            raw = (
                dot(q[sl], k_ref[...], NT)
                + skewed(dot(q[sl], kr_ref[low : low + span, :], NT))
                + t_ref[:, sl].T
            )
            scores = jnp.where(valid, raw * scale, MASKED)
            top = jnp.max(scores, axis=-1, keepdims=True)
            expd = jnp.exp(scores - top)
            probs = (expd * (1.0 / jnp.sum(expd, axis=-1, keepdims=True))).astype(BF)
            p_ref[head, sl, :] = probs
            ctx = dot(probs, v_ref[...], NN).astype(BF)
            if head == 0:
                c_ref[sl, :] = ctx
            else:
                c_ref[sl, :] = jnp.where(mine, ctx, c_ref[sl, :])


def attend(total, q, k, v, kr, qr):
    rows, width = q.shape
    groups = width // 128
    cols = lambda r: pl.BlockSpec((r, 128), lambda p: (0, p))
    return pl.pallas_call(
        lambda *refs: attend_kernel(*refs, rows=rows, tile=rows),
        grid=(groups,),
        in_specs=[pl.BlockSpec(memory_space=pltpu.SMEM)]
        + [cols(rows)] * 3
        + [cols(2 * rows)] * 2,
        out_specs=[cols(rows), pl.BlockSpec((2, rows, rows), lambda p: (p, 0, 0))],
        out_shape=[
            jax.ShapeDtypeStruct((rows, width), BF),
            jax.ShapeDtypeStruct((2 * groups, rows, rows), BF),
        ],
        scratch_shapes=[pltpu.VMEM((rows, rows), F32)],
        cost_estimate=pl.CostEstimate(
            flops=25 << 30, bytes_accessed=12 << 20, transcendentals=12 * rows * rows
        ),
        name="attend",
    )(total, q, k, v, kr, qr)


def attend_back_kernel(
    q_ref, k_ref, v_ref, kr_ref, qr_ref, dc_ref, p_ref, *refs, rows, tile,
):
    d_ref, dpos_ref, ds_ref, dvt_ref = refs[-4:]
    dq_ref, dk_ref, dv_ref = d_ref.at[0], d_ref.at[1], d_ref.at[2]
    dqr_ref, dkr_ref = dpos_ref.at[0], dpos_ref.at[1]
    span = rows + tile
    scale = (3.0 * HD) ** (-0.5)
    lane = lax.broadcasted_iota(jnp.int32, (1, 128), 1)
    flip = (
        lax.broadcasted_iota(jnp.int32, (tile, tile), 0)
        + lax.broadcasted_iota(jnp.int32, (tile, tile), 1)
        == tile - 1
    ).astype(BF)
    dkr_ref[...] = jnp.zeros_like(dkr_ref)
    dqr_ref[...] = jnp.zeros_like(dqr_ref)
    zeros = jnp.zeros((tile, tile), F32)

    def unskewed(flipped):
        wide = jnp.concatenate([flipped, zeros], axis=1)
        return pltpu.roll(wide, 0, 1, stride=1, stride_axis=0).astype(BF)

    for head in range(2):
        mine = (lane >= head * HD) & (lane < (head + 1) * HD)
        only = lambda ref: jnp.where(mine, ref[...], 0).astype(BF)
        q, k, dc = only(q_ref), only(k_ref), only(dc_ref)
        dct = dc.astype(F32).T.astype(BF)
        dvt = jnp.zeros((128, rows), F32)
        for b in range(rows // tile):
            sl = slice(b * tile, (b + 1) * tile)
            low = rows - tile - b * tile
            dp = dot(dc[sl], v_ref[...], NT)
            pb = p_ref[head, sl, :]
            p = pb.astype(F32)
            pdp = p * dp
            delta = jnp.sum(pdp, axis=-1, keepdims=True)
            ds = ((pdp - p * delta) * scale).astype(BF)
            ds_ref[sl, :] = ds
            dvt = dvt + dot(dct[:, sl], pb, NN)
            d = unskewed(dot(flip, ds, NN))
            qt = dot(flip, q[sl], NN).T.astype(BF)
            dq = dot(ds, k_ref[...], NN) + dot(
                flip, dot(d, kr_ref[low : low + span, :], NN).astype(BF), NN
            )
            if head == 0:
                dq_ref[sl, :] = dq.astype(BF)
            else:
                dq_ref[sl, :] = jnp.where(mine, dq.astype(BF), dq_ref[sl, :])
            dkr_ref[:, low : low + span] += dot(qt, d, NN)
        if head == 0:
            dvt_ref[...] = dvt
        else:
            dv_ref[...] = (dvt_ref[...] + dvt).T.astype(BF)
        for b in range(rows // tile):
            sl = slice(b * tile, (b + 1) * tile)
            low = rows - tile - b * tile
            dst = dot(flip, ds_ref[:, sl], NT)
            d = unskewed(dst)
            dk = dot(dst.astype(BF), q_ref[...], NN) + dot(d, qr_ref[low : low + span, :], NN)
            dk = dot(flip, dk.astype(BF), NN).astype(BF)
            if head == 0:
                dk_ref[sl, :] = dk
            else:
                dk_ref[sl, :] = jnp.where(mine, dk, dk_ref[sl, :])
            kt = dot(flip, k[sl], NN).T.astype(BF)
            dqr_ref[:, low : low + span] += dot(kt, d, NN)


def attend_back(q, k, v, kr, qr, dc, probs, first, groups, before):
    rows, width = q.shape
    cols = lambda r: pl.BlockSpec((r, 128), lambda p: (0, first + p))
    skip = [pl.BlockSpec(memory_space=pl.ANY)] * len(before)
    share = groups / (width // 128)
    return pl.pallas_call(
        lambda *refs: attend_back_kernel(*refs, rows=rows, tile=rows // 2),
        grid=(groups,),
        in_specs=[cols(rows)] * 3
        + [cols(2 * rows)] * 2
        + [cols(rows), pl.BlockSpec((2, rows, rows), lambda p: (first + p, 0, 0))]
        + skip,
        out_specs=[
            pl.BlockSpec((3, rows, 128), lambda p: (0, 0, first + p)),
            pl.BlockSpec((2, 128, 2 * rows), lambda p: (0, first + p, 0)),
        ],
        out_shape=[
            jax.ShapeDtypeStruct((3, rows, width), BF),
            jax.ShapeDtypeStruct((2, width, 2 * rows), F32),
        ],
        scratch_shapes=[pltpu.VMEM((rows, rows), BF), pltpu.VMEM((128, rows), F32)],
        input_output_aliases={7 + i: i for i in range(len(before))},
        cost_estimate=pl.CostEstimate(
            flops=int(42e9 * share), bytes_accessed=int(18e6 * share), transcendentals=0
        ),
        name="attend_back",
    )(q, k, v, kr, qr, dc, probs, *before)


STRIPES = 32
VECTORS = 10


def cost(flops, moved, transcendentals=0):
    return pl.CostEstimate(flops=flops, bytes_accessed=moved, transcendentals=transcendentals)


def big(**extra):
    return pltpu.CompilerParams(vmem_limit_bytes=60 << 20, **extra)


def stripe_marks(width, dtype):
    part = width // STRIPES
    column = lax.broadcasted_iota(jnp.int32, (STRIPES, width), 1)
    stripe = lax.broadcasted_iota(jnp.int32, (STRIPES, width), 0)
    owner = (column >= stripe * part) & (column < stripe * part + part)
    place = lax.broadcasted_iota(jnp.int32, (128, width), 0)
    spot = (lax.broadcasted_iota(jnp.int32, (128, width), 1) % part == place).astype(dtype)
    return owner, spot


def pack_kernel(*refs, mats, vectors, fan):
    first_ref, second_ref = refs[-2:]
    at = 0
    for ref in refs[:mats]:
        first_ref[at : at + ref.shape[0], :] = ref[...]
        at += ref.shape[0]
    first_ref[at:, :] = jnp.zeros_like(first_ref[at:, :])
    for i, ref in enumerate(refs[mats : mats + vectors]):
        lane = 0 if i < 8 else 128
        first_ref[at + i % 8 : at + i % 8 + 1, lane : lane + ref.shape[0]] = ref[...].reshape(1, -1)
    outer_ref, inner_ref, output_ref = refs[mats + vectors : mats + vectors + 3]
    width = outer_ref.shape[1]
    at = outer_ref.shape[0]
    second_ref[:at, :] = outer_ref[...]
    for f in range(fan):
        rows = inner_ref.shape[0]
        second_ref[at : at + rows, :] = inner_ref[:, f * width : (f + 1) * width]
        at += rows
    second_ref[at:, :] = output_ref[...]


def pack(mats, vectors, outer, inner, output, fan):
    width = outer.shape[1]
    first = sum(m.shape[0] for m in mats) + 8
    second = outer.shape[0] + fan * inner.shape[0] + output.shape[0]
    return pl.pallas_call(
        lambda *refs: pack_kernel(*refs, mats=len(mats), vectors=len(vectors), fan=fan),
        out_shape=[jax.ShapeDtypeStruct((first, width), BF), jax.ShapeDtypeStruct((second, width), BF)],
        name="pack",
    )(*mats, *vectors, outer, inner, output)


def project_kernel(where_ref, *refs, fan):
    blocks, (x_ref, bucket_ref) = refs[:10], refs[10:12]
    q_ref, k_ref, v_ref, kr_ref, qr_ref, vecs_ref, w_ref, table_ref, onehot_ref, vec_ref = refs[12:]
    step = pl.program_id(0)
    width = x_ref.shape[1]
    span = q_ref.shape[1]
    buckets = onehot_ref.shape[1]
    me = where_ref[0]

    def place(out, near, far):
        for r in range(STRIPES // 2):
            for ref, core in ((near, 0), (far, 1)):
                out[me ^ ((r // 4) * 2 + (r % 4) * 8 + core)] = ref[r]

    for i in range(3):
        place(w_ref.at[i], blocks[2 * i], blocks[2 * i + 1])

    @pl.when(step == 0)
    def _():
        place(table_ref, blocks[6], blocks[7])
        place(vec_ref, blocks[8], blocks[9])
        index = lax.broadcasted_iota(jnp.int32, onehot_ref.shape, 1)
        onehot_ref[...] = (bucket_ref[...] == index).astype(F32).astype(BF)
        owner, spot = stripe_marks(width, BF)
        vecs_ref[...] = jnp.zeros_like(vecs_ref)

        def spread(block, marks, mine):
            return jnp.sum(jnp.where(mine, dot(block, marks, NN), 0.0), axis=0, keepdims=True)

        for i in range(VECTORS - 1):
            lanes = slice(0, 128) if i < 8 else slice(128, 256)
            vecs_ref[i : i + 1, :] = spread(vec_ref[:, i % 8, lanes], spot, owner)
        block = vec_ref[:, (VECTORS - 1) % 8, 128:256]
        part = width * fan // STRIPES
        for f in range(fan):
            column = lax.broadcasted_iota(jnp.int32, (STRIPES, width), 1) + f * width
            stripe = lax.broadcasted_iota(jnp.int32, (STRIPES, width), 0)
            mine = (column >= stripe * part) & (column < stripe * part + part)
            place_at = lax.broadcasted_iota(jnp.int32, (128, width), 0)
            marks = lax.broadcasted_iota(jnp.int32, (128, width), 1) + f * width
            marks = (marks % part == place_at).astype(BF)
            row = VECTORS - 1 + f
            vecs_ref[row : row + 1, :] = spread(block, marks, mine)

    x = x_ref[...]
    table = table_ref.reshape(buckets, width)[...]
    columns = pl.ds(pl.multiple_of(step * span, 128), span)
    bias = [vecs_ref[i : i + 1, columns] for i in range(3)]
    mats = [w_ref.at[i].reshape(width, span)[...] for i in range(3)]
    for i, out in enumerate((q_ref, k_ref, v_ref)):
        out[...] = (dot(x, mats[i], NN) + bias[i]).astype(BF)
    for i, out in ((0, qr_ref), (1, kr_ref)):
        pos = (dot(table, mats[i], NN) + bias[i]).astype(BF)
        out[...] = dot(onehot_ref[...], pos, NN).astype(BF)


def project_all(where, near, far, x, bucket_column, fan):
    rows, width = x.shape
    part = width // STRIPES
    span = 256
    weight = lambda i: [pl.BlockSpec((STRIPES // 2, part, span), lambda p: (0, i, p))] * 2
    small = lambda i: [pl.BlockSpec((STRIPES // 2, 8, width), lambda p: (0, i, 0))] * 2
    buckets = 8 * STRIPES
    whole = lambda shape: pl.BlockSpec(shape, lambda p: (0,) * len(shape))
    cols = lambda r: pl.BlockSpec((r, span), lambda p: (0, p))
    shape = jax.ShapeDtypeStruct
    out = lambda r: shape((r, width), BF)
    return pl.pallas_call(
        lambda *refs: project_kernel(*refs, fan=fan),
        grid=(width // span,),
        in_specs=[pl.BlockSpec(memory_space=pltpu.SMEM)] + weight(0) + weight(1) + weight(2)
        + small(3 * part // 8) + small(3 * part // 8 + 1)
        + [whole((rows, width)), whole((2 * rows, 1))],
        out_specs=[cols(rows)] * 3 + [cols(2 * rows)] * 2
        + [whole((16, width)), pl.BlockSpec((3, STRIPES, part, span), lambda p: (0, 0, 0, p)),
           whole((STRIPES, 8, width))],
        out_shape=[out(rows)] * 3 + [out(2 * rows)] * 2
        + [shape((16, width), F32), shape((3, STRIPES, part, width), BF), shape((STRIPES, 8, width), BF)],
        scratch_shapes=[pltpu.VMEM((2 * rows, buckets), BF), pltpu.VMEM((STRIPES, 8, width), BF)],
        compiler_params=big(),
        cost_estimate=cost(4 << 30, 12 << 20),
        name="project",
    )(where, *([near, far] * 5), x, bucket_column)


def normal_parts(hidden):
    centered = hidden - jnp.mean(hidden, axis=-1, keepdims=True)
    inverse = lax.rsqrt(jnp.mean(centered * centered, axis=-1, keepdims=True) + EPSILON)
    return centered * inverse, inverse


def normal_back(upstream, normed, inverse, gain):
    scaled = upstream * gain
    return inverse * (
        scaled
        - jnp.mean(scaled, axis=-1, keepdims=True)
        - normed * jnp.mean(scaled * normed, axis=-1, keepdims=True)
    )


def forward_kernel(ctx_ref, x_ref, cot_ref, vecs_ref, wo_ref, wi_ref, w2_ref,
                   act_ref, slope_ref, out_ref, og_ref, sg_ref, n1_ref, inv_ref, low_ref, vg_ref,
                   first_ref, acc_ref, *, fan):
    step = pl.program_id(0)
    rows, width = x_ref.shape
    vec = lambda i: vecs_ref[i : i + 1, :]

    @pl.when(step == 0)
    def _():
        attended = dot(ctx_ref[...], wo_ref.reshape(width, width)[...], NN) + vec(3)
        normed, inverse = normal_parts(x_ref[...].astype(F32) + attended)
        n1_ref[...] = normed
        inv_ref[...] = jnp.broadcast_to(inverse, inv_ref.shape)
        first = normed * vec(4) + vec(5)
        first_ref[...] = first
        low_ref[...] = first.astype(BF)
        acc_ref[...] = first + vec(6)

    pre = dot(low_ref[...], wi_ref.reshape(width, width)[...], NN) + vecs_ref[pl.ds(9 + step, 1), :]
    half = 0.5 + 0.5 * lax.erf(pre * 0.7071067811865476)
    act = (pre * half).astype(BF)
    act_ref[...] = act
    slope_ref[...] = (half + pre * (jnp.exp(-0.5 * pre * pre) * 0.3989422804014327)).astype(BF)
    acc_ref[...] += dot(act, w2_ref.reshape(width, width)[...], NN)

    @pl.when(step == fan - 1)
    def _():
        normed, inverse = normal_parts(acc_ref[...])
        out_ref[...] = (normed * vec(7) + vec(8)).astype(BF)
        upstream = cot_ref[...].astype(F32)
        column = lambda a: jnp.sum(a, axis=0, keepdims=True)
        sg = normal_back(upstream, normed, inverse, vec(7))
        sg_ref[...] = sg
        og = sg.astype(BF)
        og_ref[...] = og
        vg_ref[...] = jnp.zeros_like(vg_ref)
        vg_ref[0:1, :] = column(upstream * normed)
        vg_ref[1:2, :] = column(upstream)
        vg_ref[2:3, :] = column(og.astype(F32))


def feed_forward(ctx, x, cot, vecs, packed, fan):
    rows, width = x.shape
    part = width // STRIPES
    whole = lambda shape: pl.BlockSpec(shape, lambda f: (0,) * len(shape))
    chunk = pl.BlockSpec((rows, width), lambda f: (0, f))
    full = whole((rows, width))
    shape = jax.ShapeDtypeStruct
    return pl.pallas_call(
        lambda *refs: forward_kernel(*refs, fan=fan),
        grid=(fan,),
        in_specs=[full, full, full, whole((16, width)),
                  pl.BlockSpec((STRIPES, part, width), lambda f: (0, 2 * fan, 0)),
                  pl.BlockSpec((STRIPES, part, width), lambda f: (0, fan + f, 0)),
                  pl.BlockSpec((STRIPES // fan, part * fan, width), lambda f: (f, 0, 0))],
        out_specs=[chunk, chunk, full, full, full, full, whole((rows, 128)), full, whole((8, width))],
        out_shape=[shape((rows, fan * width), BF), shape((rows, fan * width), BF),
                   shape((rows, width), BF), shape((rows, width), BF), shape((rows, width), F32),
                   shape((rows, width), F32), shape((rows, 128), F32), shape((rows, width), BF),
                   shape((8, width), F32)],
        scratch_shapes=[pltpu.VMEM((rows, width), F32)] * 2,
        compiler_params=big(),
        cost_estimate=cost(12 << 30, 24 << 20),
        name="feed_forward",
    )(ctx, x, cot, vecs, packed, packed, packed)


def halves(grad, own, part):
    blocks = grad.reshape((grad.shape[0] // (2 * part), 2, part, grad.shape[1]))
    even, odd = blocks[:, 0], blocks[:, 1]
    return jnp.where(own == 0, even, odd).astype(BF), jnp.where(own == 0, odd, even).astype(BF)


def outer_grad_kernel(own_ref, act_ref, og_ref, keep_ref, send_ref):
    grad = dot(act_ref[...], og_ref[...], TN)
    keep_ref[...], send_ref[...] = halves(grad, own_ref[1], keep_ref.shape[1])


def outer_grads(own, act, og, fan):
    rows, width = og.shape
    part = width // STRIPES * fan
    block = pl.BlockSpec((STRIPES // 2 // fan, part, width), lambda f: (f, 0, 0))
    half = jax.ShapeDtypeStruct((STRIPES // 2, part, width), BF)
    return pl.pallas_call(
        outer_grad_kernel,
        grid=(fan,),
        in_specs=[pl.BlockSpec(memory_space=pltpu.SMEM),
                  pl.BlockSpec((rows, width), lambda f: (0, f)),
                  pl.BlockSpec((rows, width), lambda f: (0, 0))],
        out_specs=[block, block],
        out_shape=[half, half],
        compiler_params=big(),
        cost_estimate=cost(3 << 30, 9 << 20),
        name="outer_grads",
    )(own, act, og)


def backward_kernel(own_ref, og_ref, sg_ref, n1_ref, inv_ref, low_ref, ctx_ref, vecs_ref, slope_ref,
                    w2_ref, wi_ref, wo_ref, keep_ref, send_ref, cg_ref, fg_ref, vg_ref,
                    acc_ref, lowt_ref, *, fan):
    step = pl.program_id(0)
    rows, width = og_ref.shape
    part = width // STRIPES
    column = lambda a: jnp.sum(a, axis=0, keepdims=True)

    @pl.when(step == 0)
    def _():
        acc_ref[...] = sg_ref[...]
        lowt_ref[...] = low_ref[...].T
        vg_ref[...] = jnp.zeros_like(vg_ref)

    @pl.when(step < fan)
    def _():
        ig = dot(og_ref[...], w2_ref.reshape(width, width)[...], NT) * slope_ref[...].astype(F32)
        ig = ig.astype(BF)
        acc_ref[...] += dot(ig, wi_ref.reshape(width, width)[...], NT)
        vg_ref[pl.ds(step, 1), :] = column(ig.astype(F32))
        keep_ref[...], send_ref[...] = halves(dot(lowt_ref[...], ig, NN), own_ref[1], part)

    @pl.when(step == fan)
    def _():
        total = acc_ref[...]
        normed = n1_ref[...]
        vg_ref[4:5, :] = column(total * normed)
        vg_ref[5:6, :] = column(total)
        fg = normal_back(total, normed, inv_ref[:, 0:1], vecs_ref[4:5, :])
        fg_ref[...] = fg
        ag = fg.astype(BF)
        vg_ref[6:7, :] = column(ag.astype(F32))
        cg_ref[...] = dot(ag, wo_ref.reshape(width, width)[...], NT).astype(BF)
        keep_ref[...], send_ref[...] = halves(dot(ctx_ref[...], ag, TN), own_ref[1], part)


def feed_back(own, og, sg, n1, inv, low, ctx, vecs, slope, packed, fan):
    rows, width = og.shape
    part = width // STRIPES
    whole = lambda shape: pl.BlockSpec(shape, lambda f: (0,) * len(shape))
    full = whole((rows, width))
    last = lambda f: jnp.minimum(f, fan - 1)
    block = pl.BlockSpec((STRIPES // 2, part, width), lambda f: (0, f, 0))
    shape = jax.ShapeDtypeStruct
    half = shape((STRIPES // 2, part * (fan + 1), width), BF)
    return pl.pallas_call(
        lambda *refs: backward_kernel(*refs, fan=fan),
        grid=(fan + 1,),
        in_specs=[pl.BlockSpec(memory_space=pltpu.SMEM), full, full, full, whole((rows, 128)), full, full,
                  whole((16, width)), pl.BlockSpec((rows, width), lambda f: (0, last(f))),
                  pl.BlockSpec((STRIPES // fan, part * fan, width), lambda f: (last(f), 0, 0)),
                  pl.BlockSpec((STRIPES, part, width), lambda f: (0, fan + last(f), 0)),
                  pl.BlockSpec((STRIPES, part, width), lambda f: (0, 2 * fan, 0))],
        out_specs=[block, block, full, full, whole((8, width))],
        out_shape=[half, half, shape((rows, width), BF), shape((rows, width), F32), shape((8, width), F32)],
        scratch_shapes=[pltpu.VMEM((rows, width), F32), pltpu.VMEM((width, rows), BF)],
        compiler_params=big(),
        cost_estimate=cost(14 << 30, 26 << 20),
        name="feed_back",
    )(own, og, sg, n1, inv, low, ctx, vecs, slope, packed, packed, packed)


def project_back_kernel(own_ref, d_ref, dpos_ref, w_ref, table_ref, x_ref, fg_ref, vg1_ref, vg2_ref,
                        bucket_ref, keep_ref, send_ref, tg_ref,
                        xt_ref, tt_ref, onehot_ref, pos_ref, vec_ref, tab_ref, bias_ref, *, fan):
    step = pl.program_id(0)
    rows, width = x_ref.shape
    buckets = onehot_ref.shape[1]
    part = width // STRIPES
    own = own_ref[1]
    column = lambda a: jnp.sum(a, axis=0, keepdims=True)

    @pl.when(step == 0)
    def _():
        xt_ref[...] = x_ref[...].T
        tt_ref[...] = table_ref.reshape(buckets, width)[...].T
        index = lax.broadcasted_iota(jnp.int32, onehot_ref.shape, 1)
        onehot_ref[...] = (bucket_ref[...] == index).astype(F32).astype(BF)
        tg_ref[...] = fg_ref[...]
        tab_ref[...] = jnp.zeros_like(tab_ref)

    @pl.when(step < 3)
    def _():
        d = d_ref[0]
        w = w_ref.at[0].reshape(width, width)[...]
        tg_ref[...] += dot(d, w, NT)
        pos_ref[...] = jnp.zeros_like(pos_ref)

        @pl.when(step < 2)
        def _():
            turned = dot(dpos_ref[0].astype(BF), onehot_ref[...], NN)
            pos_ref[...] = turned.T
            tab_ref[...] += dot(pos_ref[...].astype(BF), w, NT)

        bias_ref[pl.ds(step, 1), :] = column(d.astype(F32)) + column(pos_ref[...])
        grad = dot(xt_ref[...], d, NN) + dot(tt_ref[...], pos_ref[...].astype(BF), NN)
        keep_ref[...], send_ref[...] = halves(grad, own, part)

    @pl.when(step == 3)
    def _():
        vec_ref[...] = jnp.zeros_like(vec_ref)
        owner, spot = stripe_marks(width, BF)

        def cut(row, marks, mine):
            return dot(jnp.where(mine, jnp.broadcast_to(row, mine.shape), 0.0).astype(BF), marks, NT)

        grads = [bias_ref[0:1, :], bias_ref[1:2, :], bias_ref[2:3, :], vg2_ref[6:7, :], vg2_ref[4:5, :],
                 vg2_ref[5:6, :], vg1_ref[2:3, :], vg1_ref[0:1, :], vg1_ref[1:2, :]]
        for i, row in enumerate(grads):
            lanes = slice(0, 128) if i < 8 else slice(128, 256)
            vec_ref[:, i % 8, lanes] = cut(row, spot, owner)
        broad = width * fan // STRIPES
        total = jnp.zeros((STRIPES, 128), F32)
        for f in range(fan):
            column_at = lax.broadcasted_iota(jnp.int32, (STRIPES, width), 1) + f * width
            stripe = lax.broadcasted_iota(jnp.int32, (STRIPES, width), 0)
            mine = (column_at >= stripe * broad) & (column_at < stripe * broad + broad)
            place = lax.broadcasted_iota(jnp.int32, (128, width), 0)
            marks = lax.broadcasted_iota(jnp.int32, (128, width), 1) + f * width
            total += cut(vg2_ref[f : f + 1, :], (marks % broad == place).astype(BF), mine)
        vec_ref[:, (VECTORS - 1) % 8, 128:256] = total
        blocks = tab_ref[...].reshape((STRIPES // 2, 2, 8, width))
        vectors = vec_ref[...].reshape((STRIPES // 2, 2, 8, width))
        zero = jnp.zeros((STRIPES // 2, part - 16, width), BF)
        for out, pick in ((keep_ref, own == 0), (send_ref, own != 0)):
            out[:, 0:8] = jnp.where(pick, blocks[:, 0], blocks[:, 1]).astype(BF)
            out[:, 8:16] = jnp.where(pick, vectors[:, 0], vectors[:, 1]).astype(BF)
            out[:, 16:part] = zero


def project_back(own, d, dpos, mats, table, x, fg, vg1, vg2, bucket_column, fan):
    rows, width = x.shape
    part = width // STRIPES
    buckets = 8 * STRIPES
    whole = lambda shape: pl.BlockSpec(shape, lambda g: (0,) * len(shape))
    block = pl.BlockSpec((STRIPES // 2, part, width), lambda g: (0, g, 0))
    shape = jax.ShapeDtypeStruct
    half = shape((STRIPES // 2, part * 4, width), BF)
    return pl.pallas_call(
        lambda *refs: project_back_kernel(*refs, fan=fan),
        grid=(4,),
        in_specs=[pl.BlockSpec(memory_space=pltpu.SMEM),
                  pl.BlockSpec((1, rows, width), lambda g: (jnp.minimum(g, 2), 0, 0)),
                  pl.BlockSpec((1, width, 2 * rows), lambda g: (jnp.minimum(g, 1), 0, 0)),
                  pl.BlockSpec((1, STRIPES, part, width), lambda g: (jnp.minimum(g, 2), 0, 0, 0)),
                  whole((STRIPES, 8, width)),
                  whole((rows, width)), whole((rows, width)), whole((8, width)), whole((8, width)),
                  whole((2 * rows, 1))],
        out_specs=[block, block, whole((rows, width))],
        out_shape=[half, half, shape((rows, width), F32)],
        scratch_shapes=[pltpu.VMEM((width, rows), BF), pltpu.VMEM((width, buckets), BF),
                        pltpu.VMEM((2 * rows, buckets), BF), pltpu.VMEM((buckets, width), F32),
                        pltpu.VMEM((STRIPES, 8, width), F32), pltpu.VMEM((buckets, width), F32),
                        pltpu.VMEM((8, width), F32)],
        compiler_params=big(),
        cost_estimate=cost(6 << 30, 20 << 20),
        name="project_back",
    )(own, d, dpos, mats, table, x, fg, vg1, vg2, bucket_column)


def near_hop_kernel(where_ref, keep_ref, got_ref, *out_refs):
    for r, out in enumerate(out_refs):
        at = where_ref[2] ^ r
        out[0] = (keep_ref[at].astype(F32) + got_ref[at].astype(F32)).astype(BF)


def near_hop(where, keep, got):
    count, rows, width = keep.shape
    group = pl.BlockSpec((4, rows, width), lambda z: (z, 0, 0))
    return pl.pallas_call(
        near_hop_kernel,
        grid=(count // 4,),
        in_specs=[pl.BlockSpec(memory_space=pltpu.SMEM), group, group],
        out_specs=[pl.BlockSpec((1, rows, width), lambda z: (z, 0, 0))] * 4,
        out_shape=[jax.ShapeDtypeStruct((count // 4, rows, width), BF)] * 4,
        compiler_params=big(),
        cost_estimate=cost(keep.size, 6 * keep.size),
        name="near_hop",
    )(where, keep, got)


def far_hop_kernel(where_ref, *refs):
    for r, out in enumerate(refs[4:]):
        at = where_ref[3] ^ r
        out[0] = sum(ref[at].astype(F32) for ref in refs[:4]).astype(BF)


def far_hop(where, parts):
    count, rows, width = parts[0].shape
    return pl.pallas_call(
        far_hop_kernel,
        in_specs=[pl.BlockSpec(memory_space=pltpu.SMEM)] + [pl.BlockSpec(memory_space=pltpu.VMEM)] * 4,
        out_shape=[jax.ShapeDtypeStruct((1, rows, width), BF)] * 4,
        compiler_params=big(),
        cost_estimate=cost(4 * parts[0].size, 10 * parts[0].size),
        name="far_hop",
    )(where, *parts)


def gather_rows(block):
    return lax.all_gather(block, AXES, axis=0, tiled=False)


def xor_permute(block, mask, count):
    return lax.ppermute(block, AXES, [(d, d ^ mask) for d in range(count)])


class Scatter:
    def __init__(self, where, keep, send, count):
        self.where, self.keep, self.count = where, keep, count
        self.got = xor_permute(send, 1, count)

    def near(self, *after):
        got = tie(self.got, after)
        parts = near_hop(self.where, self.keep, got)
        self.keep, self.sent = parts[0], parts[1:]
        self.got = [xor_permute(part, 2 * r, self.count) for r, part in enumerate(self.sent, 1)]

    def far(self, *after):
        got = tie(self.got, after)
        parts = far_hop(self.where, [self.keep] + list(got))
        self.keep, self.sent = parts[0], parts[1:]
        self.got = [xor_permute(part, 8 * r, self.count) for r, part in enumerate(self.sent, 1)]

    def total(self):
        return sum(part[0].astype(F32) for part in [self.keep] + self.got)


def tie(value, other):
    return lax.optimization_barrier((value, other))[0]


def scatter_plain(keep, send, parts, count):
    blocks = jnp.stack([keep, send], axis=1).reshape((STRIPES,) + keep.shape[1:])
    sums, at = [], 0
    for part in parts:
        whole = blocks[:, at : at + part]
        rows = STRIPES * part
        flat = whole.reshape(count, rows // count, whole.shape[2])
        sums.append(lax.psum_scatter(flat.astype(F32), AXES, scatter_dimension=0, tiled=False))
        at += part
    return sums


def make_body(counts):
    count = counts[0] * counts[1]
    direct = counts == (8, 4)

    def body(
        tokens, lengths, buckets,
        query_weight, query_bias, key_weight, key_bias, value_weight, value_bias,
        output_weight, output_bias, relative_table, first_gain, first_shift,
        inner_weight, inner_bias, outer_weight, outer_bias, second_gain, second_shift,
        cotangent,
    ):
        rows, width = tokens.shape[1:]
        fan = inner_weight.shape[1] // width
        vectors = (
            query_bias, key_bias, value_bias, output_bias, first_gain, first_shift,
            outer_bias, second_gain, second_shift, inner_bias,
        )
        first_mats = (query_weight, key_weight, value_weight, relative_table)
        second_mats = [outer_weight]
        second_mats += [inner_weight[:, f * width : (f + 1) * width] for f in range(fan)]
        second_mats += [output_weight]

        def vector_rows(pieces):
            lead = pieces[0].shape[:-1]
            tile = jnp.zeros(lead + (8, width), BF)
            for i, piece in enumerate(pieces):
                lane = 0 if i < 8 else 128
                tile = tile.at[..., i % 8, lane : lane + piece.shape[-1]].set(piece)
            return tile

        me = lax.axis_index("wide") * counts[1] + lax.axis_index("narrow")
        if direct:
            first_pack, second_pack = pack(first_mats, vectors, outer_weight, inner_weight, output_weight, fan)
            second_all = gather_rows(second_pack)
            everyone = lambda block, step: jnp.concatenate(
                [block] + [xor_permute(block, step * r, count) for r in (1, 2, 3)]
            )
            near = everyone(everyone(first_pack[None], 8), 2)
            far = xor_permute(near, 1, count)
            where = jnp.stack([me, me & 1, (me >> 1) & 3, me >> 3]).astype(jnp.int32)
        else:
            whole = lambda block: lax.all_gather(block, AXES, axis=0, tiled=True)
            striped = lambda block: whole(block).reshape(STRIPES, -1, width)
            spread = [whole(v).reshape(STRIPES, -1) for v in vectors]
            first_all = jnp.concatenate(
                [striped(m) for m in first_mats] + [vector_rows(spread)], axis=1
            )
            second_all = jnp.concatenate([striped(m) for m in second_mats], axis=1)
            first_all = first_all.reshape((4, 4, 2) + first_all.shape[1:]).transpose(2, 1, 0, 3, 4)
            near, far = first_all.reshape((2, STRIPES // 2) + first_all.shape[3:])
            where = jnp.zeros((4,), jnp.int32)

        flat = tokens.reshape(rows, width)
        bucket_column = jnp.pad(buckets[::-1], (0, 1), constant_values=-1).reshape(-1, 1)
        q, k, v, kr, qr, vecs, mats, table = project_all(where, near, far, flat, bucket_column, fan)
        total = lengths[0, 0:1] + lengths[0, 1:2]
        context, probs = attend(total, q, k, v, kr, qr)
        cot = cotangent.reshape(rows, width)
        act, slope, layer_out, og, sg, n1, inv, low, vg1 = feed_forward(
            context, flat, cot, vecs, second_all, fan
        )
        outer_keep, outer_send = outer_grads(where, act, og, fan)
        og = tie(og, outer_send)
        inner_keep, inner_send, context_grad, fg, vg2 = feed_back(
            where, og, sg, n1, inv, low, context, vecs, slope, second_all, fan
        )
        groups = width // 128
        third = groups // 3
        back = lambda dc, i, before: attend_back(
            q, k, v, kr, qr, dc, probs, i * third, third, before
        )
        if direct:
            outer = Scatter(where, outer_keep, outer_send, count)
            outer.near(context_grad)
            inner = Scatter(where, inner_keep, inner_send, count)
            grads = back(tie(context_grad, outer.sent), 0, ())
            inner.near(grads[0])
            grads = back(tie(context_grad, inner.sent), 1, grads)
            outer.far(grads[0])
            grads = back(tie(context_grad, outer.sent), 2, grads)
            inner.far(grads[0])
            d, dpos = tie(tuple(grads), inner.sent)
        else:
            grads = ()
            for i in range(3):
                grads = back(context_grad, i, grads)
            d, dpos = grads
        last_keep, last_send, tokens_grad = project_back(
            where, d, dpos, mats, table, flat, fg, vg1, vg2, bucket_column, fan
        )

        part = width // STRIPES
        if direct:
            last = Scatter(where, last_keep, last_send, count)
            last.near()
            last.far()
            outer_out, inner_sum, last_sum = outer.total(), inner.total(), last.total()
            inner_parts = [inner_sum[f * part : (f + 1) * part] for f in range(fan + 1)]
            query_out, key_out, value_out = [last_sum[i * part : (i + 1) * part] for i in range(3)]
            table_out = last_sum[3 * part : 3 * part + 8]
            tile = last_sum[3 * part + 8 : 3 * part + 16]
            pieces = [
                tile[i % 8, (0 if i < 8 else 128) :][: piece.shape[0]]
                for i, piece in enumerate(vectors)
            ]
        else:
            (outer_out,) = scatter_plain(outer_keep, outer_send, (fan * part,), count)
            inner_parts = scatter_plain(inner_keep, inner_send, (part,) * (fan + 1), count)
            query_out, key_out, value_out, table_out, _ = scatter_plain(
                last_keep, last_send, (part,) * 3 + (8, part - 8), count
            )
            blocks = jnp.stack([last_keep, last_send], axis=1).reshape(STRIPES, -1, width)
            tile = blocks[:, 3 * part + 8 : 3 * part + 16].astype(F32)
            pieces = []
            for i, piece in enumerate(vectors):
                lane = 0 if i < 8 else 128
                length = piece.shape[0] * count // STRIPES
                line = tile[:, i % 8, lane : lane + length].reshape(-1)
                pieces.append(lax.psum_scatter(line, AXES, scatter_dimension=0, tiled=True))
        inner_out = jnp.concatenate(inner_parts[:fan], axis=1)
        output_out = inner_parts[fan]
        (qb, kb, vb, ob, g1, s1, outb, g2, s2, inb) = pieces
        return (
            layer_out.reshape(tokens.shape), tokens_grad.reshape(tokens.shape),
            query_out, qb, key_out, kb, value_out, vb, output_out, ob, table_out, g1, s1,
            inner_out, inb, outer_out, outb, g2, s2,
        )

    return body


def solution(mesh):
    counts = (mesh.shape["wide"], mesh.shape["narrow"])
    rows3, rows2, rows1 = P(AXES, None, None), P(AXES, None), P(AXES)
    params = (
        rows2, rows1, rows2, rows1, rows2, rows1, rows2, rows1, rows2, rows1, rows1,
        rows2, rows1, rows2, rows1, rows1, rows1,
    )
    return jax.shard_map(
        make_body(counts),
        mesh=mesh,
        in_specs=(rows3, rows2, P()) + params + (rows3,),
        out_specs=(rows3, rows3) + params,
        check_vma=False,
    )
```

```python
import jax
import jax.numpy as jnp
from jax import lax
from jax.experimental import pallas as pl
from jax.experimental.pallas import tpu as pltpu
from jax.sharding import PartitionSpec as P

HD = 64
EPSILON = 1e-05
MASKED = -1000000000.0
AXES = ("wide", "narrow")
BF = jnp.bfloat16
F32 = jnp.float32
NT = (((1,), (1,)), ((), ()))
NN = (((1,), (0,)), ((), ()))
TN = (((0,), (0,)), ((), ()))


def dot(left, right, dims):
    return lax.dot_general(left, right, dims, preferred_element_type=F32)


def half_lanes(block):
    first = lax.broadcasted_iota(jnp.int32, (1, 128), 1) < HD
    return jnp.where(first, block, 0).astype(BF), jnp.where(first, 0, block).astype(BF)


def stacked(block):
    return jnp.concatenate(half_lanes(block), axis=0)


def attend_kernel(tot_ref, q_ref, k_ref, v_ref, kr_ref, qr_ref, c_ref, p_ref, t_ref, *, rows, tile):
    span = rows + tile
    scale = (3.0 * HD) ** (-0.5) * 1.4426950408889634
    column = lax.broadcasted_iota(jnp.int32, (1, rows), 1)
    valid = column < tot_ref[0]

    def skewed(grid_scores):
        return pltpu.roll(grid_scores, span - (tile - 1), 1, stride=1, stride_axis=0)[:, :rows]

    values = stacked(v_ref[...])
    for b in range(rows // tile):
        sl = slice(b * tile, (b + 1) * tile)
        low = rows - tile - b * tile
        grid_scores = dot(stacked(k_ref[sl, :]), qr_ref[low : low + span, :], NT)
        for head in range(2):
            t_ref[head, sl, :] = skewed(grid_scores[head * tile : (head + 1) * tile])
    for b in range(rows // tile):
        sl = slice(b * tile, (b + 1) * tile)
        low = rows - tile - b * tile
        q = stacked(q_ref[sl, :])
        grid_scores = dot(q, kr_ref[low : low + span, :], NT)
        raw = (
            dot(q, k_ref[...], NT)
            + jnp.concatenate([skewed(grid_scores[:tile]), skewed(grid_scores[tile:])], axis=0)
            + jnp.concatenate([t_ref[0, :, sl].T, t_ref[1, :, sl].T], axis=0)
        )
        scores = jnp.where(valid, raw * scale, MASKED)
        top = jnp.max(scores, axis=-1, keepdims=True)
        expd = jnp.exp2(scores - top)
        probs = (expd * (1.0 / jnp.sum(expd, axis=-1, keepdims=True))).astype(BF)
        p_ref[0, sl, :] = probs[:tile]
        p_ref[1, sl, :] = probs[tile:]
        both = jnp.concatenate([probs[:tile], probs[tile:]], axis=1)
        c_ref[sl, :] = dot(both, values, NN).astype(BF)


def attend(total, q, k, v, kr, qr):
    rows, width = q.shape
    groups = width // 128
    cols = lambda r: pl.BlockSpec((r, 128), lambda p: (0, p))
    return pl.pallas_call(
        lambda *refs: attend_kernel(*refs, rows=rows, tile=rows // 2),
        grid=(groups,),
        in_specs=[pl.BlockSpec(memory_space=pltpu.SMEM)]
        + [cols(rows)] * 3
        + [cols(2 * rows)] * 2,
        out_specs=[cols(rows), pl.BlockSpec((2, rows, rows), lambda p: (p, 0, 0))],
        out_shape=[
            jax.ShapeDtypeStruct((rows, width), BF),
            jax.ShapeDtypeStruct((2 * groups, rows, rows), BF),
        ],
        scratch_shapes=[pltpu.VMEM((2, rows, rows), F32)],
        compiler_params=pltpu.CompilerParams(vmem_limit_bytes=60 << 20),
        cost_estimate=pl.CostEstimate(
            flops=25 << 30, bytes_accessed=12 << 20, transcendentals=12 * rows * rows
        ),
        name="attend",
    )(total, q, k, v, kr, qr)


def attend_back_kernel(
    q_ref, k_ref, v_ref, kr_ref, qr_ref, dc_ref, p_ref, onehot_ref, *refs, rows, tile,
):
    d_ref, pos_ref, ds_ref, dqr_ref, dkr_ref = refs[-5:]
    dq_ref, dk_ref, dv_ref = d_ref.at[0], d_ref.at[1], d_ref.at[2]
    span = rows + tile
    scale = (3.0 * HD) ** (-0.5)
    upper = lax.broadcasted_iota(jnp.int32, (128, 1), 0) < HD
    flip = (
        lax.broadcasted_iota(jnp.int32, (tile, tile), 0)
        + lax.broadcasted_iota(jnp.int32, (tile, tile), 1)
        == tile - 1
    ).astype(BF)
    dkr_ref[...] = jnp.zeros_like(dkr_ref)
    dqr_ref[...] = jnp.zeros_like(dqr_ref)
    zeros = jnp.zeros((tile, tile), F32)
    beside = lambda *parts: jnp.concatenate(parts, axis=1)
    above = lambda *parts: jnp.concatenate(parts, axis=0)

    def unskewed(flipped):
        return pltpu.roll(beside(flipped, zeros), 0, 1, stride=1, stride_axis=0).astype(BF)

    def turned(block):
        across = block.T
        return beside(jnp.where(upper, across, 0), jnp.where(upper, 0, across)).astype(BF)

    keys, queries = stacked(k_ref[...]), stacked(q_ref[...])
    kr, qr = half_lanes(kr_ref[...]), half_lanes(qr_ref[...])
    dvt = jnp.zeros((128, rows), F32)
    for b in range(rows // tile):
        sl = slice(b * tile, (b + 1) * tile)
        low = rows - tile - b * tile
        high = low + span
        dc = dc_ref[sl, :]
        dp = dot(stacked(dc), v_ref[...], NT)
        pb = above(p_ref[0, sl, :], p_ref[1, sl, :])
        p = pb.astype(F32)
        pdp = p * dp
        delta = jnp.sum(pdp, axis=-1, keepdims=True)
        ds = ((pdp - p * delta) * scale).astype(BF)
        dsa, dsb = ds[:tile], ds[tile:]
        ds_ref[0, sl, :] = dsa
        ds_ref[1, sl, :] = dsb
        dvt = dvt + dot(turned(dc.astype(F32)), pb, NN)
        da, db = unskewed(dot(flip, dsa, NN)), unskewed(dot(flip, dsb, NN))
        rel = dot(beside(da, db), above(kr[0][low:high], kr[1][low:high]), NN).astype(BF)
        dq_ref[sl, :] = (dot(beside(dsa, dsb), keys, NN) + dot(flip, rel, NN)).astype(BF)
        dkr_ref[:, low:high] += dot(turned(dot(flip, q_ref[sl, :], NN)), above(da, db), NN)
    dv_ref[...] = dvt.T.astype(BF)
    for b in range(rows // tile):
        sl = slice(b * tile, (b + 1) * tile)
        low = rows - tile - b * tile
        high = low + span
        ta, tb = dot(flip, ds_ref[0, :, sl], NT), dot(flip, ds_ref[1, :, sl], NT)
        da, db = unskewed(ta), unskewed(tb)
        dk = dot(
            beside(ta.astype(BF), tb.astype(BF), da, db),
            above(queries, qr[0][low:high], qr[1][low:high]),
            NN,
        )
        dk_ref[sl, :] = dot(flip, dk.astype(BF), NN).astype(BF)
        dqr_ref[:, low:high] += dot(turned(dot(flip, k_ref[sl, :], NN)), above(da, db), NN)
    pos_ref[0] = dot(dqr_ref[...].astype(BF), onehot_ref[...], NN)
    pos_ref[1] = dot(dkr_ref[...].astype(BF), onehot_ref[...], NN)


def attend_back(q, k, v, kr, qr, dc, probs, onehot, first, groups, before):
    rows, width = q.shape
    buckets = onehot.shape[1]
    cols = lambda r: pl.BlockSpec((r, 128), lambda p: (0, first + p))
    skip = [pl.BlockSpec(memory_space=pl.ANY)] * len(before)
    share = groups / (width // 128)
    return pl.pallas_call(
        lambda *refs: attend_back_kernel(*refs, rows=rows, tile=rows // 2),
        grid=(groups,),
        in_specs=[cols(rows)] * 3
        + [cols(2 * rows)] * 2
        + [cols(rows), pl.BlockSpec((2, rows, rows), lambda p: (first + p, 0, 0)),
           pl.BlockSpec((2 * rows, buckets), lambda p: (0, 0))]
        + skip,
        out_specs=[
            pl.BlockSpec((3, rows, 128), lambda p: (0, 0, first + p)),
            pl.BlockSpec((2, 128, buckets), lambda p: (0, first + p, 0)),
        ],
        out_shape=[
            jax.ShapeDtypeStruct((3, rows, width), BF),
            jax.ShapeDtypeStruct((2, width, buckets), F32),
        ],
        scratch_shapes=[pltpu.VMEM((2, rows, rows), BF)] + [pltpu.VMEM((128, 2 * rows), F32)] * 2,
        compiler_params=pltpu.CompilerParams(vmem_limit_bytes=60 << 20),
        input_output_aliases={8 + i: i for i in range(len(before))},
        cost_estimate=pl.CostEstimate(
            flops=int(40e9 * share), bytes_accessed=int(18e6 * share), transcendentals=0
        ),
        name="attend_back",
    )(q, k, v, kr, qr, dc, probs, onehot, *before)


STRIPES = 32
VECTORS = 10


def cost(flops, moved, transcendentals=0):
    return pl.CostEstimate(flops=flops, bytes_accessed=moved, transcendentals=transcendentals)


def big(megabytes=60):
    return pltpu.CompilerParams(vmem_limit_bytes=megabytes << 20)


def stripe_marks(width, dtype):
    part = width // STRIPES
    column = lax.broadcasted_iota(jnp.int32, (STRIPES, width), 1)
    stripe = lax.broadcasted_iota(jnp.int32, (STRIPES, width), 0)
    owner = (column >= stripe * part) & (column < stripe * part + part)
    place = lax.broadcasted_iota(jnp.int32, (128, width), 0)
    spot = (lax.broadcasted_iota(jnp.int32, (128, width), 1) % part == place).astype(dtype)
    return owner, spot


def pack_kernel(*refs, mats, vectors, fan):
    first_ref, second_ref = refs[-2:]
    at = 0
    for ref in refs[:mats]:
        first_ref[at : at + ref.shape[0], :] = ref[...]
        at += ref.shape[0]
    first_ref[at:, :] = jnp.zeros_like(first_ref[at:, :])
    for i, ref in enumerate(refs[mats : mats + vectors]):
        lane = 0 if i < 8 else 128
        first_ref[at + i % 8 : at + i % 8 + 1, lane : lane + ref.shape[0]] = ref[...].reshape(1, -1)
    outer_ref, inner_ref, output_ref = refs[mats + vectors : mats + vectors + 3]
    width = outer_ref.shape[1]
    at = outer_ref.shape[0]
    second_ref[:at, :] = outer_ref[...]
    for f in range(fan):
        rows = inner_ref.shape[0]
        second_ref[at : at + rows, :] = inner_ref[:, f * width : (f + 1) * width]
        at += rows
    second_ref[at:, :] = output_ref[...]


def pack(mats, vectors, outer, inner, output, fan):
    width = outer.shape[1]
    first = sum(m.shape[0] for m in mats) + 8
    second = outer.shape[0] + fan * inner.shape[0] + output.shape[0]
    return pl.pallas_call(
        lambda *refs: pack_kernel(*refs, mats=len(mats), vectors=len(vectors), fan=fan),
        out_shape=[jax.ShapeDtypeStruct((first, width), BF), jax.ShapeDtypeStruct((second, width), BF)],
        name="pack",
    )(*mats, *vectors, outer, inner, output)


def project_kernel(where_ref, *refs, fan):
    blocks, (x_ref, bucket_ref) = refs[:10], refs[10:12]
    q_ref, k_ref, v_ref, kr_ref, qr_ref, vecs_ref, w_ref, onehot_ref, xt_ref, tt_ref = refs[12:22]
    table_ref, vec_ref = refs[22:]
    step = pl.program_id(0)
    width = x_ref.shape[1]
    span = q_ref.shape[1]
    buckets = onehot_ref.shape[1]
    me = where_ref[0]

    def place(out, near, far):
        for r in range(STRIPES // 2):
            for ref, core in ((near, 0), (far, 1)):
                out[me ^ ((r // 4) * 2 + (r % 4) * 8 + core)] = ref[r]

    for i in range(3):
        place(w_ref.at[i], blocks[2 * i], blocks[2 * i + 1])

    @pl.when(step == 0)
    def _():
        place(table_ref, blocks[6], blocks[7])
        place(vec_ref, blocks[8], blocks[9])
        xt_ref[...] = x_ref[...].T
        tt_ref[...] = table_ref.reshape(buckets, width)[...].T
        index = lax.broadcasted_iota(jnp.int32, onehot_ref.shape, 1)
        onehot_ref[...] = (bucket_ref[...] == index).astype(F32).astype(BF)
        owner, spot = stripe_marks(width, BF)
        vecs_ref[...] = jnp.zeros_like(vecs_ref)

        def spread(block, marks, mine):
            return jnp.sum(jnp.where(mine, dot(block, marks, NN), 0.0), axis=0, keepdims=True)

        for i in range(VECTORS - 1):
            lanes = slice(0, 128) if i < 8 else slice(128, 256)
            vecs_ref[i : i + 1, :] = spread(vec_ref[:, i % 8, lanes], spot, owner)
        block = vec_ref[:, (VECTORS - 1) % 8, 128:256]
        part = width * fan // STRIPES
        for f in range(fan):
            column = lax.broadcasted_iota(jnp.int32, (STRIPES, width), 1) + f * width
            stripe = lax.broadcasted_iota(jnp.int32, (STRIPES, width), 0)
            mine = (column >= stripe * part) & (column < stripe * part + part)
            place_at = lax.broadcasted_iota(jnp.int32, (128, width), 0)
            marks = lax.broadcasted_iota(jnp.int32, (128, width), 1) + f * width
            marks = (marks % part == place_at).astype(BF)
            row = VECTORS - 1 + f
            vecs_ref[row : row + 1, :] = spread(block, marks, mine)

    x = x_ref[...]
    table = table_ref.reshape(buckets, width)[...]
    columns = pl.ds(pl.multiple_of(step * span, 128), span)
    bias = [vecs_ref[i : i + 1, columns] for i in range(3)]
    mats = [w_ref.at[i].reshape(width, span)[...] for i in range(3)]
    for i, out in enumerate((q_ref, k_ref, v_ref)):
        out[...] = (dot(x, mats[i], NN) + bias[i]).astype(BF)
    for i, out in ((0, qr_ref), (1, kr_ref)):
        pos = (dot(table, mats[i], NN) + bias[i]).astype(BF)
        out[...] = dot(onehot_ref[...], pos, NN).astype(BF)


def project_all(where, near, far, x, bucket_column, fan):
    rows, width = x.shape
    part = width // STRIPES
    span = 256
    weight = lambda i: [pl.BlockSpec((STRIPES // 2, part, span), lambda p: (0, i, p))] * 2
    small = lambda i: [pl.BlockSpec((STRIPES // 2, 8, width), lambda p: (0, i, 0))] * 2
    buckets = 8 * STRIPES
    whole = lambda shape: pl.BlockSpec(shape, lambda p: (0,) * len(shape))
    cols = lambda r: pl.BlockSpec((r, span), lambda p: (0, p))
    shape = jax.ShapeDtypeStruct
    out = lambda r: shape((r, width), BF)
    return pl.pallas_call(
        lambda *refs: project_kernel(*refs, fan=fan),
        grid=(width // span,),
        in_specs=[pl.BlockSpec(memory_space=pltpu.SMEM)] + weight(0) + weight(1) + weight(2)
        + small(3 * part // 8) + small(3 * part // 8 + 1)
        + [whole((rows, width)), whole((2 * rows, 1))],
        out_specs=[cols(rows)] * 3 + [cols(2 * rows)] * 2
        + [whole((16, width)), pl.BlockSpec((3, STRIPES, part, span), lambda p: (0, 0, 0, p)),
           whole((2 * rows, buckets)), whole((width, rows)), whole((width, buckets))],
        out_shape=[out(rows)] * 3 + [out(2 * rows)] * 2
        + [shape((16, width), F32), shape((3, STRIPES, part, width), BF), shape((2 * rows, buckets), BF),
           shape((width, rows), BF), shape((width, buckets), BF)],
        scratch_shapes=[pltpu.VMEM((STRIPES, 8, width), BF)] * 2,
        compiler_params=big(),
        cost_estimate=cost(4 << 30, 12 << 20),
        name="project",
    )(where, *([near, far] * 5), x, bucket_column)


def normal_parts(hidden):
    centered = hidden - jnp.mean(hidden, axis=-1, keepdims=True)
    inverse = lax.rsqrt(jnp.mean(centered * centered, axis=-1, keepdims=True) + EPSILON)
    return centered * inverse, inverse


def normal_back(upstream, normed, inverse, gain):
    scaled = upstream * gain
    return inverse * (
        scaled
        - jnp.mean(scaled, axis=-1, keepdims=True)
        - normed * jnp.mean(scaled * normed, axis=-1, keepdims=True)
    )


def halves_to(keep_ref, send_ref, grad, own):
    part = keep_ref.shape[1]
    blocks = grad.reshape((grad.shape[0] // (2 * part), 2, part, grad.shape[1]))
    even, odd = blocks[:, 0].astype(BF), blocks[:, 1].astype(BF)

    @pl.when(own == 0)
    def _():
        keep_ref[...] = even
        send_ref[...] = odd

    @pl.when(own != 0)
    def _():
        keep_ref[...] = odd
        send_ref[...] = even


def feed_kernel(where_ref, vecs_ref, ctx_hbm, x_hbm, cot_hbm, packed_hbm,
                out_hbm, outer_hbm, keep_hbm, send_hbm, cg_hbm, fg_hbm, vg_ref,
                ctx, x, cot, wo, wi, w2, act, slope, low, turned, og, n1, inv, acc, first,
                stage, keep, send, fetch, chunk_fetch, flush, outer_flush, keep_flush, *, fan):
    rows, width = ctx.shape
    part = width // STRIPES
    own = where_ref[1]
    vec = lambda i: vecs_ref[i : i + 1, :]
    column = lambda a: jnp.sum(a, axis=0, keepdims=True)
    copy = pltpu.make_async_copy
    ins = [copy(ctx_hbm, ctx, fetch.at[0]),
           copy(packed_hbm.at[:, pl.ds(2 * fan * part, part), :], wo, fetch.at[1]),
           copy(x_hbm, x, fetch.at[2]), copy(cot_hbm, cot, fetch.at[3])]

    def chunk_copies(f):
        inner = pl.ds(pl.multiple_of((fan + f) * part, 8), part)
        outer = pl.ds(f * (STRIPES // fan), STRIPES // fan)
        return (copy(packed_hbm.at[:, inner, :], wi.at[f], chunk_fetch.at[0, f]),
                copy(packed_hbm.at[outer, pl.ds(0, fan * part), :], w2.at[f], chunk_fetch.at[1, f]))

    for one in ins[:3]:
        one.start()
    for f in range(fan):
        for one in chunk_copies(f):
            one.start()
    ins[3].start()
    vg_ref[...] = jnp.zeros_like(vg_ref)
    ins[0].wait()
    ins[1].wait()
    attended = dot(ctx[...], wo.reshape(width, width)[...], NN) + vec(3)
    ins[2].wait()
    normed, inverse = normal_parts(x[...].astype(F32) + attended)
    n1[...] = normed
    inv[...] = jnp.broadcast_to(inverse, inv.shape)
    start = normed * vec(4) + vec(5)
    low[...] = start.astype(BF)
    acc[...] = start + vec(6)

    def forward(f, carry):
        for one in chunk_copies(f):
            one.wait()
        pre = dot(low[...], wi.at[f].reshape(width, width)[...], NN) + vecs_ref[pl.ds(9 + f, 1), :]
        half = 0.5 + 0.5 * lax.erf(pre * 0.7071067811865476)
        active = (pre * half).astype(BF)
        act[f] = active
        slope[f] = (half + pre * (jnp.exp(-0.5 * pre * pre) * 0.3989422804014327)).astype(BF)
        acc[...] += dot(active, w2.at[f].reshape(width, width)[...], NN)
        return carry

    lax.fori_loop(0, fan, forward, 0)
    turned[...] = low[...].T
    normed, inverse = normal_parts(acc[...])
    low[...] = (normed * vec(7) + vec(8)).astype(BF)
    outs = [copy(low, out_hbm, flush.at[0]), copy(cot, cg_hbm, flush.at[1]), copy(first, fg_hbm, flush.at[2])]
    outs[0].start()
    ins[3].wait()
    upstream = cot[...].astype(F32)
    vg_ref[8:9, :] = column(upstream * normed)
    vg_ref[9:10, :] = column(upstream)
    second = normal_back(upstream, normed, inverse, vec(7))
    acc[...] = second
    og[...] = second.astype(BF)
    vg_ref[10:11, :] = column(og[...].astype(F32))

    def outer_copy(f):
        return copy(stage.at[f % 2], outer_hbm.at[pl.ds(pl.multiple_of(f * width, 8), width), :],
                    outer_flush.at[f % 2])

    def outer_grad(f, carry):
        @pl.when(f >= 2)
        def _():
            outer_copy(f - 2).wait()

        stage[f % 2] = dot(act[f], og[...], TN).astype(BF)
        outer_copy(f).start()
        return carry

    lax.fori_loop(0, fan, outer_grad, 0)

    def keep_copies(f):
        place = pl.ds(pl.multiple_of(f * part, 8), part)
        return (copy(keep.at[f % 2], keep_hbm.at[:, place, :], keep_flush.at[0, f % 2]),
                copy(send.at[f % 2], send_hbm.at[:, place, :], keep_flush.at[1, f % 2]))

    def leave(f, grad):
        @pl.when(f >= 2)
        def _():
            for one in keep_copies(f - 2):
                one.wait()

        halves_to(keep.at[f % 2], send.at[f % 2], grad, own)
        for one in keep_copies(f):
            one.start()

    def backward(f, carry):
        grad = dot(og[...], w2.at[f].reshape(width, width)[...], NT) * slope[f].astype(F32)
        ig = grad.astype(BF)
        acc[...] += dot(ig, wi.at[f].reshape(width, width)[...], NT)
        vg_ref[pl.ds(f, 1), :] = column(ig.astype(F32))
        leave(f, dot(turned[...], ig, NN))
        return carry

    lax.fori_loop(0, fan, backward, 0)
    total = acc[...]
    normed = n1[...]
    vg_ref[4:5, :] = column(total * normed)
    vg_ref[5:6, :] = column(total)
    grad = normal_back(total, normed, inv[:, 0:1], vec(4))
    first[...] = grad
    outs[2].start()
    ag = grad.astype(BF)
    vg_ref[6:7, :] = column(ag.astype(F32))
    leave(fan, dot(ctx[...], ag, TN))
    cot[...] = dot(ag, wo.reshape(width, width)[...], NT).astype(BF)
    outs[1].start()
    for one in outs:
        one.wait()
    for f in (fan - 2, fan - 1):
        outer_copy(f).wait()
    for f in (fan - 1, fan):
        for one in keep_copies(f):
            one.wait()


def feed(where, vecs, ctx, x, cot, packed, fan):
    rows, width = x.shape
    part = width // STRIPES
    shape = jax.ShapeDtypeStruct
    hbm = pl.BlockSpec(memory_space=pl.ANY)
    half = shape((STRIPES // 2, part * (fan + 1), width), BF)
    low, high = pltpu.VMEM((rows, width), BF), pltpu.VMEM((rows, width), F32)
    sem = pltpu.SemaphoreType.DMA
    return pl.pallas_call(
        lambda *refs: feed_kernel(*refs, fan=fan),
        in_specs=[pl.BlockSpec(memory_space=pltpu.SMEM), pl.BlockSpec(memory_space=pltpu.VMEM)] + [hbm] * 4,
        out_specs=[hbm] * 6 + [pl.BlockSpec(memory_space=pltpu.VMEM)],
        out_shape=[shape((rows, width), BF), shape((fan * width, width), BF), half, half,
                   shape((rows, width), BF), shape((rows, width), F32), shape((16, width), F32)],
        scratch_shapes=[low, low, low, pltpu.VMEM((STRIPES, part, width), BF),
                        pltpu.VMEM((fan, STRIPES, part, width), BF),
                        pltpu.VMEM((fan, STRIPES // fan, part * fan, width), BF),
                        pltpu.VMEM((fan, rows, width), BF), pltpu.VMEM((fan, rows, width), BF), low,
                        pltpu.VMEM((width, rows), BF), low, high, pltpu.VMEM((rows, 128), F32), high, high,
                        pltpu.VMEM((2, width, width), BF)]
        + [pltpu.VMEM((2, STRIPES // 2, part, width), BF)] * 2
        + [sem((4,)), sem((2, fan)), sem((3,)), sem((2,)), sem((2, 2))],
        compiler_params=big(),
        name="feed",
    )(where, vecs, ctx, x, cot, packed)


def project_back_kernel(own_ref, d_ref, pos_ref, w_ref, xt_ref, tt_ref, vg2_ref,
                        keep_ref, send_ref, vec_ref, tab_ref, bias_ref, *, fan):
    step = pl.program_id(0)
    width, rows = xt_ref.shape
    buckets = tt_ref.shape[1]
    part = width // STRIPES
    own = own_ref[1]

    @pl.when(step == 0)
    def _():
        tab_ref[...] = jnp.zeros_like(tab_ref)

    @pl.when(step < 3)
    def _():
        d = d_ref[0]
        ones = jnp.ones((8, rows), BF)
        bias_ref[step] = dot(ones, d, NN)

        @pl.when(step < 2)
        def _():
            pos = pos_ref[0].astype(BF)
            tab_ref[...] += dot(w_ref.at[0].reshape(width, width)[...], pos, NN)
            bias_ref[step] += dot(jnp.ones((8, buckets), BF), pos, NT)
            grad = dot(xt_ref[...], d, NN) + dot(tt_ref[...], pos, NT)
            halves_to(keep_ref, send_ref, grad, own)

        @pl.when(step == 2)
        def _():
            halves_to(keep_ref, send_ref, dot(xt_ref[...], d, NN), own)

    @pl.when(step == 3)
    def _():
        vec_ref[...] = jnp.zeros_like(vec_ref)
        owner, spot = stripe_marks(width, BF)

        def cut(row, marks, mine):
            return dot(jnp.where(mine, jnp.broadcast_to(row, mine.shape), 0.0).astype(BF), marks, NT)

        bias = [bias_ref[i, 0:1, :] for i in range(3)]
        grads = bias + [vg2_ref[6:7, :], vg2_ref[4:5, :],
                        vg2_ref[5:6, :], vg2_ref[10:11, :], vg2_ref[8:9, :], vg2_ref[9:10, :]]
        for i, row in enumerate(grads):
            lanes = slice(0, 128) if i < 8 else slice(128, 256)
            vec_ref[:, i % 8, lanes] = cut(row, spot, owner)
        broad = width * fan // STRIPES
        total = jnp.zeros((STRIPES, 128), F32)
        for f in range(fan):
            column_at = lax.broadcasted_iota(jnp.int32, (STRIPES, width), 1) + f * width
            stripe = lax.broadcasted_iota(jnp.int32, (STRIPES, width), 0)
            mine = (column_at >= stripe * broad) & (column_at < stripe * broad + broad)
            place = lax.broadcasted_iota(jnp.int32, (128, width), 0)
            marks = lax.broadcasted_iota(jnp.int32, (128, width), 1) + f * width
            total += cut(vg2_ref[f : f + 1, :], (marks % broad == place).astype(BF), mine)
        vec_ref[:, (VECTORS - 1) % 8, 128:256] = total
        blocks = tab_ref[...].T.reshape((STRIPES // 2, 2, 8, width))
        vectors = vec_ref[...].reshape((STRIPES // 2, 2, 8, width))
        zero = jnp.zeros((STRIPES // 2, part - 16, width), BF)
        for out, pick in ((keep_ref, own == 0), (send_ref, own != 0)):
            out[:, 0:8] = jnp.where(pick, blocks[:, 0], blocks[:, 1]).astype(BF)
            out[:, 8:16] = jnp.where(pick, vectors[:, 0], vectors[:, 1]).astype(BF)
            out[:, 16:part] = zero


def project_back(own, d, pos, mats, xt, tt, vg, fan):
    width, rows = xt.shape
    part = width // STRIPES
    buckets = tt.shape[1]
    whole = lambda shape: pl.BlockSpec(shape, lambda g: (0,) * len(shape))
    block = pl.BlockSpec((STRIPES // 2, part, width), lambda g: (0, g, 0))
    shape = jax.ShapeDtypeStruct
    half = shape((STRIPES // 2, part * 4, width), BF)
    return pl.pallas_call(
        lambda *refs: project_back_kernel(*refs, fan=fan),
        grid=(4,),
        in_specs=[pl.BlockSpec(memory_space=pltpu.SMEM),
                  pl.BlockSpec((1, rows, width), lambda g: (jnp.minimum(g, 2), 0, 0)),
                  pl.BlockSpec((1, width, buckets), lambda g: (jnp.minimum(g, 1), 0, 0)),
                  pl.BlockSpec((1, STRIPES, part, width), lambda g: (jnp.minimum(g, 1), 0, 0, 0)),
                  whole((width, rows)), whole((width, buckets)), whole((16, width))],
        out_specs=[block, block],
        out_shape=[half, half],
        scratch_shapes=[pltpu.VMEM((STRIPES, 8, width), F32), pltpu.VMEM((width, buckets), F32),
                        pltpu.VMEM((3, 8, width), F32)],
        compiler_params=big(),
        cost_estimate=cost(4 << 30, 12 << 20),
        name="project_back",
    )(own, d, pos, mats, xt, tt, vg)


def token_grad_kernel(fg_ref, d_ref, w_ref, out_ref):
    width = out_ref.shape[1]

    @pl.when(pl.program_id(0) == 0)
    def _():
        out_ref[...] = fg_ref[...]

    out_ref[...] += dot(d_ref[0], w_ref.at[0].reshape(width, width)[...], NT)


def token_grads(fg, d, mats):
    rows, width = fg.shape
    full = pl.BlockSpec((rows, width), lambda g: (0, 0))
    return pl.pallas_call(
        token_grad_kernel,
        grid=(3,),
        in_specs=[full, pl.BlockSpec((1, rows, width), lambda g: (g, 0, 0)),
                  pl.BlockSpec((1,) + mats.shape[1:], lambda g: (g, 0, 0, 0))],
        out_specs=full,
        out_shape=jax.ShapeDtypeStruct((rows, width), F32),
        compiler_params=big(24),
        cost_estimate=cost(2 << 30, 10 << 20),
        name="token_grads",
    )(fg, d, mats)


def near_hop_kernel(where_ref, keep_ref, got_ref, *out_refs):
    for r, out in enumerate(out_refs):
        at = where_ref[2] ^ r
        out[0] = (keep_ref[at].astype(F32) + got_ref[at].astype(F32)).astype(BF)


def near_hop(where, keep, got):
    count, rows, width = keep.shape
    group = pl.BlockSpec((4, rows, width), lambda z: (z, 0, 0))
    return pl.pallas_call(
        near_hop_kernel,
        grid=(count // 4,),
        in_specs=[pl.BlockSpec(memory_space=pltpu.SMEM), group, group],
        out_specs=[pl.BlockSpec((1, rows, width), lambda z: (z, 0, 0))] * 4,
        out_shape=[jax.ShapeDtypeStruct((count // 4, rows, width), BF)] * 4,
        compiler_params=big(16),
        cost_estimate=cost(keep.size, 6 * keep.size),
        name="near_hop",
    )(where, keep, got)


def finish_kernel(*refs, parts, vectors):
    ins, outer_ref, mats, lines = refs[:parts], refs[parts], refs[parts + 1 : -vectors - 1], refs[-vectors - 1 : -1]
    refs[-1][...] = outer_ref[0].astype(F32)
    add = lambda rows: sum(ref[0, rows, :].astype(F32) for ref in ins)
    at = 0
    for ref in mats:
        ref[...] = add(slice(at, at + ref.shape[0]))
        at += ref.shape[0]
    tile = add(slice(at, at + 8))
    for i, ref in enumerate(lines):
        lane = 0 if i < 8 else 128
        ref[...] = tile[i % 8, lane : lane + ref.shape[0]]


def finish(parts, outer, mat_rows, sizes):
    width = parts[0].shape[2]
    return pl.pallas_call(
        lambda *refs: finish_kernel(*refs, parts=len(parts), vectors=len(sizes)),
        out_shape=[jax.ShapeDtypeStruct((rows, width), F32) for rows in mat_rows]
        + [jax.ShapeDtypeStruct((size,), F32) for size in sizes]
        + [jax.ShapeDtypeStruct(outer.shape[1:], F32)],
        compiler_params=big(16),
        name="finish",
    )(*parts, outer)


def far_hop_kernel(where_ref, *refs):
    for r, out in enumerate(refs[4:]):
        at = where_ref[3] ^ r
        out[0] = sum(ref[at].astype(F32) for ref in refs[:4]).astype(BF)


def far_hop(where, parts):
    count, rows, width = parts[0].shape
    return pl.pallas_call(
        far_hop_kernel,
        in_specs=[pl.BlockSpec(memory_space=pltpu.SMEM)] + [pl.BlockSpec(memory_space=pltpu.VMEM)] * 4,
        out_shape=[jax.ShapeDtypeStruct((1, rows, width), BF)] * 4,
        compiler_params=big(16),
        cost_estimate=cost(4 * parts[0].size, 10 * parts[0].size),
        name="far_hop",
    )(where, *parts)


def gather_rows(block):
    return lax.all_gather(block, AXES, axis=0, tiled=False)


def scatter_rows(blocks):
    return lax.psum_scatter(blocks, AXES, scatter_dimension=0, tiled=False)


def xor_permute(block, mask, count):
    return lax.ppermute(block, AXES, [(d, d ^ mask) for d in range(count)])


def in_vmem(block):
    return pltpu.with_memory_space_constraint(block, pltpu.VMEM)


class Scatter:
    def __init__(self, where, keep, send, count):
        self.where, self.keep, self.count = where, keep, count
        self.got = xor_permute(send, 1, count)

    def near(self, *after):
        got = tie(self.got, after)
        parts = near_hop(self.where, self.keep, in_vmem(got))
        self.keep, self.sent = parts[0], parts[1:]
        self.got = [xor_permute(part, 2 * r, self.count) for r, part in enumerate(self.sent, 1)]

    def far(self, *after):
        got = tie(self.got, after)
        parts = far_hop(self.where, [self.keep] + [in_vmem(part) for part in got])
        self.keep, self.sent = parts[0], parts[1:]
        self.got = [xor_permute(part, 8 * r, self.count) for r, part in enumerate(self.sent, 1)]

    def total(self):
        return sum(part[0].astype(F32) for part in [self.keep] + self.got)


def tie(value, other):
    if isinstance(other, tuple) and not other:
        return value
    return lax.optimization_barrier((value, other))[0]


def scatter_plain(keep, send, parts, count):
    blocks = jnp.stack([keep, send], axis=1).reshape((STRIPES,) + keep.shape[1:])
    sums, at = [], 0
    for part in parts:
        whole = blocks[:, at : at + part]
        rows = STRIPES * part
        flat = whole.reshape(count, rows // count, whole.shape[2])
        sums.append(lax.psum_scatter(flat.astype(F32), AXES, scatter_dimension=0, tiled=False))
        at += part
    return sums


def make_body(counts):
    count = counts[0] * counts[1]
    direct = counts == (8, 4)

    def body(
        tokens, lengths, buckets,
        query_weight, query_bias, key_weight, key_bias, value_weight, value_bias,
        output_weight, output_bias, relative_table, first_gain, first_shift,
        inner_weight, inner_bias, outer_weight, outer_bias, second_gain, second_shift,
        cotangent,
    ):
        rows, width = tokens.shape[1:]
        fan = inner_weight.shape[1] // width
        vectors = (
            query_bias, key_bias, value_bias, output_bias, first_gain, first_shift,
            outer_bias, second_gain, second_shift, inner_bias,
        )
        first_mats = (query_weight, key_weight, value_weight, relative_table)
        second_mats = [outer_weight]
        second_mats += [inner_weight[:, f * width : (f + 1) * width] for f in range(fan)]
        second_mats += [output_weight]

        def vector_rows(pieces):
            lead = pieces[0].shape[:-1]
            tile = jnp.zeros(lead + (8, width), BF)
            for i, piece in enumerate(pieces):
                lane = 0 if i < 8 else 128
                tile = tile.at[..., i % 8, lane : lane + piece.shape[-1]].set(piece)
            return tile

        me = lax.axis_index("wide") * counts[1] + lax.axis_index("narrow")
        if direct:
            first_pack, second_pack = pack(first_mats, vectors, outer_weight, inner_weight, output_weight, fan)
            second_all = gather_rows(second_pack)
            everyone = lambda block, step: jnp.concatenate(
                [block] + [xor_permute(block, step * r, count) for r in (1, 2, 3)]
            )
            near = everyone(everyone(first_pack[None], 8), 2)
            far = xor_permute(near, 1, count)
            where = jnp.stack([me, me & 1, (me >> 1) & 3, me >> 3]).astype(jnp.int32)
        else:
            whole = lambda block: lax.all_gather(block, AXES, axis=0, tiled=True)
            striped = lambda block: whole(block).reshape(STRIPES, -1, width)
            spread = [whole(v).reshape(STRIPES, -1) for v in vectors]
            first_all = jnp.concatenate(
                [striped(m) for m in first_mats] + [vector_rows(spread)], axis=1
            )
            second_all = jnp.concatenate([striped(m) for m in second_mats], axis=1)
            first_all = first_all.reshape((4, 4, 2) + first_all.shape[1:]).transpose(2, 1, 0, 3, 4)
            near, far = first_all.reshape((2, STRIPES // 2) + first_all.shape[3:])
            where = jnp.zeros((4,), jnp.int32)

        flat = tokens.reshape(rows, width)
        bucket_column = jnp.pad(buckets[::-1], (0, 1), constant_values=-1).reshape(-1, 1)
        q, k, v, kr, qr, vecs, mats, onehot, xt, tt = project_all(where, near, far, flat, bucket_column, fan)
        total = lengths[0, 0:1] + lengths[0, 1:2]
        context, probs = attend(total, q, k, v, kr, qr)
        cot = cotangent.reshape(rows, width)
        layer_out, outer_grad, inner_keep, inner_send, context_grad, fg, vg = feed(
            where, vecs, context, flat, cot, second_all, fan
        )
        outer_blocks = outer_grad.reshape(count, -1, width)
        groups = width // 128
        back = lambda dc, first, pairs, before: attend_back(
            q, k, v, kr, qr, dc, probs, onehot, first, pairs, before
        )
        if direct:
            outer_sum = scatter_rows(outer_blocks)
            inner = Scatter(where, inner_keep, inner_send, count)
            grads = back(context_grad, 0, 1, ())
            inner.near(grads[0])
            grads = back(tie(context_grad, inner.sent), 1, groups - 1, grads)
            inner.far(grads[0])
            d, pos = tie(tuple(grads), inner.sent)
        else:
            outer_out = scatter_rows(outer_blocks.astype(F32))
            grads = back(context_grad, 0, 1, ())
            d, pos = back(context_grad, 1, groups - 1, grads)
        last_keep, last_send = project_back(where, d, pos, mats, xt, tt, vg, fan)

        part = width // STRIPES
        if direct:
            last = Scatter(where, last_keep, last_send, count)
            last.near()
            tokens_grad = token_grads(fg, tie(d, last.sent), mats)
            last.far(tokens_grad)
            inner.got = tie(inner.got, tokens_grad)
            inner_sum = inner.total()
            inner_parts = [inner_sum[f * part : (f + 1) * part] for f in range(fan + 1)]
            query_out, key_out, value_out, table_out, *pieces, outer_out = finish(
                [last.keep] + [in_vmem(got) for got in last.got],
                outer_sum[None], (part, part, part, 8), [piece.shape[0] for piece in vectors],
            )
        else:
            tokens_grad = token_grads(fg, d, mats)
            inner_parts = scatter_plain(inner_keep, inner_send, (part,) * (fan + 1), count)
            query_out, key_out, value_out, table_out, _ = scatter_plain(
                last_keep, last_send, (part,) * 3 + (8, part - 8), count
            )
            blocks = jnp.stack([last_keep, last_send], axis=1).reshape(STRIPES, -1, width)
            tile = blocks[:, 3 * part + 8 : 3 * part + 16].astype(F32)
            pieces = []
            for i, piece in enumerate(vectors):
                lane = 0 if i < 8 else 128
                length = piece.shape[0] * count // STRIPES
                line = tile[:, i % 8, lane : lane + length].reshape(-1)
                pieces.append(lax.psum_scatter(line, AXES, scatter_dimension=0, tiled=True))
        inner_out = jnp.concatenate(inner_parts[:fan], axis=1)
        output_out = inner_parts[fan]
        (qb, kb, vb, ob, g1, s1, outb, g2, s2, inb) = pieces
        return (
            layer_out.reshape(tokens.shape), tokens_grad.reshape(tokens.shape),
            query_out, qb, key_out, kb, value_out, vb, output_out, ob, table_out, g1, s1,
            inner_out, inb, outer_out, outb, g2, s2,
        )

    return body


def solution(mesh):
    counts = (mesh.shape["wide"], mesh.shape["narrow"])
    rows3, rows2, rows1 = P(AXES, None, None), P(AXES, None), P(AXES)
    params = (
        rows2, rows1, rows2, rows1, rows2, rows1, rows2, rows1, rows2, rows1, rows1,
        rows2, rows1, rows2, rows1, rows1, rows1,
    )
    return jax.shard_map(
        make_body(counts),
        mesh=mesh,
        in_specs=(rows3, rows2, P()) + params + (rows3,),
        out_specs=(rows3, rows3) + params,
        check_vma=False,
    )
```

```python
import jax
import jax.numpy as jnp
from jax import lax
from jax.experimental import pallas as pl
from jax.experimental.pallas import tpu as pltpu
from jax.sharding import PartitionSpec as P

HD = 64
EPSILON = 1e-05
MASKED = -1000000000.0
AXES = ("wide", "narrow")
BF = jnp.bfloat16
F32 = jnp.float32
NT = (((1,), (1,)), ((), ()))
NN = (((1,), (0,)), ((), ()))
TN = (((0,), (0,)), ((), ()))


def dot(left, right, dims):
    return lax.dot_general(left, right, dims, preferred_element_type=F32)


def half_lanes(block):
    first = lax.broadcasted_iota(jnp.int32, (1, 128), 1) < HD
    return jnp.where(first, block, 0).astype(BF), jnp.where(first, 0, block).astype(BF)


def stacked(block):
    return jnp.concatenate(half_lanes(block), axis=0)


def attend_kernel(tot_ref, q_ref, k_ref, v_ref, kr_ref, qr_ref, c_ref, p_ref, t_ref, *, rows, tile):
    span = rows + tile
    scale = (3.0 * HD) ** (-0.5) * 1.4426950408889634
    column = lax.broadcasted_iota(jnp.int32, (1, rows), 1)
    valid = column < tot_ref[0]

    def skewed(grid_scores):
        return pltpu.roll(grid_scores, span - (tile - 1), 1, stride=1, stride_axis=0)[:, :rows]

    values = stacked(v_ref[...])
    for b in range(rows // tile):
        sl = slice(b * tile, (b + 1) * tile)
        low = rows - tile - b * tile
        grid_scores = dot(stacked(k_ref[sl, :]), qr_ref[low : low + span, :], NT)
        for head in range(2):
            t_ref[head, sl, :] = skewed(grid_scores[head * tile : (head + 1) * tile])
    for b in range(rows // tile):
        sl = slice(b * tile, (b + 1) * tile)
        low = rows - tile - b * tile
        q = stacked(q_ref[sl, :])
        grid_scores = dot(q, kr_ref[low : low + span, :], NT)
        raw = (
            dot(q, k_ref[...], NT)
            + jnp.concatenate([skewed(grid_scores[:tile]), skewed(grid_scores[tile:])], axis=0)
            + jnp.concatenate([t_ref[0, :, sl].T, t_ref[1, :, sl].T], axis=0)
        )
        scores = jnp.where(valid, raw * scale, MASKED)
        top = jnp.max(scores, axis=-1, keepdims=True)
        expd = jnp.exp2(scores - top)
        probs = (expd * (1.0 / jnp.sum(expd, axis=-1, keepdims=True))).astype(BF)
        p_ref[0, sl, :] = probs[:tile]
        p_ref[1, sl, :] = probs[tile:]
        both = jnp.concatenate([probs[:tile], probs[tile:]], axis=1)
        c_ref[sl, :] = dot(both, values, NN).astype(BF)


def attend(total, q, k, v, kr, qr):
    rows, width = q.shape
    groups = width // 128
    cols = lambda r: pl.BlockSpec((r, 128), lambda p: (0, p))
    return pl.pallas_call(
        lambda *refs: attend_kernel(*refs, rows=rows, tile=rows // 2),
        grid=(groups,),
        in_specs=[pl.BlockSpec(memory_space=pltpu.SMEM)]
        + [cols(rows)] * 3
        + [cols(2 * rows)] * 2,
        out_specs=[cols(rows), pl.BlockSpec((2, rows, rows), lambda p: (p, 0, 0))],
        out_shape=[
            jax.ShapeDtypeStruct((rows, width), BF),
            jax.ShapeDtypeStruct((2 * groups, rows, rows), BF),
        ],
        scratch_shapes=[pltpu.VMEM((2, rows, rows), F32)],
        compiler_params=pltpu.CompilerParams(vmem_limit_bytes=60 << 20),
        cost_estimate=pl.CostEstimate(
            flops=25 << 30, bytes_accessed=12 << 20, transcendentals=12 * rows * rows
        ),
        name="attend",
    )(total, q, k, v, kr, qr)


def attend_back_kernel(
    q_ref, k_ref, v_ref, kr_ref, qr_ref, dc_ref, p_ref, onehot_ref, *refs, rows, tile,
):
    d_ref, pos_ref, ds_ref, dqr_ref, dkr_ref = refs[-5:]
    dq_ref, dk_ref, dv_ref = d_ref.at[0], d_ref.at[1], d_ref.at[2]
    span = rows + tile
    scale = (3.0 * HD) ** (-0.5)
    upper = lax.broadcasted_iota(jnp.int32, (128, 1), 0) < HD
    flip = (
        lax.broadcasted_iota(jnp.int32, (tile, tile), 0)
        + lax.broadcasted_iota(jnp.int32, (tile, tile), 1)
        == tile - 1
    ).astype(BF)
    dkr_ref[...] = jnp.zeros_like(dkr_ref)
    dqr_ref[...] = jnp.zeros_like(dqr_ref)
    zeros = jnp.zeros((tile, tile), F32)
    beside = lambda *parts: jnp.concatenate(parts, axis=1)
    above = lambda *parts: jnp.concatenate(parts, axis=0)

    def unskewed(flipped):
        return pltpu.roll(beside(flipped, zeros), 0, 1, stride=1, stride_axis=0).astype(BF)

    def turned(block):
        across = block.T
        return beside(jnp.where(upper, across, 0), jnp.where(upper, 0, across)).astype(BF)

    keys, queries = stacked(k_ref[...]), stacked(q_ref[...])
    kr, qr = half_lanes(kr_ref[...]), half_lanes(qr_ref[...])
    dvt = jnp.zeros((128, rows), F32)
    for b in range(rows // tile):
        sl = slice(b * tile, (b + 1) * tile)
        low = rows - tile - b * tile
        high = low + span
        dc = dc_ref[sl, :]
        dp = dot(stacked(dc), v_ref[...], NT)
        pb = above(p_ref[0, sl, :], p_ref[1, sl, :])
        p = pb.astype(F32)
        pdp = p * dp
        delta = jnp.sum(pdp, axis=-1, keepdims=True)
        ds = ((pdp - p * delta) * scale).astype(BF)
        dsa, dsb = ds[:tile], ds[tile:]
        ds_ref[0, sl, :] = dsa
        ds_ref[1, sl, :] = dsb
        dvt = dvt + dot(turned(dc.astype(F32)), pb, NN)
        da, db = unskewed(dot(flip, dsa, NN)), unskewed(dot(flip, dsb, NN))
        rel = dot(beside(da, db), above(kr[0][low:high], kr[1][low:high]), NN).astype(BF)
        dq_ref[sl, :] = (dot(beside(dsa, dsb), keys, NN) + dot(flip, rel, NN)).astype(BF)
        dkr_ref[:, low:high] += dot(turned(dot(flip, q_ref[sl, :], NN)), above(da, db), NN)
    dv_ref[...] = dvt.T.astype(BF)
    for b in range(rows // tile):
        sl = slice(b * tile, (b + 1) * tile)
        low = rows - tile - b * tile
        high = low + span
        ta, tb = dot(flip, ds_ref[0, :, sl], NT), dot(flip, ds_ref[1, :, sl], NT)
        da, db = unskewed(ta), unskewed(tb)
        dk = dot(
            beside(ta.astype(BF), tb.astype(BF), da, db),
            above(queries, qr[0][low:high], qr[1][low:high]),
            NN,
        )
        dk_ref[sl, :] = dot(flip, dk.astype(BF), NN).astype(BF)
        dqr_ref[:, low:high] += dot(turned(dot(flip, k_ref[sl, :], NN)), above(da, db), NN)
    pos_ref[0] = dot(dqr_ref[...].astype(BF), onehot_ref[...], NN).astype(BF)
    pos_ref[1] = dot(dkr_ref[...].astype(BF), onehot_ref[...], NN).astype(BF)


def attend_back(q, k, v, kr, qr, dc, probs, onehot, first, groups, before):
    rows, width = q.shape
    buckets = onehot.shape[1]
    cols = lambda r: pl.BlockSpec((r, 128), lambda p: (0, first + p))
    skip = [pl.BlockSpec(memory_space=pl.ANY)] * len(before)
    share = groups / (width // 128)
    return pl.pallas_call(
        lambda *refs: attend_back_kernel(*refs, rows=rows, tile=rows // 2),
        grid=(groups,),
        in_specs=[cols(rows)] * 3
        + [cols(2 * rows)] * 2
        + [cols(rows), pl.BlockSpec((2, rows, rows), lambda p: (first + p, 0, 0)),
           pl.BlockSpec((2 * rows, buckets), lambda p: (0, 0))]
        + skip,
        out_specs=[
            pl.BlockSpec((3, rows, 128), lambda p: (0, 0, first + p)),
            pl.BlockSpec((2, 128, buckets), lambda p: (0, first + p, 0)),
        ],
        out_shape=[
            jax.ShapeDtypeStruct((3, rows, width), BF),
            jax.ShapeDtypeStruct((2, width, buckets), BF),
        ],
        scratch_shapes=[pltpu.VMEM((2, rows, rows), BF)] + [pltpu.VMEM((128, 2 * rows), F32)] * 2,
        compiler_params=pltpu.CompilerParams(vmem_limit_bytes=54 << 20),
        input_output_aliases={8 + i: i for i in range(len(before))},
        cost_estimate=pl.CostEstimate(
            flops=int(40e9 * share), bytes_accessed=int(18e6 * share), transcendentals=0
        ),
        name="attend_back",
    )(q, k, v, kr, qr, dc, probs, onehot, *before)


STRIPES = 32
VECTORS = 10


def cost(flops, moved, transcendentals=0):
    return pl.CostEstimate(flops=flops, bytes_accessed=moved, transcendentals=transcendentals)


def big(megabytes=60):
    return pltpu.CompilerParams(vmem_limit_bytes=megabytes << 20)


def stripe_marks(width, dtype):
    part = width // STRIPES
    column = lax.broadcasted_iota(jnp.int32, (STRIPES, width), 1)
    stripe = lax.broadcasted_iota(jnp.int32, (STRIPES, width), 0)
    owner = (column >= stripe * part) & (column < stripe * part + part)
    place = lax.broadcasted_iota(jnp.int32, (128, width), 0)
    spot = (lax.broadcasted_iota(jnp.int32, (128, width), 1) % part == place).astype(dtype)
    return owner, spot


def pack_kernel(*refs, mats, vectors, fan):
    first_ref, second_ref = refs[-2:]
    at = 0
    for ref in refs[:mats]:
        first_ref[at : at + ref.shape[0], :] = ref[...]
        at += ref.shape[0]
    first_ref[at:, :] = jnp.zeros_like(first_ref[at:, :])
    for i, ref in enumerate(refs[mats : mats + vectors]):
        lane = 0 if i < 8 else 128
        first_ref[at + i % 8 : at + i % 8 + 1, lane : lane + ref.shape[0]] = ref[...].reshape(1, -1)
    outer_ref, inner_ref, output_ref = refs[mats + vectors : mats + vectors + 3]
    width = outer_ref.shape[1]
    at = outer_ref.shape[0]
    second_ref[:at, :] = outer_ref[...]
    for f in range(fan):
        rows = inner_ref.shape[0]
        second_ref[at : at + rows, :] = inner_ref[:, f * width : (f + 1) * width]
        at += rows
    second_ref[at:, :] = output_ref[...]


def pack(mats, vectors, outer, inner, output, fan):
    width = outer.shape[1]
    first = sum(m.shape[0] for m in mats) + 8
    second = outer.shape[0] + fan * inner.shape[0] + output.shape[0]
    return pl.pallas_call(
        lambda *refs: pack_kernel(*refs, mats=len(mats), vectors=len(vectors), fan=fan),
        out_shape=[jax.ShapeDtypeStruct((first, width), BF), jax.ShapeDtypeStruct((second, width), BF)],
        name="pack",
    )(*mats, *vectors, outer, inner, output)


def project_kernel(where_ref, *refs, fan):
    blocks, (x_ref, bucket_ref) = refs[:10], refs[10:12]
    q_ref, k_ref, v_ref, kr_ref, qr_ref, vecs_ref, w_ref, onehot_ref, xt_ref, tt_ref = refs[12:22]
    table_ref, vec_ref = refs[22:]
    step = pl.program_id(0)
    width = x_ref.shape[1]
    span = q_ref.shape[1]
    buckets = onehot_ref.shape[1]
    me = where_ref[0]

    def place(out, near, far):
        for r in range(STRIPES // 2):
            for ref, core in ((near, 0), (far, 1)):
                out[me ^ ((r // 4) * 2 + (r % 4) * 8 + core)] = ref[r]

    for i in range(3):
        place(w_ref.at[i], blocks[2 * i], blocks[2 * i + 1])

    @pl.when(step == 0)
    def _():
        place(table_ref, blocks[6], blocks[7])
        place(vec_ref, blocks[8], blocks[9])
        xt_ref[...] = x_ref[...].T
        tt_ref[...] = table_ref.reshape(buckets, width)[...].T
        index = lax.broadcasted_iota(jnp.int32, onehot_ref.shape, 1)
        onehot_ref[...] = (bucket_ref[...] == index).astype(F32).astype(BF)
        owner, spot = stripe_marks(width, BF)
        vecs_ref[...] = jnp.zeros_like(vecs_ref)

        def spread(block, marks, mine):
            return jnp.sum(jnp.where(mine, dot(block, marks, NN), 0.0), axis=0, keepdims=True)

        for i in range(VECTORS - 1):
            lanes = slice(0, 128) if i < 8 else slice(128, 256)
            vecs_ref[i : i + 1, :] = spread(vec_ref[:, i % 8, lanes], spot, owner)
        block = vec_ref[:, (VECTORS - 1) % 8, 128:256]
        part = width * fan // STRIPES
        for f in range(fan):
            column = lax.broadcasted_iota(jnp.int32, (STRIPES, width), 1) + f * width
            stripe = lax.broadcasted_iota(jnp.int32, (STRIPES, width), 0)
            mine = (column >= stripe * part) & (column < stripe * part + part)
            place_at = lax.broadcasted_iota(jnp.int32, (128, width), 0)
            marks = lax.broadcasted_iota(jnp.int32, (128, width), 1) + f * width
            marks = (marks % part == place_at).astype(BF)
            row = VECTORS - 1 + f
            vecs_ref[row : row + 1, :] = spread(block, marks, mine)

    x = x_ref[...]
    table = table_ref.reshape(buckets, width)[...]
    columns = pl.ds(pl.multiple_of(step * span, 128), span)
    bias = [vecs_ref[i : i + 1, columns] for i in range(3)]
    mats = [w_ref.at[i].reshape(width, span)[...] for i in range(3)]
    for i, out in enumerate((q_ref, k_ref, v_ref)):
        out[...] = (dot(x, mats[i], NN) + bias[i]).astype(BF)
    for i, out in ((0, qr_ref), (1, kr_ref)):
        pos = (dot(table, mats[i], NN) + bias[i]).astype(BF)
        out[...] = dot(onehot_ref[...], pos, NN).astype(BF)


def project_all(where, near, far, x, bucket_column, fan):
    rows, width = x.shape
    part = width // STRIPES
    span = 256
    weight = lambda i: [pl.BlockSpec((STRIPES // 2, part, span), lambda p: (0, i, p))] * 2
    small = lambda i: [pl.BlockSpec((STRIPES // 2, 8, width), lambda p: (0, i, 0))] * 2
    buckets = 8 * STRIPES
    whole = lambda shape: pl.BlockSpec(shape, lambda p: (0,) * len(shape))
    cols = lambda r: pl.BlockSpec((r, span), lambda p: (0, p))
    shape = jax.ShapeDtypeStruct
    out = lambda r: shape((r, width), BF)
    return pl.pallas_call(
        lambda *refs: project_kernel(*refs, fan=fan),
        grid=(width // span,),
        in_specs=[pl.BlockSpec(memory_space=pltpu.SMEM)] + weight(0) + weight(1) + weight(2)
        + small(3 * part // 8) + small(3 * part // 8 + 1)
        + [whole((rows, width)), whole((2 * rows, 1))],
        out_specs=[cols(rows)] * 3 + [cols(2 * rows)] * 2
        + [whole((16, width)), pl.BlockSpec((3, STRIPES, part, span), lambda p: (0, 0, 0, p)),
           whole((2 * rows, buckets)), whole((width, rows)), whole((width, buckets))],
        out_shape=[out(rows)] * 3 + [out(2 * rows)] * 2
        + [shape((16, width), F32), shape((3, STRIPES, part, width), BF), shape((2 * rows, buckets), BF),
           shape((width, rows), BF), shape((width, buckets), BF)],
        scratch_shapes=[pltpu.VMEM((STRIPES, 8, width), BF)] * 2,
        compiler_params=big(),
        cost_estimate=cost(4 << 30, 12 << 20),
        name="project",
    )(where, *([near, far] * 5), x, bucket_column)


def normal_parts(hidden):
    centered = hidden - jnp.mean(hidden, axis=-1, keepdims=True)
    inverse = lax.rsqrt(jnp.mean(centered * centered, axis=-1, keepdims=True) + EPSILON)
    return centered * inverse, inverse


def normal_back(upstream, normed, inverse, gain):
    scaled = upstream * gain
    return inverse * (
        scaled
        - jnp.mean(scaled, axis=-1, keepdims=True)
        - normed * jnp.mean(scaled * normed, axis=-1, keepdims=True)
    )


def halves_to(keep_ref, send_ref, grad, own):
    part = keep_ref.shape[1]
    blocks = grad.reshape((grad.shape[0] // (2 * part), 2, part, grad.shape[1]))
    even, odd = blocks[:, 0].astype(BF), blocks[:, 1].astype(BF)

    @pl.when(own == 0)
    def _():
        keep_ref[...] = even
        send_ref[...] = odd

    @pl.when(own != 0)
    def _():
        keep_ref[...] = odd
        send_ref[...] = even


def feed_forward_kernel(vecs_ref, ctx_hbm, x_hbm, cot_hbm, packed_hbm,
                        out_hbm, outer_hbm, slope_hbm, og_hbm, low_hbm, n1_hbm, inv_hbm, second_hbm, vg_ref,
                        ctx, x, cot, wo, wi, w2, act, slope, low, og, n1, inv, acc, out, stage,
                        fetch, chunk_fetch, flush, slope_flush, outer_flush, *, fan):
    rows, width = ctx.shape
    part = width // STRIPES
    vec = lambda i: vecs_ref[i : i + 1, :]
    column = lambda a: jnp.sum(a, axis=0, keepdims=True)
    copy = pltpu.make_async_copy
    ins = [copy(ctx_hbm, ctx, fetch.at[0]),
           copy(packed_hbm.at[:, pl.ds(2 * fan * part, part), :], wo, fetch.at[1]),
           copy(x_hbm, x, fetch.at[2]), copy(cot_hbm, cot, fetch.at[3])]

    def chunk_copies(f):
        inner = pl.ds(pl.multiple_of((fan + f) * part, 8), part)
        outer = pl.ds(f * (STRIPES // fan), STRIPES // fan)
        return (copy(packed_hbm.at[:, inner, :], wi.at[f], chunk_fetch.at[0, f]),
                copy(packed_hbm.at[outer, pl.ds(0, fan * part), :], w2.at[f], chunk_fetch.at[1, f]))

    for one in ins[:3]:
        one.start()
    for f in range(fan):
        for one in chunk_copies(f):
            one.start()
    ins[3].start()
    outs = [copy(n1, n1_hbm, flush.at[0]), copy(inv, inv_hbm, flush.at[1]), copy(low, low_hbm, flush.at[2]),
            copy(out, out_hbm, flush.at[3]), copy(acc, second_hbm, flush.at[4]), copy(og, og_hbm, flush.at[5])]
    vg_ref[...] = jnp.zeros_like(vg_ref)
    ins[0].wait()
    ins[1].wait()
    attended = dot(ctx[...], wo.reshape(width, width)[...], NN) + vec(3)
    ins[2].wait()
    normed, inverse = normal_parts(x[...].astype(F32) + attended)
    n1[...] = normed
    inv[...] = jnp.broadcast_to(inverse, inv.shape)
    start = normed * vec(4) + vec(5)
    low[...] = start.astype(BF)
    acc[...] = start + vec(6)
    for one in outs[:3]:
        one.start()

    def slope_copy(f):
        return copy(slope.at[f], slope_hbm.at[f], slope_flush.at[f])

    def forward(f, carry):
        for one in chunk_copies(f):
            one.wait()
        pre = dot(low[...], wi.at[f].reshape(width, width)[...], NN) + vecs_ref[pl.ds(9 + f, 1), :]
        half = 0.5 + 0.5 * lax.erf(pre * 0.7071067811865476)
        active = (pre * half).astype(BF)
        act[f] = active
        slope[f] = (half + pre * (jnp.exp(-0.5 * pre * pre) * 0.3989422804014327)).astype(BF)
        slope_copy(f).start()
        acc[...] += dot(active, w2.at[f].reshape(width, width)[...], NN)
        return carry

    lax.fori_loop(0, fan, forward, 0)
    normed, inverse = normal_parts(acc[...])
    out[...] = (normed * vec(7) + vec(8)).astype(BF)
    outs[3].start()
    ins[3].wait()
    upstream = cot[...].astype(F32)
    vg_ref[8:9, :] = column(upstream * normed)
    vg_ref[9:10, :] = column(upstream)
    second = normal_back(upstream, normed, inverse, vec(7))
    acc[...] = second
    outs[4].start()
    og[...] = second.astype(BF)
    outs[5].start()
    vg_ref[10:11, :] = column(og[...].astype(F32))

    def outer_copy(f):
        return copy(stage.at[f % 2], outer_hbm.at[pl.ds(pl.multiple_of(f * width, 8), width), :],
                    outer_flush.at[f % 2])

    def outer_grad(f, carry):
        @pl.when(f >= 2)
        def _():
            outer_copy(f - 2).wait()

        stage[f % 2] = dot(act[f], og[...], TN).astype(BF)
        outer_copy(f).start()
        return carry

    lax.fori_loop(0, fan, outer_grad, 0)
    for one in outs:
        one.wait()
    for f in range(fan):
        slope_copy(f).wait()
    for f in (fan - 2, fan - 1):
        outer_copy(f).wait()


def feed_forward(vecs, ctx, x, cot, packed, fan):
    rows, width = x.shape
    part = width // STRIPES
    shape = jax.ShapeDtypeStruct
    hbm = pl.BlockSpec(memory_space=pl.ANY)
    vmem = pl.BlockSpec(memory_space=pltpu.VMEM)
    low, high = pltpu.VMEM((rows, width), BF), pltpu.VMEM((rows, width), F32)
    sem = pltpu.SemaphoreType.DMA
    return pl.pallas_call(
        lambda *refs: feed_forward_kernel(*refs, fan=fan),
        in_specs=[vmem] + [hbm] * 4,
        out_specs=[hbm] * 8 + [vmem],
        out_shape=[shape((rows, width), BF), shape((fan * width, width), BF), shape((fan, rows, width), BF),
                   shape((rows, width), BF), shape((rows, width), BF), shape((rows, width), F32),
                   shape((rows, 128), F32), shape((rows, width), F32), shape((16, width), F32)],
        scratch_shapes=[low, low, low, pltpu.VMEM((STRIPES, part, width), BF),
                        pltpu.VMEM((fan, STRIPES, part, width), BF),
                        pltpu.VMEM((fan, STRIPES // fan, part * fan, width), BF),
                        pltpu.VMEM((fan, rows, width), BF), pltpu.VMEM((fan, rows, width), BF), low, low,
                        high, pltpu.VMEM((rows, 128), F32), high, low, pltpu.VMEM((2, width, width), BF),
                        sem((4,)), sem((2, fan)), sem((6,)), sem((fan,)), sem((2,))],
        compiler_params=big(),
        name="feed_forward",
    )(vecs, ctx, x, cot, packed)


def feed_back_kernel(where_ref, vecs_ref, vg_in_ref, og_hbm, low_hbm, slope_hbm, second_hbm, n1_hbm, inv_hbm,
                     ctx_hbm, packed_hbm, keep_hbm, send_hbm, cg_hbm, fg_hbm, vg_ref,
                     og, low, slope, acc, n1, inv, ctx, wo, wi, w2, turned, cg, fg, keep, send,
                     fetch, chunk_fetch, flush, keep_flush, *, fan):
    rows, width = ctx.shape
    part = width // STRIPES
    own = where_ref[1]
    column = lambda a: jnp.sum(a, axis=0, keepdims=True)
    copy = pltpu.make_async_copy

    def chunk_copies(f):
        inner = pl.ds(pl.multiple_of((fan + f) * part, 8), part)
        outer = pl.ds(f * (STRIPES // fan), STRIPES // fan)
        return (copy(packed_hbm.at[outer, pl.ds(0, fan * part), :], w2.at[f], chunk_fetch.at[0, f]),
                copy(slope_hbm.at[f], slope.at[f], chunk_fetch.at[1, f]),
                copy(packed_hbm.at[:, inner, :], wi.at[f], chunk_fetch.at[2, f]))

    ins = [copy(og_hbm, og, fetch.at[0]), copy(low_hbm, low, fetch.at[1]), copy(second_hbm, acc, fetch.at[2]),
           copy(ctx_hbm, ctx, fetch.at[3]), copy(n1_hbm, n1, fetch.at[4]), copy(inv_hbm, inv, fetch.at[5]),
           copy(packed_hbm.at[:, pl.ds(2 * fan * part, part), :], wo, fetch.at[6])]
    for one in [ins[0], *chunk_copies(0), ins[1], ins[2]]:
        one.start()
    for f in range(1, fan):
        for one in chunk_copies(f):
            one.start()
    for one in ins[3:]:
        one.start()
    vg_ref[...] = vg_in_ref[...]
    ins[1].wait()
    turned[...] = low[...].T
    ins[0].wait()
    ins[2].wait()

    def keep_copies(f):
        place = pl.ds(pl.multiple_of(f * part, 8), part)
        return (copy(keep.at[f % 2], keep_hbm.at[:, place, :], keep_flush.at[0, f % 2]),
                copy(send.at[f % 2], send_hbm.at[:, place, :], keep_flush.at[1, f % 2]))

    def leave(f, grad):
        @pl.when(f >= 2)
        def _():
            for one in keep_copies(f - 2):
                one.wait()

        halves_to(keep.at[f % 2], send.at[f % 2], grad, own)
        for one in keep_copies(f):
            one.start()

    def backward(f, carry):
        for one in chunk_copies(f):
            one.wait()
        grad = dot(og[...], w2.at[f].reshape(width, width)[...], NT) * slope[f].astype(F32)
        ig = grad.astype(BF)
        acc[...] += dot(ig, wi.at[f].reshape(width, width)[...], NT)
        vg_ref[pl.ds(f, 1), :] = column(ig.astype(F32))
        leave(f, dot(turned[...], ig, NN))
        return carry

    lax.fori_loop(0, fan, backward, 0)
    for one in ins[3:]:
        one.wait()
    total, normed = acc[...], n1[...]
    grad = normal_back(total, normed, inv[:, 0:1], vecs_ref[4:5, :])
    ag = grad.astype(BF)
    leave(fan, dot(ctx[...], ag, TN))
    cg[...] = dot(ag, wo.reshape(width, width)[...], NT).astype(BF)
    fg[...] = grad
    outs = [copy(cg, cg_hbm, flush.at[0]), copy(fg, fg_hbm, flush.at[1])]
    for one in outs:
        one.start()
    vg_ref[4:5, :] = column(total * normed)
    vg_ref[5:6, :] = column(total)
    vg_ref[6:7, :] = column(ag.astype(F32))
    for one in outs:
        one.wait()
    for f in (fan - 1, fan):
        for one in keep_copies(f):
            one.wait()


def feed_back(where, vecs, vg, og, low, slope, second, n1, inv, ctx, packed, fan):
    rows, width = ctx.shape
    part = width // STRIPES
    shape = jax.ShapeDtypeStruct
    hbm = pl.BlockSpec(memory_space=pl.ANY)
    vmem = pl.BlockSpec(memory_space=pltpu.VMEM)
    half = shape((STRIPES // 2, part * (fan + 1), width), BF)
    thin, wide = pltpu.VMEM((rows, width), BF), pltpu.VMEM((rows, width), F32)
    sem = pltpu.SemaphoreType.DMA
    return pl.pallas_call(
        lambda *refs: feed_back_kernel(*refs, fan=fan),
        in_specs=[pl.BlockSpec(memory_space=pltpu.SMEM), vmem, vmem] + [hbm] * 8,
        out_specs=[hbm] * 4 + [vmem],
        out_shape=[half, half, shape((rows, width), BF), shape((rows, width), F32), shape(vg.shape, F32)],
        scratch_shapes=[thin, thin, pltpu.VMEM((fan, rows, width), BF), wide, wide,
                        pltpu.VMEM((rows, 128), F32), thin, pltpu.VMEM((STRIPES, part, width), BF),
                        pltpu.VMEM((fan, STRIPES, part, width), BF),
                        pltpu.VMEM((fan, STRIPES // fan, part * fan, width), BF),
                        pltpu.VMEM((width, rows), BF), thin, wide]
        + [pltpu.VMEM((2, STRIPES // 2, part, width), BF)] * 2
        + [sem((7,)), sem((3, fan)), sem((2,)), sem((2, 2))],
        compiler_params=big(),
        name="feed_back",
    )(where, vecs, vg, og, low, slope, second, n1, inv, ctx, packed)


def cut(row, mine, marks):
    return dot(jnp.where(mine, jnp.broadcast_to(row, mine.shape), 0.0).astype(BF), marks, NT)


def cut_vectors_kernel(vg_ref, vec_ref, *, fan):
    width = vg_ref.shape[1]
    vec_ref[...] = jnp.zeros_like(vec_ref)
    whole = stripe_marks(width, BF)
    for i, at in enumerate((6, 4, 5, 10, 8, 9), 3):
        lanes = slice(0, 128) if i < 8 else slice(128, 256)
        vec_ref[:, i % 8, lanes] = cut(vg_ref[at : at + 1, :], *whole)
    broad = width * fan // STRIPES
    total = jnp.zeros((STRIPES, 128), F32)
    for f in range(fan):
        column_at = lax.broadcasted_iota(jnp.int32, (STRIPES, width), 1) + f * width
        stripe = lax.broadcasted_iota(jnp.int32, (STRIPES, width), 0)
        mine = (column_at >= stripe * broad) & (column_at < stripe * broad + broad)
        place = lax.broadcasted_iota(jnp.int32, (128, width), 0)
        marks = lax.broadcasted_iota(jnp.int32, (128, width), 1) + f * width
        total += cut(vg_ref[f : f + 1, :], mine, (marks % broad == place).astype(BF))
    vec_ref[:, (VECTORS - 1) % 8, 128:256] = total


def cut_vectors(vg, fan):
    return pl.pallas_call(
        lambda *refs: cut_vectors_kernel(*refs, fan=fan),
        out_shape=jax.ShapeDtypeStruct((STRIPES, 8, vg.shape[1]), F32),
        compiler_params=big(24),
        cost_estimate=pl.CostEstimate(flops=100000000000, bytes_accessed=1000000, transcendentals=0),
        name="cut_vectors",
    )(vg)


def project_back_kernel(where_ref, vec_in_ref, w, xt, tt, d_hbm, pos_hbm, *refs, fan, hops):
    keep_ref, send_ref = refs[hops : hops + 2]
    d, pos, vec_ref, chunk_fetch = refs[-4:]
    width, rows = xt.shape
    buckets = tt.shape[1]
    part = width // STRIPES
    own = where_ref[1]
    copy = pltpu.make_async_copy

    def chunk(i):
        some = [copy(d_hbm.at[i], d.at[i], chunk_fetch.at[0, i])]
        if i < 2:
            some += [copy(pos_hbm.at[i], pos.at[i], chunk_fetch.at[1, i])]
        return some

    for one in chunk(0) + chunk(1) + chunk(2):
        one.start()
    for r, out in enumerate(refs[hops + 2 : -4]):
        at = where_ref[3] ^ r
        out[0] = sum(ref[at].astype(F32) for ref in refs[:hops]).astype(BF)
    vec_ref[...] = vec_in_ref[...]
    marks = stripe_marks(width, BF)
    table = jnp.zeros((width, buckets), F32)
    ones = jnp.ones((8, rows), BF)
    for i in range(3):
        for one in chunk(i):
            one.wait()
        line = dot(ones, d[i], NN)
        grad = dot(xt[...], d[i], NN)
        if i < 2:
            low = pos[i]
            table = table + dot(w.at[i].reshape(width, width)[...], low, NN)
            line = line + dot(jnp.ones((8, buckets), BF), low, NT)
            grad = grad + dot(tt[...], low, NT)
        place = slice(i * part, (i + 1) * part)
        halves_to(keep_ref.at[:, place], send_ref.at[:, place], grad, own)
        vec_ref[:, i, 0:128] = cut(line[0:1], *marks)
    table_at, vector_at = slice(3 * part, 3 * part + 8), slice(3 * part + 8, 3 * part + 16)
    halves_to(keep_ref.at[:, table_at], send_ref.at[:, table_at], table.T, own)
    halves_to(keep_ref.at[:, vector_at], send_ref.at[:, vector_at], vec_ref[...].reshape(STRIPES * 8, width), own)


def project_back(where, d, pos, mats, xt, tt, vec, fan, parts=()):
    width, rows = xt.shape
    part = width // STRIPES
    buckets = tt.shape[1]
    hbm = pl.BlockSpec(memory_space=pl.ANY)
    vmem = pl.BlockSpec(memory_space=pltpu.VMEM)
    half = jax.ShapeDtypeStruct((STRIPES // 2, part * 3 + 16, width), BF)
    sem = pltpu.SemaphoreType.DMA
    return pl.pallas_call(
        lambda *refs: project_back_kernel(*refs, fan=fan, hops=len(parts)),
        in_specs=[pl.BlockSpec(memory_space=pltpu.SMEM)] + [vmem] * 4 + [hbm] * 2 + [vmem] * len(parts),
        out_specs=[vmem, vmem] + [vmem] * len(parts),
        out_shape=[pltpu.VMEM(half.shape, half.dtype), pltpu.VMEM(half.shape, half.dtype)]
        + [jax.ShapeDtypeStruct((1,) + part_.shape[1:], BF) for part_ in parts],
        scratch_shapes=[pltpu.VMEM((3, rows, width), BF), pltpu.VMEM((2, width, buckets), BF),
                        pltpu.VMEM((STRIPES, 8, width), F32), sem((2, 3))],
        compiler_params=big(32),
        name="project_back",
    )(where, vec, *[pltpu.with_memory_space_constraint(a, pltpu.VMEM) for a in (mats, xt, tt)],
      *[pltpu.with_memory_space_constraint(a, pltpu.HBM) for a in (d, pos)], *parts)


def token_grad_kernel(fg_ref, d_ref, w_ref, out_ref):
    width = out_ref.shape[1]

    @pl.when(pl.program_id(0) == 0)
    def _():
        out_ref[...] = fg_ref[...]

    out_ref[...] += dot(d_ref[0], w_ref.at[0].reshape(width, width)[...], NT)


def token_grads(fg, d, mats):
    rows, width = fg.shape
    full = pl.BlockSpec((rows, width), lambda g: (0, 0))
    return pl.pallas_call(
        token_grad_kernel,
        grid=(3,),
        in_specs=[full, pl.BlockSpec((1, rows, width), lambda g: (g, 0, 0)),
                  pl.BlockSpec((1,) + mats.shape[1:], lambda g: (g, 0, 0, 0))],
        out_specs=full,
        out_shape=jax.ShapeDtypeStruct((rows, width), F32),
        compiler_params=big(24),
        cost_estimate=cost(2 << 30, 10 << 20),
        name="token_grads",
    )(fg, d, mats)


def near_hop_kernel(where_ref, *refs, groups):
    keeps, gots, outs = refs[:groups], refs[groups : 2 * groups], refs[2 * groups :]
    for r, out in enumerate(outs):
        at = where_ref[2] ^ r
        row = 0
        for keep_ref, got_ref in zip(keeps, gots):
            rows = keep_ref.shape[1]
            out[0, row : row + rows] = (keep_ref[at].astype(F32) + got_ref[at].astype(F32)).astype(BF)
            row += rows


def near_hop(where, keep, got):
    count, _, width = keep[0].shape
    group = lambda block: pl.BlockSpec((4,) + block.shape[1:], lambda z: (z, 0, 0))
    rows = sum(block.shape[1] for block in keep)
    return pl.pallas_call(
        lambda *refs: near_hop_kernel(*refs, groups=len(keep)),
        grid=(count // 4,),
        in_specs=[pl.BlockSpec(memory_space=pltpu.SMEM)] + [group(block) for block in keep] * 2,
        out_specs=[pl.BlockSpec((1, rows, width), lambda z: (z, 0, 0))] * 4,
        out_shape=[jax.ShapeDtypeStruct((count // 4, rows, width), BF)] * 4,
        compiler_params=big(16),
        name="near_hop",
    )(where, *keep, *got)


def finish_kernel(*refs, parts, vectors):
    ins, outer_ref, mats, lines = refs[:parts], refs[parts], refs[parts + 1 : -vectors - 1], refs[-vectors - 1 : -1]
    refs[-1][...] = outer_ref[0].astype(F32)
    add = lambda rows: sum(ref[0, rows, :].astype(F32) for ref in ins)
    at = 0
    for ref in mats:
        ref[...] = add(slice(at, at + ref.shape[0]))
        at += ref.shape[0]
    tile = add(slice(at, at + 8))
    for i, ref in enumerate(lines):
        lane = 0 if i < 8 else 128
        ref[...] = tile[i % 8, lane : lane + ref.shape[0]]


def finish(parts, outer, mat_rows, sizes):
    width = parts[0].shape[2]
    return pl.pallas_call(
        lambda *refs: finish_kernel(*refs, parts=len(parts), vectors=len(sizes)),
        out_shape=[jax.ShapeDtypeStruct((rows, width), F32) for rows in mat_rows]
        + [jax.ShapeDtypeStruct((size,), F32) for size in sizes]
        + [jax.ShapeDtypeStruct(outer.shape[1:], F32)],
        compiler_params=big(16),
        name="finish",
    )(*parts, outer)


def far_hop_kernel(where_ref, *refs):
    for r, out in enumerate(refs[4:]):
        at = where_ref[3] ^ r
        out[0] = sum(ref[at].astype(F32) for ref in refs[:4]).astype(BF)


def far_hop(where, parts):
    count, rows, width = parts[0].shape
    return pl.pallas_call(
        far_hop_kernel,
        in_specs=[pl.BlockSpec(memory_space=pltpu.SMEM)] + [pl.BlockSpec(memory_space=pltpu.VMEM)] * 4,
        out_shape=[jax.ShapeDtypeStruct((1, rows, width), BF)] * 4,
        compiler_params=big(16),
        cost_estimate=cost(4 * parts[0].size, 10 * parts[0].size),
        name="far_hop",
    )(where, *parts)


def gather_rows(block):
    return lax.all_gather(block, AXES, axis=0, tiled=False)


def scatter_rows(blocks):
    return lax.psum_scatter(blocks, AXES, scatter_dimension=0, tiled=False)


def xor_permute(block, mask, count):
    return lax.ppermute(block, AXES, [(d, d ^ mask) for d in range(count)])


def in_vmem(block):
    return pltpu.with_memory_space_constraint(block, pltpu.VMEM)


class Scatter:
    def __init__(self, where, count, space):
        self.where, self.count, self.space = where, count, space
        self.keep, self.got = [], []

    def add(self, keep, send):
        self.keep.append(keep)
        self.got.append(xor_permute(send, 1, self.count))

    def near(self, *after):
        got = tie(self.got, after)
        keep = [pltpu.with_memory_space_constraint(part, self.space) for part in self.keep]
        parts = near_hop(self.where, keep, [in_vmem(part) for part in got])
        self.keep, self.sent = parts[0], parts[1:]
        self.got = [xor_permute(part, 2 * r, self.count) for r, part in enumerate(self.sent, 1)]

    def far(self, *after):
        got = tie(self.got, after)
        parts = far_hop(self.where, [self.keep] + [in_vmem(part) for part in got])
        self.keep, self.sent = parts[0], parts[1:]
        self.got = [xor_permute(part, 8 * r, self.count) for r, part in enumerate(self.sent, 1)]

    def total(self):
        return sum(part[0].astype(F32) for part in [self.keep] + self.got)


def tie(value, other):
    if isinstance(other, tuple) and not other:
        return value
    return lax.optimization_barrier((value, other))[0]


def scatter_plain(keep, send, parts, count):
    blocks = jnp.stack([keep, send], axis=1).reshape((STRIPES,) + keep.shape[1:])
    sums, at = [], 0
    for part in parts:
        whole = blocks[:, at : at + part]
        rows = STRIPES * part
        flat = whole.reshape(count, rows // count, whole.shape[2])
        sums.append(lax.psum_scatter(flat.astype(F32), AXES, scatter_dimension=0, tiled=False))
        at += part
    return sums


def make_body(counts):
    count = counts[0] * counts[1]
    direct = counts == (8, 4)

    def body(
        tokens, lengths, buckets,
        query_weight, query_bias, key_weight, key_bias, value_weight, value_bias,
        output_weight, output_bias, relative_table, first_gain, first_shift,
        inner_weight, inner_bias, outer_weight, outer_bias, second_gain, second_shift,
        cotangent,
    ):
        rows, width = tokens.shape[1:]
        fan = inner_weight.shape[1] // width
        vectors = (
            query_bias, key_bias, value_bias, output_bias, first_gain, first_shift,
            outer_bias, second_gain, second_shift, inner_bias,
        )
        first_mats = (query_weight, key_weight, value_weight, relative_table)
        second_mats = [outer_weight]
        second_mats += [inner_weight[:, f * width : (f + 1) * width] for f in range(fan)]
        second_mats += [output_weight]

        def vector_rows(pieces):
            lead = pieces[0].shape[:-1]
            tile = jnp.zeros(lead + (8, width), BF)
            for i, piece in enumerate(pieces):
                lane = 0 if i < 8 else 128
                tile = tile.at[..., i % 8, lane : lane + piece.shape[-1]].set(piece)
            return tile

        me = lax.axis_index("wide") * counts[1] + lax.axis_index("narrow")
        if direct:
            first_pack, second_pack = pack(first_mats, vectors, outer_weight, inner_weight, output_weight, fan)
            second_all = gather_rows(second_pack)
            everyone = lambda block, step: jnp.concatenate(
                [block] + [xor_permute(block, step * r, count) for r in (1, 2, 3)]
            )
            near = everyone(everyone(first_pack[None], 8), 2)
            far = xor_permute(near, 1, count)
            where = jnp.stack([me, me & 1, (me >> 1) & 3, me >> 3]).astype(jnp.int32)
        else:
            whole = lambda block: lax.all_gather(block, AXES, axis=0, tiled=True)
            striped = lambda block: whole(block).reshape(STRIPES, -1, width)
            spread = [whole(v).reshape(STRIPES, -1) for v in vectors]
            first_all = jnp.concatenate(
                [striped(m) for m in first_mats] + [vector_rows(spread)], axis=1
            )
            second_all = jnp.concatenate([striped(m) for m in second_mats], axis=1)
            first_all = first_all.reshape((4, 4, 2) + first_all.shape[1:]).transpose(2, 1, 0, 3, 4)
            near, far = first_all.reshape((2, STRIPES // 2) + first_all.shape[3:])
            where = jnp.zeros((4,), jnp.int32)

        flat = tokens.reshape(rows, width)
        bucket_column = jnp.pad(buckets[::-1], (0, 1), constant_values=-1).reshape(-1, 1)
        q, k, v, kr, qr, vecs, mats, onehot, xt, tt = project_all(where, near, far, flat, bucket_column, fan)
        total = lengths[0, 0:1] + lengths[0, 1:2]
        context, probs = attend(total, q, k, v, kr, qr)
        cot = cotangent.reshape(rows, width)
        layer_out, outer_grad, slope, og, low, n1, inv, second, vg = feed_forward(
            vecs, context, flat, cot, second_all, fan
        )
        outer_blocks = outer_grad.reshape(count, -1, width)
        if direct:
            outer_sum = scatter_rows(outer_blocks)
        else:
            outer_out = scatter_rows(outer_blocks.astype(F32))
        inner_keep, inner_send, context_grad, fg, vg = feed_back(
            where, vecs, vg, og, low, slope, second, n1, inv, context, second_all, fan
        )
        vec = cut_vectors(vg, fan)
        if direct:
            inner = Scatter(where, count, pltpu.HBM)
            inner.add(inner_keep, inner_send)
            inner.near(vec)
            context_grad = tie(context_grad, inner.sent)
        d, pos = attend_back(q, k, v, kr, qr, context_grad, probs, onehot, 0, width // 128, ())
        if direct:
            parts = [inner.keep] + [in_vmem(got) for got in inner.got]
            last_keep, last_send, *parts = project_back(where, d, pos, mats, xt, tt, vec, fan, parts)
            inner.keep = parts[0]
            inner.got = [xor_permute(part, 8 * r, count) for r, part in enumerate(parts[1:], 1)]
        else:
            last_keep, last_send = project_back(where, d, pos, mats, xt, tt, vec, fan)

        part = width // STRIPES
        if direct:
            last = Scatter(where, count, pltpu.VMEM)
            last.add(last_keep, last_send)
            last.near()
            tokens_grad = token_grads(fg, tie(d, last.sent), mats)
            last.far(tokens_grad)
            inner.got = tie(inner.got, tokens_grad)
            inner_sum = inner.total()
            inner_parts = [inner_sum[f * part : (f + 1) * part] for f in range(fan + 1)]
            output_out = inner_parts[fan]
            query_out, key_out, value_out, table_out, *pieces, outer_out = finish(
                [last.keep] + [in_vmem(got) for got in last.got],
                outer_sum[None], (part, part, part, 8), [piece.shape[0] for piece in vectors],
            )
        else:
            tokens_grad = token_grads(fg, d, mats)
            inner_parts = scatter_plain(inner_keep, inner_send, (part,) * (fan + 1), count)
            output_out = inner_parts[fan]
            query_out, key_out, value_out, table_out, _ = scatter_plain(
                last_keep, last_send, (part,) * 3 + (8, 8), count
            )
            blocks = jnp.stack([last_keep, last_send], axis=1).reshape(STRIPES, -1, width)
            tile = blocks[:, 3 * part + 8 : 3 * part + 16].astype(F32)
            pieces = []
            for i, piece in enumerate(vectors):
                lane = 0 if i < 8 else 128
                length = piece.shape[0] * count // STRIPES
                line = tile[:, i % 8, lane : lane + length].reshape(-1)
                pieces.append(lax.psum_scatter(line, AXES, scatter_dimension=0, tiled=True))
        inner_out = jnp.concatenate(inner_parts[:fan], axis=1)
        (qb, kb, vb, ob, g1, s1, outb, g2, s2, inb) = pieces
        return (
            layer_out.reshape(tokens.shape), tokens_grad.reshape(tokens.shape),
            query_out, qb, key_out, kb, value_out, vb, output_out, ob, table_out, g1, s1,
            inner_out, inb, outer_out, outb, g2, s2,
        )

    return body


def solution(mesh):
    counts = (mesh.shape["wide"], mesh.shape["narrow"])
    rows3, rows2, rows1 = P(AXES, None, None), P(AXES, None), P(AXES)
    params = (
        rows2, rows1, rows2, rows1, rows2, rows1, rows2, rows1, rows2, rows1, rows1,
        rows2, rows1, rows2, rows1, rows1, rows1,
    )
    return jax.shard_map(
        make_body(counts),
        mesh=mesh,
        in_specs=(rows3, rows2, P()) + params + (rows3,),
        out_specs=(rows3, rows3) + params,
        check_vma=False,
    )
```

```python
import jax
import jax.numpy as jnp
from jax import lax
from jax.experimental import pallas as pl
from jax.experimental.pallas import tpu as pltpu
from jax.sharding import PartitionSpec as P

HD = 64
EPSILON = 1e-05
MASKED = -1000000000.0
AXES = ("wide", "narrow")
BF = jnp.bfloat16
F32 = jnp.float32
NT = (((1,), (1,)), ((), ()))
NN = (((1,), (0,)), ((), ()))
TN = (((0,), (0,)), ((), ()))


def dot(left, right, dims):
    return lax.dot_general(left, right, dims, preferred_element_type=F32)


def half_lanes(block):
    first = lax.broadcasted_iota(jnp.int32, (1, 128), 1) < HD
    return jnp.where(first, block, 0).astype(BF), jnp.where(first, 0, block).astype(BF)


def stacked(block):
    return jnp.concatenate(half_lanes(block), axis=0)


def attend_kernel(tot_ref, q_ref, k_ref, v_ref, kr_ref, qr_ref, c_ref, p_ref, t_ref, *, rows, tile):
    span = rows + tile
    scale = (3.0 * HD) ** (-0.5) * 1.4426950408889634
    column = lax.broadcasted_iota(jnp.int32, (1, rows), 1)
    valid = column < tot_ref[0]

    def skewed(grid_scores):
        return pltpu.roll(grid_scores, span - (tile - 1), 1, stride=1, stride_axis=0)[:, :rows]

    values = stacked(v_ref[...])

    def places(b):
        sl = pl.ds(pl.multiple_of(b * tile, tile), tile)
        return sl, pl.ds(pl.multiple_of(rows - tile - b * tile, tile), span)

    def rows_of_keys(b, carry):
        sl, window = places(b)
        grid_scores = dot(stacked(k_ref[sl, :]), qr_ref[window, :], NT)
        for head in range(2):
            t_ref[head, sl, :] = skewed(grid_scores[head * tile : (head + 1) * tile])
        return carry

    def rows_of_queries(b, carry):
        sl, window = places(b)
        q = stacked(q_ref[sl, :])
        grid_scores = dot(q, kr_ref[window, :], NT)
        raw = (
            dot(q, k_ref[...], NT)
            + jnp.concatenate([skewed(grid_scores[:tile]), skewed(grid_scores[tile:])], axis=0)
            + jnp.concatenate([t_ref[0, :, sl].T, t_ref[1, :, sl].T], axis=0)
        )
        scores = jnp.where(valid, raw * scale, MASKED)
        top = jnp.max(scores, axis=-1, keepdims=True)
        expd = jnp.exp2(scores - top)
        probs = (expd * (1.0 / jnp.sum(expd, axis=-1, keepdims=True))).astype(BF)
        p_ref[0, sl, :] = probs[:tile]
        p_ref[1, sl, :] = probs[tile:]
        both = jnp.concatenate([probs[:tile], probs[tile:]], axis=1)
        c_ref[sl, :] = dot(both, values, NN).astype(BF)
        return carry

    lax.fori_loop(0, rows // tile, rows_of_keys, 0)
    lax.fori_loop(0, rows // tile, rows_of_queries, 0)


def attend(total, q, k, v, kr, qr):
    rows, width = q.shape
    groups = width // 128
    cols = lambda r: pl.BlockSpec((r, 128), lambda p: (0, p))
    return pl.pallas_call(
        lambda *refs: attend_kernel(*refs, rows=rows, tile=rows // 2),
        grid=(groups,),
        in_specs=[pl.BlockSpec(memory_space=pltpu.SMEM)]
        + [cols(rows)] * 3
        + [cols(2 * rows)] * 2,
        out_specs=[cols(rows), pl.BlockSpec((2, rows, rows), lambda p: (p, 0, 0))],
        out_shape=[
            jax.ShapeDtypeStruct((rows, width), BF),
            jax.ShapeDtypeStruct((2 * groups, rows, rows), BF),
        ],
        scratch_shapes=[pltpu.VMEM((2, rows, rows), F32)],
        compiler_params=pltpu.CompilerParams(vmem_limit_bytes=60 << 20),
        cost_estimate=pl.CostEstimate(
            flops=25 << 30, bytes_accessed=12 << 20, transcendentals=12 * rows * rows
        ),
        name="attend",
    )(total, q, k, v, kr, qr)


def attend_back_kernel(
    q_ref, k_ref, v_ref, kr_ref, qr_ref, dc_ref, p_ref, onehot_ref, *refs, rows, tile,
):
    d_ref, pos_ref, ds_ref, dqr_ref, dkr_ref = refs[-5:]
    dq_ref, dk_ref, dv_ref = d_ref.at[0], d_ref.at[1], d_ref.at[2]
    span = rows + tile
    scale = (3.0 * HD) ** (-0.5)
    upper = lax.broadcasted_iota(jnp.int32, (128, 1), 0) < HD
    flip = (
        lax.broadcasted_iota(jnp.int32, (tile, tile), 0)
        + lax.broadcasted_iota(jnp.int32, (tile, tile), 1)
        == tile - 1
    ).astype(BF)
    dkr_ref[...] = jnp.zeros_like(dkr_ref)
    dqr_ref[...] = jnp.zeros_like(dqr_ref)
    zeros = jnp.zeros((tile, tile), F32)
    beside = lambda *parts: jnp.concatenate(parts, axis=1)
    above = lambda *parts: jnp.concatenate(parts, axis=0)

    def unskewed(flipped):
        return pltpu.roll(beside(flipped, zeros), 0, 1, stride=1, stride_axis=0).astype(BF)

    def turned(block):
        across = block.T
        return beside(jnp.where(upper, across, 0), jnp.where(upper, 0, across)).astype(BF)

    keys, queries = stacked(k_ref[...]), stacked(q_ref[...])
    kr, qr = half_lanes(kr_ref[...]), half_lanes(qr_ref[...])
    dvt = jnp.zeros((128, rows), F32)
    for b in range(rows // tile):
        sl = slice(b * tile, (b + 1) * tile)
        low = rows - tile - b * tile
        high = low + span
        dc = dc_ref[sl, :]
        dp = dot(stacked(dc), v_ref[...], NT)
        pb = above(p_ref[0, sl, :], p_ref[1, sl, :])
        p = pb.astype(F32)
        pdp = p * dp
        delta = jnp.sum(pdp, axis=-1, keepdims=True)
        ds = ((pdp - p * delta) * scale).astype(BF)
        dsa, dsb = ds[:tile], ds[tile:]
        ds_ref[0, sl, :] = dsa
        ds_ref[1, sl, :] = dsb
        dvt = dvt + dot(turned(dc.astype(F32)), pb, NN)
        da, db = unskewed(dot(flip, dsa, NN)), unskewed(dot(flip, dsb, NN))
        rel = dot(beside(da, db), above(kr[0][low:high], kr[1][low:high]), NN).astype(BF)
        dq_ref[sl, :] = (dot(beside(dsa, dsb), keys, NN) + dot(flip, rel, NN)).astype(BF)
        dkr_ref[:, low:high] += dot(turned(dot(flip, q_ref[sl, :], NN)), above(da, db), NN)
    dv_ref[...] = dvt.T.astype(BF)
    for b in range(rows // tile):
        sl = slice(b * tile, (b + 1) * tile)
        low = rows - tile - b * tile
        high = low + span
        ta, tb = dot(flip, ds_ref[0, :, sl], NT), dot(flip, ds_ref[1, :, sl], NT)
        da, db = unskewed(ta), unskewed(tb)
        dk = dot(
            beside(ta.astype(BF), tb.astype(BF), da, db),
            above(queries, qr[0][low:high], qr[1][low:high]),
            NN,
        )
        dk_ref[sl, :] = dot(flip, dk.astype(BF), NN).astype(BF)
        dqr_ref[:, low:high] += dot(turned(dot(flip, k_ref[sl, :], NN)), above(da, db), NN)
    pos_ref[0] = dot(dqr_ref[...].astype(BF), onehot_ref[...], NN).astype(BF)
    pos_ref[1] = dot(dkr_ref[...].astype(BF), onehot_ref[...], NN).astype(BF)


def attend_back(q, k, v, kr, qr, dc, probs, onehot, first, groups, before):
    rows, width = q.shape
    buckets = onehot.shape[1]
    cols = lambda r: pl.BlockSpec((r, 128), lambda p: (0, first + p))
    skip = [pl.BlockSpec(memory_space=pl.ANY)] * len(before)
    share = groups / (width // 128)
    return pl.pallas_call(
        lambda *refs: attend_back_kernel(*refs, rows=rows, tile=rows // 2),
        grid=(groups,),
        in_specs=[cols(rows)] * 3
        + [cols(2 * rows)] * 2
        + [cols(rows), pl.BlockSpec((2, rows, rows), lambda p: (first + p, 0, 0)),
           pl.BlockSpec((2 * rows, buckets), lambda p: (0, 0))]
        + skip,
        out_specs=[
            pl.BlockSpec((3, rows, 128), lambda p: (0, 0, first + p)),
            pl.BlockSpec((2, 128, buckets), lambda p: (0, first + p, 0)),
        ],
        out_shape=[
            jax.ShapeDtypeStruct((3, rows, width), BF),
            jax.ShapeDtypeStruct((2, width, buckets), BF),
        ],
        scratch_shapes=[pltpu.VMEM((2, rows, rows), BF)] + [pltpu.VMEM((128, 2 * rows), F32)] * 2,
        compiler_params=pltpu.CompilerParams(vmem_limit_bytes=54 << 20),
        input_output_aliases={8 + i: i for i in range(len(before))},
        cost_estimate=pl.CostEstimate(
            flops=int(40e9 * share), bytes_accessed=int(18e6 * share), transcendentals=0
        ),
        name="attend_back",
    )(q, k, v, kr, qr, dc, probs, onehot, *before)


STRIPES = 32
VECTORS = 10


def cost(flops, moved, transcendentals=0):
    return pl.CostEstimate(flops=flops, bytes_accessed=moved, transcendentals=transcendentals)


def big(megabytes=60):
    return pltpu.CompilerParams(vmem_limit_bytes=megabytes << 20)


def stripe_marks(width, dtype):
    part = width // STRIPES
    column = lax.broadcasted_iota(jnp.int32, (STRIPES, width), 1)
    stripe = lax.broadcasted_iota(jnp.int32, (STRIPES, width), 0)
    owner = (column >= stripe * part) & (column < stripe * part + part)
    place = lax.broadcasted_iota(jnp.int32, (128, width), 0)
    spot = (lax.broadcasted_iota(jnp.int32, (128, width), 1) % part == place).astype(dtype)
    return owner, spot


def pack_kernel(*refs, mats, vectors, fan):
    first_ref, second_ref = refs[-2:]
    at = 0
    for ref in refs[:mats]:
        first_ref[at : at + ref.shape[0], :] = ref[...]
        at += ref.shape[0]
    first_ref[at:, :] = jnp.zeros_like(first_ref[at:, :])
    for i, ref in enumerate(refs[mats : mats + vectors]):
        lane = 0 if i < 8 else 128
        first_ref[at + i % 8 : at + i % 8 + 1, lane : lane + ref.shape[0]] = ref[...].reshape(1, -1)
    outer_ref, inner_ref, output_ref = refs[mats + vectors : mats + vectors + 3]
    width = outer_ref.shape[1]
    at = outer_ref.shape[0]
    second_ref[:at, :] = outer_ref[...]
    for f in range(fan):
        rows = inner_ref.shape[0]
        second_ref[at : at + rows, :] = inner_ref[:, f * width : (f + 1) * width]
        at += rows
    second_ref[at:, :] = output_ref[...]


def pack(mats, vectors, outer, inner, output, fan):
    width = outer.shape[1]
    first = sum(m.shape[0] for m in mats) + 8
    second = outer.shape[0] + fan * inner.shape[0] + output.shape[0]
    return pl.pallas_call(
        lambda *refs: pack_kernel(*refs, mats=len(mats), vectors=len(vectors), fan=fan),
        out_shape=[jax.ShapeDtypeStruct((first, width), BF), jax.ShapeDtypeStruct((second, width), BF)],
        name="pack",
    )(*mats, *vectors, outer, inner, output)


def project_kernel(where_ref, *refs, fan):
    blocks, (x_ref, bucket_ref) = refs[:10], refs[10:12]
    q_ref, k_ref, v_ref, kr_ref, qr_ref, vecs_ref, w_ref, onehot_ref, xt_ref, tt_ref = refs[12:22]
    table_ref, vec_ref = refs[22:]
    step = pl.program_id(0)
    width = x_ref.shape[1]
    span = q_ref.shape[1]
    buckets = onehot_ref.shape[1]
    me = where_ref[0]

    def place(out, near, far):
        for r in range(STRIPES // 2):
            for ref, core in ((near, 0), (far, 1)):
                out[me ^ ((r // 4) * 2 + (r % 4) * 8 + core)] = ref[r]

    for i in range(3):
        place(w_ref.at[i], blocks[2 * i], blocks[2 * i + 1])

    @pl.when(step == 0)
    def _():
        place(table_ref, blocks[6], blocks[7])
        place(vec_ref, blocks[8], blocks[9])
        xt_ref[...] = x_ref[...].T
        tt_ref[...] = table_ref.reshape(buckets, width)[...].T
        index = lax.broadcasted_iota(jnp.int32, onehot_ref.shape, 1)
        onehot_ref[...] = (bucket_ref[...] == index).astype(F32).astype(BF)
        owner, spot = stripe_marks(width, BF)
        vecs_ref[...] = jnp.zeros_like(vecs_ref)

        def spread(block, marks, mine):
            return jnp.sum(jnp.where(mine, dot(block, marks, NN), 0.0), axis=0, keepdims=True)

        for i in range(VECTORS - 1):
            lanes = slice(0, 128) if i < 8 else slice(128, 256)
            vecs_ref[i : i + 1, :] = spread(vec_ref[:, i % 8, lanes], spot, owner)
        block = vec_ref[:, (VECTORS - 1) % 8, 128:256]
        part = width * fan // STRIPES
        for f in range(fan):
            column = lax.broadcasted_iota(jnp.int32, (STRIPES, width), 1) + f * width
            stripe = lax.broadcasted_iota(jnp.int32, (STRIPES, width), 0)
            mine = (column >= stripe * part) & (column < stripe * part + part)
            place_at = lax.broadcasted_iota(jnp.int32, (128, width), 0)
            marks = lax.broadcasted_iota(jnp.int32, (128, width), 1) + f * width
            marks = (marks % part == place_at).astype(BF)
            row = VECTORS - 1 + f
            vecs_ref[row : row + 1, :] = spread(block, marks, mine)

    x = x_ref[...]
    table = table_ref.reshape(buckets, width)[...]
    columns = pl.ds(pl.multiple_of(step * span, 128), span)
    bias = [vecs_ref[i : i + 1, columns] for i in range(3)]
    mats = [w_ref.at[i].reshape(width, span)[...] for i in range(3)]
    for i, out in enumerate((q_ref, k_ref, v_ref)):
        out[...] = (dot(x, mats[i], NN) + bias[i]).astype(BF)
    for i, out in ((0, qr_ref), (1, kr_ref)):
        pos = (dot(table, mats[i], NN) + bias[i]).astype(BF)
        out[...] = dot(onehot_ref[...], pos, NN).astype(BF)


def project_all(where, near, far, x, bucket_column, fan):
    rows, width = x.shape
    part = width // STRIPES
    span = 256
    weight = lambda i: [pl.BlockSpec((STRIPES // 2, part, span), lambda p: (0, i, p))] * 2
    small = lambda i: [pl.BlockSpec((STRIPES // 2, 8, width), lambda p: (0, i, 0))] * 2
    buckets = 8 * STRIPES
    whole = lambda shape: pl.BlockSpec(shape, lambda p: (0,) * len(shape))
    cols = lambda r: pl.BlockSpec((r, span), lambda p: (0, p))
    shape = jax.ShapeDtypeStruct
    out = lambda r: shape((r, width), BF)
    return pl.pallas_call(
        lambda *refs: project_kernel(*refs, fan=fan),
        grid=(width // span,),
        in_specs=[pl.BlockSpec(memory_space=pltpu.SMEM)] + weight(0) + weight(1) + weight(2)
        + small(3 * part // 8) + small(3 * part // 8 + 1)
        + [whole((rows, width)), whole((2 * rows, 1))],
        out_specs=[cols(rows)] * 3 + [cols(2 * rows)] * 2
        + [whole((16, width)), pl.BlockSpec((3, STRIPES, part, span), lambda p: (0, 0, 0, p)),
           whole((2 * rows, buckets)), whole((width, rows)), whole((width, buckets))],
        out_shape=[out(rows)] * 3 + [out(2 * rows)] * 2
        + [shape((16, width), F32), shape((3, STRIPES, part, width), BF), shape((2 * rows, buckets), BF),
           shape((width, rows), BF), shape((width, buckets), BF)],
        scratch_shapes=[pltpu.VMEM((STRIPES, 8, width), BF)] * 2,
        compiler_params=big(),
        cost_estimate=cost(4 << 30, 12 << 20),
        name="project",
    )(where, *([near, far] * 5), x, bucket_column)


def normal_parts(hidden):
    centered = hidden - jnp.mean(hidden, axis=-1, keepdims=True)
    inverse = lax.rsqrt(jnp.mean(centered * centered, axis=-1, keepdims=True) + EPSILON)
    return centered * inverse, inverse


def normal_back(upstream, normed, inverse, gain):
    scaled = upstream * gain
    return inverse * (
        scaled
        - jnp.mean(scaled, axis=-1, keepdims=True)
        - normed * jnp.mean(scaled * normed, axis=-1, keepdims=True)
    )


def halves_to(keep_ref, send_ref, grad, own):
    part = keep_ref.shape[1]
    blocks = grad.reshape((grad.shape[0] // (2 * part), 2, part, grad.shape[1]))
    even, odd = blocks[:, 0].astype(BF), blocks[:, 1].astype(BF)

    @pl.when(own == 0)
    def _():
        keep_ref[...] = even
        send_ref[...] = odd

    @pl.when(own != 0)
    def _():
        keep_ref[...] = odd
        send_ref[...] = even


def feed_forward_kernel(vecs_ref, ctx_hbm, x_hbm, cot_hbm, packed_hbm,
                        out_hbm, outer_hbm, slope_hbm, og_hbm, low_hbm, n1_hbm, inv_hbm, second_hbm, vg_ref,
                        ctx, x, cot, wo, wi, w2, act, slope, low, og, n1, inv, acc, out, stage,
                        fetch, chunk_fetch, flush, slope_flush, outer_flush, *, fan):
    rows, width = ctx.shape
    part = width // STRIPES
    vec = lambda i: vecs_ref[i : i + 1, :]
    column = lambda a: jnp.sum(a, axis=0, keepdims=True)
    copy = pltpu.make_async_copy
    ins = [copy(ctx_hbm, ctx, fetch.at[0]),
           copy(packed_hbm.at[:, pl.ds(2 * fan * part, part), :], wo, fetch.at[1]),
           copy(x_hbm, x, fetch.at[2]), copy(cot_hbm, cot, fetch.at[3])]

    def chunk_copies(f):
        inner = pl.ds(pl.multiple_of((fan + f) * part, 8), part)
        outer = pl.ds(f * (STRIPES // fan), STRIPES // fan)
        return (copy(packed_hbm.at[:, inner, :], wi.at[f], chunk_fetch.at[0, f]),
                copy(packed_hbm.at[outer, pl.ds(0, fan * part), :], w2.at[f], chunk_fetch.at[1, f]))

    for one in ins[:3]:
        one.start()
    for f in range(fan):
        for one in chunk_copies(f):
            one.start()
    ins[3].start()
    outs = [copy(n1, n1_hbm, flush.at[0]), copy(inv, inv_hbm, flush.at[1]), copy(low, low_hbm, flush.at[2]),
            copy(out, out_hbm, flush.at[3]), copy(acc, second_hbm, flush.at[4]), copy(og, og_hbm, flush.at[5])]
    vg_ref[...] = jnp.zeros_like(vg_ref)
    ins[0].wait()
    ins[1].wait()
    attended = dot(ctx[...], wo.reshape(width, width)[...], NN) + vec(3)
    ins[2].wait()
    normed, inverse = normal_parts(x[...].astype(F32) + attended)
    n1[...] = normed
    inv[...] = jnp.broadcast_to(inverse, inv.shape)
    start = normed * vec(4) + vec(5)
    low[...] = start.astype(BF)
    acc[...] = start + vec(6)
    for one in outs[:3]:
        one.start()

    def slope_copy(f):
        return copy(slope.at[f], slope_hbm.at[f], slope_flush.at[f])

    def forward(f, carry):
        for one in chunk_copies(f):
            one.wait()
        pre = dot(low[...], wi.at[f].reshape(width, width)[...], NN) + vecs_ref[pl.ds(9 + f, 1), :]
        half = 0.5 + 0.5 * lax.erf(pre * 0.7071067811865476)
        active = (pre * half).astype(BF)
        act[f] = active
        slope[f] = (half + pre * (jnp.exp(-0.5 * pre * pre) * 0.3989422804014327)).astype(BF)
        slope_copy(f).start()
        acc[...] += dot(active, w2.at[f].reshape(width, width)[...], NN)
        return carry

    lax.fori_loop(0, fan, forward, 0)
    normed, inverse = normal_parts(acc[...])
    out[...] = (normed * vec(7) + vec(8)).astype(BF)
    outs[3].start()
    ins[3].wait()
    upstream = cot[...].astype(F32)
    vg_ref[8:9, :] = column(upstream * normed)
    vg_ref[9:10, :] = column(upstream)
    second = normal_back(upstream, normed, inverse, vec(7))
    acc[...] = second
    outs[4].start()
    og[...] = second.astype(BF)
    outs[5].start()
    vg_ref[10:11, :] = column(og[...].astype(F32))

    def outer_copy(f):
        return copy(stage.at[f % 2], outer_hbm.at[pl.ds(pl.multiple_of(f * width, 8), width), :],
                    outer_flush.at[f % 2])

    def outer_grad(f, carry):
        @pl.when(f >= 2)
        def _():
            outer_copy(f - 2).wait()

        stage[f % 2] = dot(act[f], og[...], TN).astype(BF)
        outer_copy(f).start()
        return carry

    lax.fori_loop(0, fan, outer_grad, 0)
    for one in outs:
        one.wait()
    for f in range(fan):
        slope_copy(f).wait()
    for f in (fan - 2, fan - 1):
        outer_copy(f).wait()


def feed_forward(vecs, ctx, x, cot, packed, fan):
    rows, width = x.shape
    part = width // STRIPES
    shape = jax.ShapeDtypeStruct
    hbm = pl.BlockSpec(memory_space=pl.ANY)
    vmem = pl.BlockSpec(memory_space=pltpu.VMEM)
    low, high = pltpu.VMEM((rows, width), BF), pltpu.VMEM((rows, width), F32)
    sem = pltpu.SemaphoreType.DMA
    return pl.pallas_call(
        lambda *refs: feed_forward_kernel(*refs, fan=fan),
        in_specs=[vmem] + [hbm] * 4,
        out_specs=[hbm] * 8 + [vmem],
        out_shape=[shape((rows, width), BF), shape((fan * width, width), BF), shape((fan, rows, width), BF),
                   shape((rows, width), BF), shape((rows, width), BF), shape((rows, width), F32),
                   shape((rows, 128), F32), shape((rows, width), F32), shape((16, width), F32)],
        scratch_shapes=[low, low, low, pltpu.VMEM((STRIPES, part, width), BF),
                        pltpu.VMEM((fan, STRIPES, part, width), BF),
                        pltpu.VMEM((fan, STRIPES // fan, part * fan, width), BF),
                        pltpu.VMEM((fan, rows, width), BF), pltpu.VMEM((fan, rows, width), BF), low, low,
                        high, pltpu.VMEM((rows, 128), F32), high, low, pltpu.VMEM((2, width, width), BF),
                        sem((4,)), sem((2, fan)), sem((6,)), sem((fan,)), sem((2,))],
        compiler_params=big(),
        name="feed_forward",
    )(vecs, ctx, x, cot, packed)


def feed_back_kernel(where_ref, vecs_ref, vg_in_ref, og_hbm, low_hbm, slope_hbm, second_hbm, n1_hbm, inv_hbm,
                     ctx_hbm, packed_hbm, keep_hbm, send_hbm, cg_hbm, fg_hbm, vg_ref,
                     og, low, slope, acc, n1, inv, ctx, wo, wi, w2, turned, cg, fg, keep, send,
                     fetch, chunk_fetch, flush, keep_flush, *, fan):
    rows, width = ctx.shape
    part = width // STRIPES
    own = where_ref[1]
    column = lambda a: jnp.sum(a, axis=0, keepdims=True)
    copy = pltpu.make_async_copy

    def chunk_copies(f):
        inner = pl.ds(pl.multiple_of((fan + f) * part, 8), part)
        outer = pl.ds(f * (STRIPES // fan), STRIPES // fan)
        return (copy(packed_hbm.at[outer, pl.ds(0, fan * part), :], w2.at[f], chunk_fetch.at[0, f]),
                copy(slope_hbm.at[f], slope.at[f], chunk_fetch.at[1, f]),
                copy(packed_hbm.at[:, inner, :], wi.at[f], chunk_fetch.at[2, f]))

    ins = [copy(og_hbm, og, fetch.at[0]), copy(low_hbm, low, fetch.at[1]), copy(second_hbm, acc, fetch.at[2]),
           copy(ctx_hbm, ctx, fetch.at[3]), copy(n1_hbm, n1, fetch.at[4]), copy(inv_hbm, inv, fetch.at[5]),
           copy(packed_hbm.at[:, pl.ds(2 * fan * part, part), :], wo, fetch.at[6])]
    for one in [ins[0], *chunk_copies(0), ins[1], ins[2]]:
        one.start()
    for f in range(1, fan):
        for one in chunk_copies(f):
            one.start()
    for one in ins[3:]:
        one.start()
    vg_ref[...] = vg_in_ref[...]
    ins[1].wait()
    turned[...] = low[...].T
    ins[0].wait()
    ins[2].wait()

    def keep_copies(f):
        place = pl.ds(pl.multiple_of(f * part, 8), part)
        return (copy(keep.at[f % 2], keep_hbm.at[:, place, :], keep_flush.at[0, f % 2]),
                copy(send.at[f % 2], send_hbm.at[:, place, :], keep_flush.at[1, f % 2]))

    def leave(f, grad):
        @pl.when(f >= 2)
        def _():
            for one in keep_copies(f - 2):
                one.wait()

        halves_to(keep.at[f % 2], send.at[f % 2], grad, own)
        for one in keep_copies(f):
            one.start()

    def backward(f, carry):
        for one in chunk_copies(f):
            one.wait()
        grad = dot(og[...], w2.at[f].reshape(width, width)[...], NT) * slope[f].astype(F32)
        ig = grad.astype(BF)
        acc[...] += dot(ig, wi.at[f].reshape(width, width)[...], NT)
        vg_ref[pl.ds(f, 1), :] = column(ig.astype(F32))
        leave(f, dot(turned[...], ig, NN))
        return carry

    lax.fori_loop(0, fan, backward, 0)
    for one in ins[3:]:
        one.wait()
    total, normed = acc[...], n1[...]
    grad = normal_back(total, normed, inv[:, 0:1], vecs_ref[4:5, :])
    ag = grad.astype(BF)
    leave(fan, dot(ctx[...], ag, TN))
    cg[...] = dot(ag, wo.reshape(width, width)[...], NT).astype(BF)
    fg[...] = grad
    outs = [copy(cg, cg_hbm, flush.at[0]), copy(fg, fg_hbm, flush.at[1])]
    for one in outs:
        one.start()
    vg_ref[4:5, :] = column(total * normed)
    vg_ref[5:6, :] = column(total)
    vg_ref[6:7, :] = column(ag.astype(F32))
    for one in outs:
        one.wait()
    for f in (fan - 1, fan):
        for one in keep_copies(f):
            one.wait()


def feed_back(where, vecs, vg, og, low, slope, second, n1, inv, ctx, packed, fan):
    rows, width = ctx.shape
    part = width // STRIPES
    shape = jax.ShapeDtypeStruct
    hbm = pl.BlockSpec(memory_space=pl.ANY)
    vmem = pl.BlockSpec(memory_space=pltpu.VMEM)
    half = shape((STRIPES // 2, part * (fan + 1), width), BF)
    thin, wide = pltpu.VMEM((rows, width), BF), pltpu.VMEM((rows, width), F32)
    sem = pltpu.SemaphoreType.DMA
    return pl.pallas_call(
        lambda *refs: feed_back_kernel(*refs, fan=fan),
        in_specs=[pl.BlockSpec(memory_space=pltpu.SMEM), vmem, vmem] + [hbm] * 8,
        out_specs=[hbm] * 4 + [vmem],
        out_shape=[half, half, shape((rows, width), BF), shape((rows, width), F32), shape(vg.shape, F32)],
        scratch_shapes=[thin, thin, pltpu.VMEM((fan, rows, width), BF), wide, wide,
                        pltpu.VMEM((rows, 128), F32), thin, pltpu.VMEM((STRIPES, part, width), BF),
                        pltpu.VMEM((fan, STRIPES, part, width), BF),
                        pltpu.VMEM((fan, STRIPES // fan, part * fan, width), BF),
                        pltpu.VMEM((width, rows), BF), thin, wide]
        + [pltpu.VMEM((2, STRIPES // 2, part, width), BF)] * 2
        + [sem((7,)), sem((3, fan)), sem((2,)), sem((2, 2))],
        compiler_params=big(),
        name="feed_back",
    )(where, vecs, vg, og, low, slope, second, n1, inv, ctx, packed)


def cut(row, mine, marks):
    return dot(jnp.where(mine, jnp.broadcast_to(row, mine.shape), 0.0).astype(BF), marks, NT)


def cut_vectors_kernel(vg_ref, vec_ref, *, fan):
    width = vg_ref.shape[1]
    vec_ref[...] = jnp.zeros_like(vec_ref)
    whole = stripe_marks(width, BF)
    for i, at in enumerate((6, 4, 5, 10, 8, 9), 3):
        lanes = slice(0, 128) if i < 8 else slice(128, 256)
        vec_ref[:, i % 8, lanes] = cut(vg_ref[at : at + 1, :], *whole)
    broad = width * fan // STRIPES
    total = jnp.zeros((STRIPES, 128), F32)
    for f in range(fan):
        column_at = lax.broadcasted_iota(jnp.int32, (STRIPES, width), 1) + f * width
        stripe = lax.broadcasted_iota(jnp.int32, (STRIPES, width), 0)
        mine = (column_at >= stripe * broad) & (column_at < stripe * broad + broad)
        place = lax.broadcasted_iota(jnp.int32, (128, width), 0)
        marks = lax.broadcasted_iota(jnp.int32, (128, width), 1) + f * width
        total += cut(vg_ref[f : f + 1, :], mine, (marks % broad == place).astype(BF))
    vec_ref[:, (VECTORS - 1) % 8, 128:256] = total


def cut_vectors(vg, fan):
    return pl.pallas_call(
        lambda *refs: cut_vectors_kernel(*refs, fan=fan),
        out_shape=jax.ShapeDtypeStruct((STRIPES, 8, vg.shape[1]), F32),
        compiler_params=big(24),
        cost_estimate=pl.CostEstimate(flops=100000000000, bytes_accessed=1000000, transcendentals=0),
        name="cut_vectors",
    )(vg)


def project_back_kernel(where_ref, vec_in_ref, w, xt, tt, d_hbm, pos_hbm, *refs, fan, hops):
    keep_ref, send_ref = refs[hops : hops + 2]
    d, pos, vec_ref, grad_ref, line_ref, table_ref, chunk_fetch = refs[-7:]
    width, rows = xt.shape
    buckets = tt.shape[1]
    part = width // STRIPES
    own = where_ref[1]
    copy = pltpu.make_async_copy

    def fetch_d(i):
        return copy(d_hbm.at[i], d.at[i], chunk_fetch.at[0, i])

    def fetch_pos(i):
        return copy(pos_hbm.at[i], pos.at[i], chunk_fetch.at[1, i])

    for one in (fetch_d(0), fetch_pos(0), fetch_d(1), fetch_pos(1), fetch_d(2)):
        one.start()
    for r, out in enumerate(refs[hops + 2 : -7]):
        at = where_ref[3] ^ r
        row = 0
        for ref, got in (refs[0:2], refs[2:4])[: hops // 2]:
            rows_here = ref.shape[1]
            out[0, row : row + rows_here] = (ref[at].astype(F32) + got[at].astype(F32)).astype(BF)
            row += rows_here
    vec_ref[...] = vec_in_ref[...]
    table_ref[...] = jnp.zeros_like(table_ref)

    def project(i, carry):
        fetch_d(i).wait()
        grad_ref[...] = dot(xt[...], d[i], NN)
        line_ref[i] = dot(jnp.ones((8, rows), BF), d[i], NN)

        @pl.when(i < 2)
        def _():
            fetch_pos(i).wait()
            grad_ref[...] += dot(tt[...], pos[i], NT)
            line_ref[i] += dot(jnp.ones((8, buckets), BF), pos[i], NT)
            table_ref[...] += dot(w.at[i].reshape(width, width)[...], pos[i], NN)

        place = pl.ds(pl.multiple_of(i * part, 8), part)
        halves_to(keep_ref.at[:, place], send_ref.at[:, place], grad_ref[...], own)
        return carry

    lax.fori_loop(0, 3, project, 0)
    marks = stripe_marks(width, BF)
    for i in range(3):
        vec_ref[:, i, 0:128] = cut(line_ref[i, 0:1], *marks)
    table_at, vector_at = slice(3 * part, 3 * part + 8), slice(3 * part + 8, 3 * part + 16)
    halves_to(keep_ref.at[:, table_at], send_ref.at[:, table_at], table_ref[...].T, own)
    halves_to(keep_ref.at[:, vector_at], send_ref.at[:, vector_at], vec_ref[...].reshape(STRIPES * 8, width), own)


def project_back(where, d, pos, mats, xt, tt, vec, fan, parts=()):
    width, rows = xt.shape
    part = width // STRIPES
    buckets = tt.shape[1]
    hbm = pl.BlockSpec(memory_space=pl.ANY)
    vmem = pl.BlockSpec(memory_space=pltpu.VMEM)
    half = jax.ShapeDtypeStruct((STRIPES // 2, part * 3 + 16, width), BF)
    sem = pltpu.SemaphoreType.DMA
    return pl.pallas_call(
        lambda *refs: project_back_kernel(*refs, fan=fan, hops=len(parts)),
        in_specs=[pl.BlockSpec(memory_space=pltpu.SMEM)] + [vmem] * 4 + [hbm] * 2 + [vmem] * len(parts),
        out_specs=[vmem, vmem] + [vmem] * len(parts),
        out_shape=[pltpu.VMEM(half.shape, half.dtype), pltpu.VMEM(half.shape, half.dtype)]
        + [jax.ShapeDtypeStruct((1, sum(part_.shape[1] for part_ in parts[::2]), width), BF)] * len(parts),
        scratch_shapes=[pltpu.VMEM((3, rows, width), BF), pltpu.VMEM((2, width, buckets), BF),
                        pltpu.VMEM((STRIPES, 8, width), F32), pltpu.VMEM((width, width), F32),
                        pltpu.VMEM((3, 8, width), F32), pltpu.VMEM((width, buckets), F32), sem((2, 3))],
        compiler_params=big(32),
        name="project_back",
    )(where, vec, *[pltpu.with_memory_space_constraint(a, pltpu.VMEM) for a in (mats, xt, tt)],
      *[pltpu.with_memory_space_constraint(a, pltpu.HBM) for a in (d, pos)], *parts)


def token_grad_kernel(fg_ref, d_ref, w_ref, out_ref):
    width = out_ref.shape[1]

    @pl.when(pl.program_id(0) == 0)
    def _():
        out_ref[...] = fg_ref[...]

    out_ref[...] += dot(d_ref[0], w_ref.at[0].reshape(width, width)[...], NT)


def token_grads(fg, d, mats):
    rows, width = fg.shape
    full = pl.BlockSpec((rows, width), lambda g: (0, 0))
    return pl.pallas_call(
        token_grad_kernel,
        grid=(3,),
        in_specs=[full, pl.BlockSpec((1, rows, width), lambda g: (g, 0, 0)),
                  pl.BlockSpec((1,) + mats.shape[1:], lambda g: (g, 0, 0, 0))],
        out_specs=full,
        out_shape=jax.ShapeDtypeStruct((rows, width), F32),
        compiler_params=big(24),
        cost_estimate=cost(2 << 30, 10 << 20),
        name="token_grads",
    )(fg, d, mats)


def near_hop_kernel(where_ref, *refs, groups):
    keeps, gots, outs = refs[:groups], refs[groups : 2 * groups], refs[2 * groups :]
    for r, out in enumerate(outs):
        at = where_ref[2] ^ r
        row = 0
        for keep_ref, got_ref in zip(keeps, gots):
            rows = keep_ref.shape[1]
            out[0, row : row + rows] = (keep_ref[at].astype(F32) + got_ref[at].astype(F32)).astype(BF)
            row += rows


def near_hop(where, keep, got):
    count, _, width = keep[0].shape
    group = lambda block: pl.BlockSpec((4,) + block.shape[1:], lambda z: (z, 0, 0))
    rows = sum(block.shape[1] for block in keep)
    return pl.pallas_call(
        lambda *refs: near_hop_kernel(*refs, groups=len(keep)),
        grid=(count // 4,),
        in_specs=[pl.BlockSpec(memory_space=pltpu.SMEM)] + [group(block) for block in keep] * 2,
        out_specs=[pl.BlockSpec((1, rows, width), lambda z: (z, 0, 0))] * 4,
        out_shape=[jax.ShapeDtypeStruct((count // 4, rows, width), BF)] * 4,
        compiler_params=big(16),
        name="near_hop",
    )(where, *keep, *got)


def finish_kernel(*refs, parts, vectors):
    ins, outer_ref, mats, lines = refs[:parts], refs[parts], refs[parts + 1 : -vectors - 1], refs[-vectors - 1 : -1]
    refs[-1][...] = outer_ref[0].astype(F32)
    add = lambda rows: sum(ref[0, rows, :].astype(F32) for ref in ins)
    at = 0
    for ref in mats:
        ref[...] = add(slice(at, at + ref.shape[0]))
        at += ref.shape[0]
    tile = add(slice(at, at + 8))
    for i, ref in enumerate(lines):
        lane = 0 if i < 8 else 128
        ref[...] = tile[i % 8, lane : lane + ref.shape[0]]


def finish(parts, outer, mat_rows, sizes):
    width = parts[0].shape[2]
    return pl.pallas_call(
        lambda *refs: finish_kernel(*refs, parts=len(parts), vectors=len(sizes)),
        out_shape=[jax.ShapeDtypeStruct((rows, width), F32) for rows in mat_rows]
        + [jax.ShapeDtypeStruct((size,), F32) for size in sizes]
        + [jax.ShapeDtypeStruct(outer.shape[1:], F32)],
        compiler_params=big(16),
        name="finish",
    )(*parts, outer)


def first_turn_kernel(where_ref, keep_ref, got_ref, a_keep, a_send, b_keep, b_send):
    y, x = where_ref[2] & 1, where_ref[2] >> 1
    cut = a_keep.shape[1]
    first, second = slice(0, cut), slice(cut, keep_ref.shape[1])
    add = lambda at, rows: (keep_ref[at, rows, :].astype(F32) + got_ref[at, rows, :].astype(F32)).astype(BF)
    for i in range(2):
        a_keep[i] = add(i * 2 + y, first)
        a_send[i] = add(i * 2 + 1 - y, first)
        b_keep[i] = add(x * 2 + i, second)
        b_send[i] = add((1 - x) * 2 + i, second)


def first_turn(where, keep, got, cut):
    count, rows, width = keep.shape
    group = pl.BlockSpec((4, rows, width), lambda z: (z, 0, 0))
    parts = (cut, cut, rows - cut, rows - cut)
    return pl.pallas_call(
        first_turn_kernel,
        grid=(count // 4,),
        in_specs=[pl.BlockSpec(memory_space=pltpu.SMEM), group, group],
        out_specs=[pl.BlockSpec((2, part, width), lambda z: (z, 0, 0)) for part in parts],
        out_shape=[jax.ShapeDtypeStruct((count // 2, part, width), BF) for part in parts],
        compiler_params=big(16),
        name="first_turn",
    )(where, keep, got)


def second_turn_kernel(where_ref, a_ref, a_got, b_ref, b_got, a_keep, a_send, b_keep, b_send):
    y, x = where_ref[2] & 1, where_ref[2] >> 1
    for ref, got, own, keep, send in ((a_ref, a_got, x, a_keep, a_send), (b_ref, b_got, y, b_keep, b_send)):
        for z in range(keep.shape[0]):
            for out, at in ((keep, z * 2 + own), (send, z * 2 + 1 - own)):
                out[z] = (ref[at].astype(F32) + got[at].astype(F32)).astype(BF)


def second_turn(where, a_keep, a_got, b_keep, b_got):
    vmem = pl.BlockSpec(memory_space=pltpu.VMEM)
    shape = lambda block: jax.ShapeDtypeStruct((block.shape[0] // 2,) + block.shape[1:], BF)
    return pl.pallas_call(
        second_turn_kernel,
        in_specs=[pl.BlockSpec(memory_space=pltpu.SMEM)] + [vmem] * 4,
        out_shape=[shape(a_keep)] * 2 + [shape(b_keep)] * 2,
        compiler_params=big(16),
        name="second_turn",
    )(where, a_keep, a_got, b_keep, b_got)


def far_hop_kernel(where_ref, *refs):
    for r, out in enumerate(refs[4:]):
        at = where_ref[3] ^ r
        out[0] = sum(ref[at].astype(F32) for ref in refs[:4]).astype(BF)


def far_hop(where, parts):
    count, rows, width = parts[0].shape
    return pl.pallas_call(
        far_hop_kernel,
        in_specs=[pl.BlockSpec(memory_space=pltpu.SMEM)] + [pl.BlockSpec(memory_space=pltpu.VMEM)] * 4,
        out_shape=[jax.ShapeDtypeStruct((1, rows, width), BF)] * 4,
        compiler_params=big(16),
        cost_estimate=cost(4 * parts[0].size, 10 * parts[0].size),
        name="far_hop",
    )(where, *parts)


def gather_rows(block):
    return lax.all_gather(block, AXES, axis=0, tiled=False)


def scatter_rows(blocks):
    return lax.psum_scatter(blocks, AXES, scatter_dimension=0, tiled=False)


def xor_permute(block, mask, count):
    return lax.ppermute(block, AXES, [(d, d ^ mask) for d in range(count)])


def in_vmem(block):
    return pltpu.with_memory_space_constraint(block, pltpu.VMEM)


class Scatter:
    def __init__(self, where, count, space):
        self.where, self.count, self.space = where, count, space
        self.keep, self.got = [], []

    def add(self, keep, send):
        self.keep.append(keep)
        self.got.append(xor_permute(send, 1, self.count))

    def near(self, *after):
        got = tie(self.got, after)
        keep = [pltpu.with_memory_space_constraint(part, self.space) for part in self.keep]
        parts = near_hop(self.where, keep, [in_vmem(part) for part in got])
        self.keep, self.sent = parts[0], parts[1:]
        self.got = [xor_permute(part, 2 * r, self.count) for r, part in enumerate(self.sent, 1)]

    def far(self, *after):
        got = tie(self.got, after)
        parts = far_hop(self.where, [self.keep] + [in_vmem(part) for part in got])
        self.keep, self.sent = parts[0], parts[1:]
        self.got = [xor_permute(part, 8 * r, self.count) for r, part in enumerate(self.sent, 1)]

    def total(self):
        return sum(part[0].astype(F32) for part in [self.keep] + self.got)


def tie(value, other):
    if isinstance(other, tuple) and not other:
        return value
    return lax.optimization_barrier((value, other))[0]


def scatter_plain(keep, send, parts, count):
    blocks = jnp.stack([keep, send], axis=1).reshape((STRIPES,) + keep.shape[1:])
    sums, at = [], 0
    for part in parts:
        whole = blocks[:, at : at + part]
        rows = STRIPES * part
        flat = whole.reshape(count, rows // count, whole.shape[2])
        sums.append(lax.psum_scatter(flat.astype(F32), AXES, scatter_dimension=0, tiled=False))
        at += part
    return sums


def make_body(counts):
    count = counts[0] * counts[1]
    direct = counts == (8, 4)

    def body(
        tokens, lengths, buckets,
        query_weight, query_bias, key_weight, key_bias, value_weight, value_bias,
        output_weight, output_bias, relative_table, first_gain, first_shift,
        inner_weight, inner_bias, outer_weight, outer_bias, second_gain, second_shift,
        cotangent,
    ):
        rows, width = tokens.shape[1:]
        fan = inner_weight.shape[1] // width
        vectors = (
            query_bias, key_bias, value_bias, output_bias, first_gain, first_shift,
            outer_bias, second_gain, second_shift, inner_bias,
        )
        first_mats = (query_weight, key_weight, value_weight, relative_table)
        second_mats = [outer_weight]
        second_mats += [inner_weight[:, f * width : (f + 1) * width] for f in range(fan)]
        second_mats += [output_weight]

        def vector_rows(pieces):
            lead = pieces[0].shape[:-1]
            tile = jnp.zeros(lead + (8, width), BF)
            for i, piece in enumerate(pieces):
                lane = 0 if i < 8 else 128
                tile = tile.at[..., i % 8, lane : lane + piece.shape[-1]].set(piece)
            return tile

        me = lax.axis_index("wide") * counts[1] + lax.axis_index("narrow")
        if direct:
            first_pack, second_pack = pack(first_mats, vectors, outer_weight, inner_weight, output_weight, fan)
            second_all = gather_rows(second_pack)
            everyone = lambda block, step: jnp.concatenate(
                [block] + [xor_permute(block, step * r, count) for r in (1, 2, 3)]
            )
            near = everyone(everyone(first_pack[None], 8), 2)
            far = xor_permute(near, 1, count)
            where = jnp.stack([me, me & 1, (me >> 1) & 3, me >> 3]).astype(jnp.int32)
        else:
            whole = lambda block: lax.all_gather(block, AXES, axis=0, tiled=True)
            striped = lambda block: whole(block).reshape(STRIPES, -1, width)
            spread = [whole(v).reshape(STRIPES, -1) for v in vectors]
            first_all = jnp.concatenate(
                [striped(m) for m in first_mats] + [vector_rows(spread)], axis=1
            )
            second_all = jnp.concatenate([striped(m) for m in second_mats], axis=1)
            first_all = first_all.reshape((4, 4, 2) + first_all.shape[1:]).transpose(2, 1, 0, 3, 4)
            near, far = first_all.reshape((2, STRIPES // 2) + first_all.shape[3:])
            where = jnp.zeros((4,), jnp.int32)

        flat = tokens.reshape(rows, width)
        bucket_column = jnp.pad(buckets[::-1], (0, 1), constant_values=-1).reshape(-1, 1)
        q, k, v, kr, qr, vecs, mats, onehot, xt, tt = project_all(where, near, far, flat, bucket_column, fan)
        total = lengths[0, 0:1] + lengths[0, 1:2]
        context, probs = attend(total, q, k, v, kr, qr)
        cot = cotangent.reshape(rows, width)
        layer_out, outer_grad, slope, og, low, n1, inv, second, vg = feed_forward(
            vecs, context, flat, cot, second_all, fan
        )
        outer_blocks = outer_grad.reshape(count, -1, width)
        if direct:
            outer_sum = scatter_rows(outer_blocks)
        else:
            outer_out = scatter_rows(outer_blocks.astype(F32))
        inner_keep, inner_send, context_grad, fg, vg = feed_back(
            where, vecs, vg, og, low, slope, second, n1, inv, context, second_all, fan
        )
        vec = cut_vectors(vg, fan)
        if direct:
            inner = Scatter(where, count, pltpu.HBM)
            inner_got = tie(xor_permute(inner_send, 1, count), vec)
            inner_keep = pltpu.with_memory_space_constraint(inner_keep, pltpu.HBM)
            a_keep, a_send, b_keep, b_send = first_turn(where, inner_keep, in_vmem(inner_got), 64)
            a_got, b_got = xor_permute(a_send, 2, count), xor_permute(b_send, 4, count)
            context_grad = tie(context_grad, (a_send, b_send))
        most = width // 128 * 2 // 3
        back = lambda dc, first, pairs, before: attend_back(
            q, k, v, kr, qr, dc, probs, onehot, first, pairs, before
        )
        grads = back(context_grad, 0, most, ())
        if direct:
            a_got, b_got = tie((a_got, b_got), grads[0])
            a_keep, a_send, b_keep, b_send = second_turn(where, a_keep, in_vmem(a_got), b_keep, in_vmem(b_got))
            a_got, b_got = xor_permute(a_send, 4, count), xor_permute(b_send, 2, count)
            context_grad = tie(context_grad, (a_send, b_send))
        d, pos = back(context_grad, most, width // 128 - most, grads)
        if direct:
            parts = [a_keep, in_vmem(a_got), b_keep, in_vmem(b_got)]
            last_keep, last_send, *parts = project_back(where, d, pos, mats, xt, tt, vec, fan, parts)
            inner.keep = parts[0]
            inner_sent = parts[1:]
        else:
            last_keep, last_send = project_back(where, d, pos, mats, xt, tt, vec, fan)

        part = width // STRIPES
        if direct:
            last = Scatter(where, count, pltpu.VMEM)
            last.add(last_keep, last_send)
            last.near()
            inner_sent[2] = tie(inner_sent[2], last.sent)
            inner.got = [xor_permute(part, 8 * r, count) for r, part in enumerate(inner_sent, 1)]
            tokens_grad = token_grads(fg, tie(d, last.sent), mats)
            last.far(tokens_grad)
            inner.got = tie(inner.got, tokens_grad)
            inner_sum = inner.total()
            inner_parts = [inner_sum[f * part : (f + 1) * part] for f in range(fan + 1)]
            output_out = inner_parts[fan]
            query_out, key_out, value_out, table_out, *pieces, outer_out = finish(
                [last.keep] + [in_vmem(got) for got in last.got],
                outer_sum[None], (part, part, part, 8), [piece.shape[0] for piece in vectors],
            )
        else:
            tokens_grad = token_grads(fg, d, mats)
            inner_parts = scatter_plain(inner_keep, inner_send, (part,) * (fan + 1), count)
            output_out = inner_parts[fan]
            query_out, key_out, value_out, table_out, _ = scatter_plain(
                last_keep, last_send, (part,) * 3 + (8, 8), count
            )
            blocks = jnp.stack([last_keep, last_send], axis=1).reshape(STRIPES, -1, width)
            tile = blocks[:, 3 * part + 8 : 3 * part + 16].astype(F32)
            pieces = []
            for i, piece in enumerate(vectors):
                lane = 0 if i < 8 else 128
                length = piece.shape[0] * count // STRIPES
                line = tile[:, i % 8, lane : lane + length].reshape(-1)
                pieces.append(lax.psum_scatter(line, AXES, scatter_dimension=0, tiled=True))
        inner_out = jnp.concatenate(inner_parts[:fan], axis=1)
        (qb, kb, vb, ob, g1, s1, outb, g2, s2, inb) = pieces
        return (
            layer_out.reshape(tokens.shape), tokens_grad.reshape(tokens.shape),
            query_out, qb, key_out, kb, value_out, vb, output_out, ob, table_out, g1, s1,
            inner_out, inb, outer_out, outb, g2, s2,
        )

    return body


def solution(mesh):
    counts = (mesh.shape["wide"], mesh.shape["narrow"])
    rows3, rows2, rows1 = P(AXES, None, None), P(AXES, None), P(AXES)
    params = (
        rows2, rows1, rows2, rows1, rows2, rows1, rows2, rows1, rows2, rows1, rows1,
        rows2, rows1, rows2, rows1, rows1, rows1,
    )
    return jax.shard_map(
        make_body(counts),
        mesh=mesh,
        in_specs=(rows3, rows2, P()) + params + (rows3,),
        out_specs=(rows3, rows3) + params,
        check_vma=False,
    )
```

```python
import jax
import jax.numpy as jnp
from jax import lax
from jax.experimental import pallas as pl
from jax.experimental.pallas import tpu as pltpu
from jax.sharding import PartitionSpec as P

HD = 64
EPSILON = 1e-05
MASKED = -1000000000.0
AXES = ("wide", "narrow")
BF = jnp.bfloat16
F32 = jnp.float32
NT = (((1,), (1,)), ((), ()))
NN = (((1,), (0,)), ((), ()))
TN = (((0,), (0,)), ((), ()))


def dot(left, right, dims):
    return lax.dot_general(left, right, dims, preferred_element_type=F32)


def half_lanes(block):
    first = lax.broadcasted_iota(jnp.int32, (1, 128), 1) < HD
    return jnp.where(first, block, 0).astype(BF), jnp.where(first, 0, block).astype(BF)


def stacked(block):
    return jnp.concatenate(half_lanes(block), axis=0)


def attend_kernel(tot_ref, q_ref, k_ref, v_ref, kr_ref, qr_ref, c_ref, p_ref, t_ref, *, rows, tile):
    span = rows + tile
    scale = (3.0 * HD) ** (-0.5) * 1.4426950408889634
    column = lax.broadcasted_iota(jnp.int32, (1, rows), 1)
    valid = column < tot_ref[0]

    def skewed(grid_scores):
        return pltpu.roll(grid_scores, span - (tile - 1), 1, stride=1, stride_axis=0)[:, :rows]

    values = stacked(v_ref[...])

    def places(b):
        sl = pl.ds(pl.multiple_of(b * tile, tile), tile)
        return sl, pl.ds(pl.multiple_of(rows - tile - b * tile, tile), span)

    def rows_of_keys(b, carry):
        sl, window = places(b)
        grid_scores = dot(stacked(k_ref[sl, :]), qr_ref[window, :], NT)
        for head in range(2):
            t_ref[head, sl, :] = skewed(grid_scores[head * tile : (head + 1) * tile])
        return carry

    def rows_of_queries(b, carry):
        sl, window = places(b)
        q = stacked(q_ref[sl, :])
        grid_scores = dot(q, kr_ref[window, :], NT)
        raw = (
            dot(q, k_ref[...], NT)
            + jnp.concatenate([skewed(grid_scores[:tile]), skewed(grid_scores[tile:])], axis=0)
            + jnp.concatenate([t_ref[0, :, sl].T, t_ref[1, :, sl].T], axis=0)
        )
        scores = jnp.where(valid, raw * scale, MASKED)
        top = jnp.max(scores, axis=-1, keepdims=True)
        expd = jnp.exp2(scores - top)
        probs = (expd * (1.0 / jnp.sum(expd, axis=-1, keepdims=True))).astype(BF)
        p_ref[0, sl, :] = probs[:tile]
        p_ref[1, sl, :] = probs[tile:]
        both = jnp.concatenate([probs[:tile], probs[tile:]], axis=1)
        c_ref[sl, :] = dot(both, values, NN).astype(BF)
        return carry

    lax.fori_loop(0, rows // tile, rows_of_keys, 0)
    lax.fori_loop(0, rows // tile, rows_of_queries, 0)


def attend(total, q, k, v, kr, qr):
    rows, width = q.shape
    groups = width // 128
    cols = lambda r: pl.BlockSpec((r, 128), lambda p: (0, p))
    return pl.pallas_call(
        lambda *refs: attend_kernel(*refs, rows=rows, tile=rows // 2),
        grid=(groups,),
        in_specs=[pl.BlockSpec(memory_space=pltpu.SMEM)]
        + [cols(rows)] * 3
        + [cols(2 * rows)] * 2,
        out_specs=[cols(rows), pl.BlockSpec((2, rows, rows), lambda p: (p, 0, 0))],
        out_shape=[
            jax.ShapeDtypeStruct((rows, width), BF),
            jax.ShapeDtypeStruct((2 * groups, rows, rows), BF),
        ],
        scratch_shapes=[pltpu.VMEM((2, rows, rows), F32)],
        compiler_params=pltpu.CompilerParams(vmem_limit_bytes=60 << 20),
        cost_estimate=pl.CostEstimate(
            flops=25 << 30, bytes_accessed=12 << 20, transcendentals=12 * rows * rows
        ),
        name="attend",
    )(total, q, k, v, kr, qr)


def attend_back_kernel(
    q_ref, k_ref, v_ref, kr_ref, qr_ref, dc_ref, p_ref, onehot_ref, *refs, rows, tile,
):
    d_ref, pos_ref, ds_ref, dqr_ref, dkr_ref = refs[-5:]
    dq_ref, dk_ref, dv_ref = d_ref.at[0], d_ref.at[1], d_ref.at[2]
    span = rows + tile
    scale = (3.0 * HD) ** (-0.5)
    upper = lax.broadcasted_iota(jnp.int32, (128, 1), 0) < HD
    flip = (
        lax.broadcasted_iota(jnp.int32, (tile, tile), 0)
        + lax.broadcasted_iota(jnp.int32, (tile, tile), 1)
        == tile - 1
    ).astype(BF)
    dkr_ref[...] = jnp.zeros_like(dkr_ref)
    dqr_ref[...] = jnp.zeros_like(dqr_ref)
    zeros = jnp.zeros((tile, tile), F32)
    beside = lambda *parts: jnp.concatenate(parts, axis=1)
    above = lambda *parts: jnp.concatenate(parts, axis=0)

    def unskewed(flipped):
        return pltpu.roll(beside(flipped, zeros), 0, 1, stride=1, stride_axis=0).astype(BF)

    def turned(block):
        across = block.T
        return beside(jnp.where(upper, across, 0), jnp.where(upper, 0, across)).astype(BF)

    keys, queries = stacked(k_ref[...]), stacked(q_ref[...])
    kr, qr = half_lanes(kr_ref[...]), half_lanes(qr_ref[...])
    dvt = jnp.zeros((128, rows), F32)
    for b in range(rows // tile):
        sl = slice(b * tile, (b + 1) * tile)
        low = rows - tile - b * tile
        high = low + span
        dc = dc_ref[sl, :]
        dp = dot(stacked(dc), v_ref[...], NT)
        pb = above(p_ref[0, sl, :], p_ref[1, sl, :])
        p = pb.astype(F32)
        pdp = p * dp
        delta = jnp.sum(pdp, axis=-1, keepdims=True)
        ds = ((pdp - p * delta) * scale).astype(BF)
        dsa, dsb = ds[:tile], ds[tile:]
        ds_ref[0, sl, :] = dsa
        ds_ref[1, sl, :] = dsb
        dvt = dvt + dot(turned(dc.astype(F32)), pb, NN)
        da, db = unskewed(dot(flip, dsa, NN)), unskewed(dot(flip, dsb, NN))
        rel = dot(beside(da, db), above(kr[0][low:high], kr[1][low:high]), NN).astype(BF)
        dq_ref[sl, :] = (dot(beside(dsa, dsb), keys, NN) + dot(flip, rel, NN)).astype(BF)
        dkr_ref[:, low:high] += dot(turned(dot(flip, q_ref[sl, :], NN)), above(da, db), NN)
    dv_ref[...] = dvt.T.astype(BF)
    for b in range(rows // tile):
        sl = slice(b * tile, (b + 1) * tile)
        low = rows - tile - b * tile
        high = low + span
        ta, tb = dot(flip, ds_ref[0, :, sl], NT), dot(flip, ds_ref[1, :, sl], NT)
        da, db = unskewed(ta), unskewed(tb)
        dk = dot(
            beside(ta.astype(BF), tb.astype(BF), da, db),
            above(queries, qr[0][low:high], qr[1][low:high]),
            NN,
        )
        dk_ref[sl, :] = dot(flip, dk.astype(BF), NN).astype(BF)
        dqr_ref[:, low:high] += dot(turned(dot(flip, k_ref[sl, :], NN)), above(da, db), NN)
    pos_ref[0] = dot(dqr_ref[...].astype(BF), onehot_ref[...], NN).astype(BF)
    pos_ref[1] = dot(dkr_ref[...].astype(BF), onehot_ref[...], NN).astype(BF)


def attend_back(q, k, v, kr, qr, dc, probs, onehot, first, groups, before):
    rows, width = q.shape
    buckets = onehot.shape[1]
    cols = lambda r: pl.BlockSpec((r, 128), lambda p: (0, first + p))
    skip = [pl.BlockSpec(memory_space=pl.ANY)] * len(before)
    share = groups / (width // 128)
    return pl.pallas_call(
        lambda *refs: attend_back_kernel(*refs, rows=rows, tile=rows // 2),
        grid=(groups,),
        in_specs=[cols(rows)] * 3
        + [cols(2 * rows)] * 2
        + [cols(rows), pl.BlockSpec((2, rows, rows), lambda p: (first + p, 0, 0)),
           pl.BlockSpec((2 * rows, buckets), lambda p: (0, 0))]
        + skip,
        out_specs=[
            pl.BlockSpec((3, rows, 128), lambda p: (0, 0, first + p)),
            pl.BlockSpec((2, 128, buckets), lambda p: (0, first + p, 0)),
        ],
        out_shape=[
            jax.ShapeDtypeStruct((3, rows, width), BF),
            jax.ShapeDtypeStruct((2, width, buckets), BF),
        ],
        scratch_shapes=[pltpu.VMEM((2, rows, rows), BF)] + [pltpu.VMEM((128, 2 * rows), F32)] * 2,
        compiler_params=pltpu.CompilerParams(vmem_limit_bytes=54 << 20),
        input_output_aliases={8 + i: i for i in range(len(before))},
        cost_estimate=pl.CostEstimate(
            flops=int(40e9 * share), bytes_accessed=int(18e6 * share), transcendentals=0
        ),
        name="attend_back",
    )(q, k, v, kr, qr, dc, probs, onehot, *before)


STRIPES = 32
VECTORS = 10


def cost(flops, moved, transcendentals=0):
    return pl.CostEstimate(flops=flops, bytes_accessed=moved, transcendentals=transcendentals)


def big(megabytes=60):
    return pltpu.CompilerParams(vmem_limit_bytes=megabytes << 20)


def stripe_marks(width, dtype):
    part = width // STRIPES
    column = lax.broadcasted_iota(jnp.int32, (STRIPES, width), 1)
    stripe = lax.broadcasted_iota(jnp.int32, (STRIPES, width), 0)
    owner = (column >= stripe * part) & (column < stripe * part + part)
    place = lax.broadcasted_iota(jnp.int32, (128, width), 0)
    spot = (lax.broadcasted_iota(jnp.int32, (128, width), 1) % part == place).astype(dtype)
    return owner, spot


def pack_kernel(*refs, mats, vectors, fan):
    first_ref, second_ref = refs[-2:]
    at = 0
    for ref in refs[:mats]:
        first_ref[at : at + ref.shape[0], :] = ref[...]
        at += ref.shape[0]
    first_ref[at:, :] = jnp.zeros_like(first_ref[at:, :])
    for i, ref in enumerate(refs[mats : mats + vectors]):
        lane = 0 if i < 8 else 128
        first_ref[at + i % 8 : at + i % 8 + 1, lane : lane + ref.shape[0]] = ref[...].reshape(1, -1)
    outer_ref, inner_ref, output_ref = refs[mats + vectors : mats + vectors + 3]
    width = outer_ref.shape[1]
    at = outer_ref.shape[0]
    second_ref[:at, :] = outer_ref[...]
    for f in range(fan):
        rows = inner_ref.shape[0]
        second_ref[at : at + rows, :] = inner_ref[:, f * width : (f + 1) * width]
        at += rows
    second_ref[at:, :] = output_ref[...]


def pack(mats, vectors, outer, inner, output, fan):
    width = outer.shape[1]
    first = sum(m.shape[0] for m in mats) + 8
    second = outer.shape[0] + fan * inner.shape[0] + output.shape[0]
    return pl.pallas_call(
        lambda *refs: pack_kernel(*refs, mats=len(mats), vectors=len(vectors), fan=fan),
        out_shape=[jax.ShapeDtypeStruct((first, width), BF), jax.ShapeDtypeStruct((second, width), BF)],
        name="pack",
    )(*mats, *vectors, outer, inner, output)


def project_kernel(where_ref, *refs, fan):
    blocks, (x_ref, bucket_ref) = refs[:10], refs[10:12]
    q_ref, k_ref, v_ref, kr_ref, qr_ref, vecs_ref, w_ref, onehot_ref, xt_ref, tt_ref = refs[12:22]
    table_ref, vec_ref = refs[22:]
    step = pl.program_id(0)
    width = x_ref.shape[1]
    span = q_ref.shape[1]
    buckets = onehot_ref.shape[1]
    me = where_ref[0]

    def place(out, near, far):
        for r in range(STRIPES // 2):
            for ref, core in ((near, 0), (far, 1)):
                out[me ^ ((r // 4) * 2 + (r % 4) * 8 + core)] = ref[r]

    for i in range(3):
        place(w_ref.at[i], blocks[2 * i], blocks[2 * i + 1])

    @pl.when(step == 0)
    def _():
        place(table_ref, blocks[6], blocks[7])
        place(vec_ref, blocks[8], blocks[9])
        xt_ref[...] = x_ref[...].T
        tt_ref[...] = table_ref.reshape(buckets, width)[...].T
        index = lax.broadcasted_iota(jnp.int32, onehot_ref.shape, 1)
        onehot_ref[...] = (bucket_ref[...] == index).astype(F32).astype(BF)
        owner, spot = stripe_marks(width, BF)
        vecs_ref[...] = jnp.zeros_like(vecs_ref)

        def spread(block, marks, mine):
            return jnp.sum(jnp.where(mine, dot(block, marks, NN), 0.0), axis=0, keepdims=True)

        for i in range(VECTORS - 1):
            lanes = slice(0, 128) if i < 8 else slice(128, 256)
            vecs_ref[i : i + 1, :] = spread(vec_ref[:, i % 8, lanes], spot, owner)
        block = vec_ref[:, (VECTORS - 1) % 8, 128:256]
        part = width * fan // STRIPES
        for f in range(fan):
            column = lax.broadcasted_iota(jnp.int32, (STRIPES, width), 1) + f * width
            stripe = lax.broadcasted_iota(jnp.int32, (STRIPES, width), 0)
            mine = (column >= stripe * part) & (column < stripe * part + part)
            place_at = lax.broadcasted_iota(jnp.int32, (128, width), 0)
            marks = lax.broadcasted_iota(jnp.int32, (128, width), 1) + f * width
            marks = (marks % part == place_at).astype(BF)
            row = VECTORS - 1 + f
            vecs_ref[row : row + 1, :] = spread(block, marks, mine)

    x = x_ref[...]
    table = table_ref.reshape(buckets, width)[...]
    columns = pl.ds(pl.multiple_of(step * span, 128), span)
    bias = [vecs_ref[i : i + 1, columns] for i in range(3)]
    mats = [w_ref.at[i].reshape(width, span)[...] for i in range(3)]
    for i, out in enumerate((q_ref, k_ref, v_ref)):
        out[...] = (dot(x, mats[i], NN) + bias[i]).astype(BF)
    for i, out in ((0, qr_ref), (1, kr_ref)):
        pos = (dot(table, mats[i], NN) + bias[i]).astype(BF)
        out[...] = dot(onehot_ref[...], pos, NN).astype(BF)


def project_all(where, near, far, x, bucket_column, fan):
    rows, width = x.shape
    part = width // STRIPES
    span = 256
    weight = lambda i: [pl.BlockSpec((STRIPES // 2, part, span), lambda p: (0, i, p))] * 2
    small = lambda i: [pl.BlockSpec((STRIPES // 2, 8, width), lambda p: (0, i, 0))] * 2
    buckets = 8 * STRIPES
    whole = lambda shape: pl.BlockSpec(shape, lambda p: (0,) * len(shape))
    cols = lambda r: pl.BlockSpec((r, span), lambda p: (0, p))
    shape = jax.ShapeDtypeStruct
    out = lambda r: shape((r, width), BF)
    return pl.pallas_call(
        lambda *refs: project_kernel(*refs, fan=fan),
        grid=(width // span,),
        in_specs=[pl.BlockSpec(memory_space=pltpu.SMEM)] + weight(0) + weight(1) + weight(2)
        + small(3 * part // 8) + small(3 * part // 8 + 1)
        + [whole((rows, width)), whole((2 * rows, 1))],
        out_specs=[cols(rows)] * 3 + [cols(2 * rows)] * 2
        + [whole((16, width)), pl.BlockSpec((3, STRIPES, part, span), lambda p: (0, 0, 0, p)),
           whole((2 * rows, buckets)), whole((width, rows)), whole((width, buckets))],
        out_shape=[out(rows)] * 3 + [out(2 * rows)] * 2
        + [shape((16, width), F32), shape((3, STRIPES, part, width), BF), shape((2 * rows, buckets), BF),
           shape((width, rows), BF), shape((width, buckets), BF)],
        scratch_shapes=[pltpu.VMEM((STRIPES, 8, width), BF)] * 2,
        compiler_params=big(),
        cost_estimate=cost(4 << 30, 12 << 20),
        name="project",
    )(where, *([near, far] * 5), x, bucket_column)


def normal_parts(hidden):
    centered = hidden - jnp.mean(hidden, axis=-1, keepdims=True)
    inverse = lax.rsqrt(jnp.mean(centered * centered, axis=-1, keepdims=True) + EPSILON)
    return centered * inverse, inverse


def normal_back(upstream, normed, inverse, gain):
    scaled = upstream * gain
    return inverse * (
        scaled
        - jnp.mean(scaled, axis=-1, keepdims=True)
        - normed * jnp.mean(scaled * normed, axis=-1, keepdims=True)
    )


def halves_to(keep_ref, send_ref, grad, own):
    part = keep_ref.shape[1]
    blocks = grad.reshape((grad.shape[0] // (2 * part), 2, part, grad.shape[1]))
    even, odd = blocks[:, 0].astype(BF), blocks[:, 1].astype(BF)

    @pl.when(own == 0)
    def _():
        keep_ref[...] = even
        send_ref[...] = odd

    @pl.when(own != 0)
    def _():
        keep_ref[...] = odd
        send_ref[...] = even


def feed_forward_kernel(vecs_ref, ctx_hbm, x_hbm, cot_hbm, packed_hbm,
                        out_hbm, outer_hbm, slope_hbm, og_hbm, low_hbm, n1_hbm, inv_hbm, second_hbm, vg_ref,
                        ctx, x, cot, wo, wi, w2, act, slope, low, og, n1, inv, acc, out, stage,
                        fetch, chunk_fetch, flush, slope_flush, outer_flush, *, fan):
    rows, width = ctx.shape
    part = width // STRIPES
    vec = lambda i: vecs_ref[i : i + 1, :]
    column = lambda a: jnp.sum(a, axis=0, keepdims=True)
    copy = pltpu.make_async_copy
    ins = [copy(ctx_hbm, ctx, fetch.at[0]),
           copy(packed_hbm.at[:, pl.ds(2 * fan * part, part), :], wo, fetch.at[1]),
           copy(x_hbm, x, fetch.at[2]), copy(cot_hbm, cot, fetch.at[3])]

    def chunk_copies(f):
        inner = pl.ds(pl.multiple_of((fan + f) * part, 8), part)
        outer = pl.ds(f * (STRIPES // fan), STRIPES // fan)
        return (copy(packed_hbm.at[:, inner, :], wi.at[f], chunk_fetch.at[0, f]),
                copy(packed_hbm.at[outer, pl.ds(0, fan * part), :], w2.at[f], chunk_fetch.at[1, f]))

    for one in ins[:3]:
        one.start()
    for f in range(fan):
        for one in chunk_copies(f):
            one.start()
    ins[3].start()
    outs = [copy(n1, n1_hbm, flush.at[0]), copy(inv, inv_hbm, flush.at[1]), copy(low, low_hbm, flush.at[2]),
            copy(out, out_hbm, flush.at[3]), copy(acc, second_hbm, flush.at[4]), copy(og, og_hbm, flush.at[5])]
    vg_ref[...] = jnp.zeros_like(vg_ref)
    ins[0].wait()
    ins[1].wait()
    attended = dot(ctx[...], wo.reshape(width, width)[...], NN) + vec(3)
    ins[2].wait()
    normed, inverse = normal_parts(x[...].astype(F32) + attended)
    n1[...] = normed
    inv[...] = jnp.broadcast_to(inverse, inv.shape)
    start = normed * vec(4) + vec(5)
    low[...] = start.astype(BF)
    acc[...] = start + vec(6)
    for one in outs[:3]:
        one.start()

    def slope_copy(f):
        return copy(slope.at[f], slope_hbm.at[f], slope_flush.at[f])

    def forward(f, carry):
        for one in chunk_copies(f):
            one.wait()
        pre = dot(low[...], wi.at[f].reshape(width, width)[...], NN) + vecs_ref[pl.ds(9 + f, 1), :]
        half = 0.5 + 0.5 * lax.erf(pre * 0.7071067811865476)
        active = (pre * half).astype(BF)
        act[f] = active
        slope[f] = (half + pre * (jnp.exp(-0.5 * pre * pre) * 0.3989422804014327)).astype(BF)
        slope_copy(f).start()
        acc[...] += dot(active, w2.at[f].reshape(width, width)[...], NN)
        return carry

    lax.fori_loop(0, fan, forward, 0)
    normed, inverse = normal_parts(acc[...])
    out[...] = (normed * vec(7) + vec(8)).astype(BF)
    outs[3].start()
    ins[3].wait()
    upstream = cot[...].astype(F32)
    vg_ref[8:9, :] = column(upstream * normed)
    vg_ref[9:10, :] = column(upstream)
    second = normal_back(upstream, normed, inverse, vec(7))
    acc[...] = second
    outs[4].start()
    og[...] = second.astype(BF)
    outs[5].start()
    vg_ref[10:11, :] = column(og[...].astype(F32))

    def outer_copy(f):
        return copy(stage.at[f % 2], outer_hbm.at[pl.ds(pl.multiple_of(f * width, 8), width), :],
                    outer_flush.at[f % 2])

    def outer_grad(f, carry):
        @pl.when(f >= 2)
        def _():
            outer_copy(f - 2).wait()

        stage[f % 2] = dot(act[f], og[...], TN).astype(BF)
        outer_copy(f).start()
        return carry

    lax.fori_loop(0, fan, outer_grad, 0)
    for one in outs:
        one.wait()
    for f in range(fan):
        slope_copy(f).wait()
    for f in (fan - 2, fan - 1):
        outer_copy(f).wait()


def feed_forward(vecs, ctx, x, cot, packed, fan):
    rows, width = x.shape
    part = width // STRIPES
    shape = jax.ShapeDtypeStruct
    hbm = pl.BlockSpec(memory_space=pl.ANY)
    vmem = pl.BlockSpec(memory_space=pltpu.VMEM)
    low, high = pltpu.VMEM((rows, width), BF), pltpu.VMEM((rows, width), F32)
    sem = pltpu.SemaphoreType.DMA
    return pl.pallas_call(
        lambda *refs: feed_forward_kernel(*refs, fan=fan),
        in_specs=[vmem] + [hbm] * 4,
        out_specs=[hbm] * 8 + [vmem],
        out_shape=[shape((rows, width), BF), shape((fan * width, width), BF), shape((fan, rows, width), BF),
                   shape((rows, width), BF), shape((rows, width), BF), shape((rows, width), F32),
                   shape((rows, 128), F32), shape((rows, width), F32), shape((16, width), F32)],
        scratch_shapes=[low, low, low, pltpu.VMEM((STRIPES, part, width), BF),
                        pltpu.VMEM((fan, STRIPES, part, width), BF),
                        pltpu.VMEM((fan, STRIPES // fan, part * fan, width), BF),
                        pltpu.VMEM((fan, rows, width), BF), pltpu.VMEM((fan, rows, width), BF), low, low,
                        high, pltpu.VMEM((rows, 128), F32), high, low, pltpu.VMEM((2, width, width), BF),
                        sem((4,)), sem((2, fan)), sem((6,)), sem((fan,)), sem((2,))],
        compiler_params=big(),
        name="feed_forward",
    )(vecs, ctx, x, cot, packed)


def feed_back_kernel(where_ref, vecs_ref, vg_in_ref, og_hbm, low_hbm, slope_hbm, second_hbm, n1_hbm, inv_hbm,
                     ctx_hbm, packed_hbm, keep_ref, send_ref, cg_hbm, fg_hbm, vg_ref,
                     og, low, slope, acc, n1, inv, ctx, wo, wi, w2, turned, cg, fg,
                     fetch, chunk_fetch, flush, *, fan):
    rows, width = ctx.shape
    part = width // STRIPES
    own = where_ref[1]
    column = lambda a: jnp.sum(a, axis=0, keepdims=True)
    copy = pltpu.make_async_copy

    def chunk_copies(f):
        inner = pl.ds(pl.multiple_of((fan + f) * part, 8), part)
        outer = pl.ds(f * (STRIPES // fan), STRIPES // fan)
        return (copy(packed_hbm.at[outer, pl.ds(0, fan * part), :], w2.at[f], chunk_fetch.at[0, f]),
                copy(slope_hbm.at[f], slope.at[f], chunk_fetch.at[1, f]),
                copy(packed_hbm.at[:, inner, :], wi.at[f], chunk_fetch.at[2, f]))

    ins = [copy(og_hbm, og, fetch.at[0]), copy(low_hbm, low, fetch.at[1]), copy(second_hbm, acc, fetch.at[2]),
           copy(ctx_hbm, ctx, fetch.at[3]), copy(n1_hbm, n1, fetch.at[4]), copy(inv_hbm, inv, fetch.at[5]),
           copy(packed_hbm.at[:, pl.ds(2 * fan * part, part), :], wo, fetch.at[6])]
    for one in [ins[0], *chunk_copies(0), ins[1], ins[2]]:
        one.start()
    for f in range(1, fan):
        for one in chunk_copies(f):
            one.start()
    for one in ins[3:]:
        one.start()
    vg_ref[...] = vg_in_ref[...]
    ins[1].wait()
    turned[...] = low[...].T
    ins[0].wait()
    ins[2].wait()

    def leave(f, grad):
        place = pl.ds(pl.multiple_of(f * part, 8), part)
        halves_to(keep_ref.at[:, place], send_ref.at[:, place], grad, own)

    def backward(f, carry):
        for one in chunk_copies(f):
            one.wait()
        grad = dot(og[...], w2.at[f].reshape(width, width)[...], NT) * slope[f].astype(F32)
        ig = grad.astype(BF)
        acc[...] += dot(ig, wi.at[f].reshape(width, width)[...], NT)
        vg_ref[pl.ds(f, 1), :] = column(ig.astype(F32))
        leave(f, dot(turned[...], ig, NN))
        return carry

    lax.fori_loop(0, fan, backward, 0)
    for one in ins[3:]:
        one.wait()
    total, normed = acc[...], n1[...]
    grad = normal_back(total, normed, inv[:, 0:1], vecs_ref[4:5, :])
    ag = grad.astype(BF)
    leave(fan, dot(ctx[...], ag, TN))
    cg[...] = dot(ag, wo.reshape(width, width)[...], NT).astype(BF)
    fg[...] = grad
    outs = [copy(cg, cg_hbm, flush.at[0]), copy(fg, fg_hbm, flush.at[1])]
    for one in outs:
        one.start()
    vg_ref[4:5, :] = column(total * normed)
    vg_ref[5:6, :] = column(total)
    vg_ref[6:7, :] = column(ag.astype(F32))
    for one in outs:
        one.wait()


def feed_back(where, vecs, vg, og, low, slope, second, n1, inv, ctx, packed, fan):
    rows, width = ctx.shape
    part = width // STRIPES
    shape = jax.ShapeDtypeStruct
    hbm = pl.BlockSpec(memory_space=pl.ANY)
    vmem = pl.BlockSpec(memory_space=pltpu.VMEM)
    half = shape((STRIPES // 2, part * (fan + 1), width), BF)
    thin, wide = pltpu.VMEM((rows, width), BF), pltpu.VMEM((rows, width), F32)
    sem = pltpu.SemaphoreType.DMA
    return pl.pallas_call(
        lambda *refs: feed_back_kernel(*refs, fan=fan),
        in_specs=[pl.BlockSpec(memory_space=pltpu.SMEM), vmem, vmem] + [hbm] * 8,
        out_specs=[vmem, vmem, hbm, hbm, vmem],
        out_shape=[pltpu.VMEM(half.shape, half.dtype)] * 2 + [shape((rows, width), BF), shape((rows, width), F32), shape(vg.shape, F32)],
        scratch_shapes=[thin, thin, pltpu.VMEM((fan, rows, width), BF), wide, wide,
                        pltpu.VMEM((rows, 128), F32), thin, pltpu.VMEM((STRIPES, part, width), BF),
                        pltpu.VMEM((fan, STRIPES, part, width), BF),
                        pltpu.VMEM((fan, STRIPES // fan, part * fan, width), BF),
                        pltpu.VMEM((width, rows), BF), thin, wide]
        + [sem((7,)), sem((3, fan)), sem((2,))],
        compiler_params=big(44),
        name="feed_back",
    )(where, vecs, vg, *[pltpu.with_memory_space_constraint(a, pltpu.HBM)
                         for a in (og, low, slope, second, n1, inv, ctx, packed)])


def cut(row, mine, marks):
    return dot(jnp.where(mine, jnp.broadcast_to(row, mine.shape), 0.0).astype(BF), marks, NT)


def cut_vectors_kernel(vg_ref, vec_ref, *, fan):
    width = vg_ref.shape[1]
    vec_ref[...] = jnp.zeros_like(vec_ref)
    whole = stripe_marks(width, BF)
    for i, at in enumerate((6, 4, 5, 10, 8, 9), 3):
        lanes = slice(0, 128) if i < 8 else slice(128, 256)
        vec_ref[:, i % 8, lanes] = cut(vg_ref[at : at + 1, :], *whole)
    broad = width * fan // STRIPES
    total = jnp.zeros((STRIPES, 128), F32)
    for f in range(fan):
        column_at = lax.broadcasted_iota(jnp.int32, (STRIPES, width), 1) + f * width
        stripe = lax.broadcasted_iota(jnp.int32, (STRIPES, width), 0)
        mine = (column_at >= stripe * broad) & (column_at < stripe * broad + broad)
        place = lax.broadcasted_iota(jnp.int32, (128, width), 0)
        marks = lax.broadcasted_iota(jnp.int32, (128, width), 1) + f * width
        total += cut(vg_ref[f : f + 1, :], mine, (marks % broad == place).astype(BF))
    vec_ref[:, (VECTORS - 1) % 8, 128:256] = total


def cut_vectors(vg, fan):
    return pl.pallas_call(
        lambda *refs: cut_vectors_kernel(*refs, fan=fan),
        out_shape=jax.ShapeDtypeStruct((STRIPES, 8, vg.shape[1]), F32),
        compiler_params=big(24),
        cost_estimate=pl.CostEstimate(flops=100000000000, bytes_accessed=1000000, transcendentals=0),
        name="cut_vectors",
    )(vg)


def project_back_kernel(where_ref, vec_in_ref, w, xt, tt, d_hbm, pos_hbm, *refs, fan, hops):
    keep_ref, send_ref = refs[hops : hops + 2]
    d, pos, vec_ref, grad_ref, line_ref, table_ref, chunk_fetch = refs[-7:]
    width, rows = xt.shape
    buckets = tt.shape[1]
    part = width // STRIPES
    own = where_ref[1]
    copy = pltpu.make_async_copy

    def fetch_d(i):
        return copy(d_hbm.at[i], d.at[i], chunk_fetch.at[0, i])

    def fetch_pos(i):
        return copy(pos_hbm.at[i], pos.at[i], chunk_fetch.at[1, i])

    for one in (fetch_d(0), fetch_pos(0), fetch_d(1), fetch_pos(1), fetch_d(2)):
        one.start()
    for r, out in enumerate(refs[hops + 2 : -7]):
        at = where_ref[3] ^ r
        row = 0
        for ref, got in (refs[0:2], refs[2:4])[: hops // 2]:
            rows_here = ref.shape[1]
            out[0, row : row + rows_here] = (ref[at].astype(F32) + got[at].astype(F32)).astype(BF)
            row += rows_here
    vec_ref[...] = vec_in_ref[...]
    table_ref[...] = jnp.zeros_like(table_ref)

    def project(i, carry):
        fetch_d(i).wait()
        grad_ref[...] = dot(xt[...], d[i], NN)
        line_ref[i] = dot(jnp.ones((8, rows), BF), d[i], NN)

        @pl.when(i < 2)
        def _():
            fetch_pos(i).wait()
            grad_ref[...] += dot(tt[...], pos[i], NT)
            line_ref[i] += dot(jnp.ones((8, buckets), BF), pos[i], NT)
            table_ref[...] += dot(w.at[i].reshape(width, width)[...], pos[i], NN)

        place = pl.ds(pl.multiple_of(i * part, 8), part)
        halves_to(keep_ref.at[:, place], send_ref.at[:, place], grad_ref[...], own)
        return carry

    lax.fori_loop(0, 3, project, 0)
    marks = stripe_marks(width, BF)
    for i in range(3):
        vec_ref[:, i, 0:128] = cut(line_ref[i, 0:1], *marks)
    table_at, vector_at = slice(3 * part, 3 * part + 8), slice(3 * part + 8, 3 * part + 16)
    halves_to(keep_ref.at[:, table_at], send_ref.at[:, table_at], table_ref[...].T, own)
    halves_to(keep_ref.at[:, vector_at], send_ref.at[:, vector_at], vec_ref[...].reshape(STRIPES * 8, width), own)


def project_back(where, d, pos, mats, xt, tt, vec, fan, parts=()):
    width, rows = xt.shape
    part = width // STRIPES
    buckets = tt.shape[1]
    hbm = pl.BlockSpec(memory_space=pl.ANY)
    vmem = pl.BlockSpec(memory_space=pltpu.VMEM)
    half = jax.ShapeDtypeStruct((STRIPES // 2, part * 3 + 16, width), BF)
    sem = pltpu.SemaphoreType.DMA
    return pl.pallas_call(
        lambda *refs: project_back_kernel(*refs, fan=fan, hops=len(parts)),
        in_specs=[pl.BlockSpec(memory_space=pltpu.SMEM)] + [vmem] * 4 + [hbm] * 2 + [vmem] * len(parts),
        out_specs=[vmem, vmem] + [vmem] * len(parts),
        out_shape=[pltpu.VMEM(half.shape, half.dtype), pltpu.VMEM(half.shape, half.dtype)]
        + [jax.ShapeDtypeStruct((1, sum(part_.shape[1] for part_ in parts[::2]), width), BF)] * len(parts),
        scratch_shapes=[pltpu.VMEM((3, rows, width), BF), pltpu.VMEM((2, width, buckets), BF),
                        pltpu.VMEM((STRIPES, 8, width), F32), pltpu.VMEM((width, width), F32),
                        pltpu.VMEM((3, 8, width), F32), pltpu.VMEM((width, buckets), F32), sem((2, 3))],
        compiler_params=big(32),
        name="project_back",
    )(where, vec, *[pltpu.with_memory_space_constraint(a, pltpu.VMEM) for a in (mats, xt, tt)],
      *[pltpu.with_memory_space_constraint(a, pltpu.HBM) for a in (d, pos)], *parts)


def token_grad_kernel(fg_ref, d_ref, w_ref, out_ref):
    width = out_ref.shape[1]

    @pl.when(pl.program_id(0) == 0)
    def _():
        out_ref[...] = fg_ref[...]

    out_ref[...] += dot(d_ref[0], w_ref.at[0].reshape(width, width)[...], NT)


def token_grads(fg, d, mats):
    rows, width = fg.shape
    full = pl.BlockSpec((rows, width), lambda g: (0, 0))
    return pl.pallas_call(
        token_grad_kernel,
        grid=(3,),
        in_specs=[full, pl.BlockSpec((1, rows, width), lambda g: (g, 0, 0)),
                  pl.BlockSpec((1,) + mats.shape[1:], lambda g: (g, 0, 0, 0))],
        out_specs=full,
        out_shape=jax.ShapeDtypeStruct((rows, width), F32),
        compiler_params=big(24),
        cost_estimate=cost(2 << 30, 10 << 20),
        name="token_grads",
    )(fg, d, mats)


def near_hop_kernel(where_ref, *refs, groups):
    keeps, gots, outs = refs[:groups], refs[groups : 2 * groups], refs[2 * groups :]
    for r, out in enumerate(outs):
        at = where_ref[2] ^ r
        row = 0
        for keep_ref, got_ref in zip(keeps, gots):
            rows = keep_ref.shape[1]
            out[0, row : row + rows] = (keep_ref[at].astype(F32) + got_ref[at].astype(F32)).astype(BF)
            row += rows


def near_hop(where, keep, got):
    count, _, width = keep[0].shape
    group = lambda block: pl.BlockSpec((4,) + block.shape[1:], lambda z: (z, 0, 0))
    rows = sum(block.shape[1] for block in keep)
    return pl.pallas_call(
        lambda *refs: near_hop_kernel(*refs, groups=len(keep)),
        grid=(count // 4,),
        in_specs=[pl.BlockSpec(memory_space=pltpu.SMEM)] + [group(block) for block in keep] * 2,
        out_specs=[pl.BlockSpec((1, rows, width), lambda z: (z, 0, 0))] * 4,
        out_shape=[jax.ShapeDtypeStruct((count // 4, rows, width), BF)] * 4,
        compiler_params=big(16),
        name="near_hop",
    )(where, *keep, *got)


def finish_kernel(*refs, parts, vectors):
    ins, outer_ref, mats, lines = refs[:parts], refs[parts], refs[parts + 1 : -vectors - 1], refs[-vectors - 1 : -1]
    refs[-1][...] = outer_ref[0].astype(F32)
    add = lambda rows: sum(ref[0, rows, :].astype(F32) for ref in ins)
    at = 0
    for ref in mats:
        ref[...] = add(slice(at, at + ref.shape[0]))
        at += ref.shape[0]
    tile = add(slice(at, at + 8))
    for i, ref in enumerate(lines):
        lane = 0 if i < 8 else 128
        ref[...] = tile[i % 8, lane : lane + ref.shape[0]]


def finish(parts, outer, mat_rows, sizes):
    width = parts[0].shape[2]
    return pl.pallas_call(
        lambda *refs: finish_kernel(*refs, parts=len(parts), vectors=len(sizes)),
        out_shape=[jax.ShapeDtypeStruct((rows, width), F32) for rows in mat_rows]
        + [jax.ShapeDtypeStruct((size,), F32) for size in sizes]
        + [jax.ShapeDtypeStruct(outer.shape[1:], F32)],
        compiler_params=big(16),
        name="finish",
    )(*parts, outer)


def first_turn_kernel(where_ref, keep_ref, got_ref, a_keep, a_send, b_keep, b_send):
    y, x = where_ref[2] & 1, where_ref[2] >> 1
    cut = a_keep.shape[1]
    first, second = slice(0, cut), slice(cut, keep_ref.shape[1])
    add = lambda at, rows: (keep_ref[at, rows, :].astype(F32) + got_ref[at, rows, :].astype(F32)).astype(BF)
    for i in range(2):
        a_keep[i] = add(i * 2 + y, first)
        a_send[i] = add(i * 2 + 1 - y, first)
        b_keep[i] = add(x * 2 + i, second)
        b_send[i] = add((1 - x) * 2 + i, second)


def first_turn(where, keep, got, cut):
    count, rows, width = keep.shape
    group = pl.BlockSpec((4, rows, width), lambda z: (z, 0, 0))
    parts = (cut, cut, rows - cut, rows - cut)
    return pl.pallas_call(
        first_turn_kernel,
        grid=(count // 4,),
        in_specs=[pl.BlockSpec(memory_space=pltpu.SMEM), group, group],
        out_specs=[pl.BlockSpec((2, part, width), lambda z: (z, 0, 0)) for part in parts],
        out_shape=[jax.ShapeDtypeStruct((count // 2, part, width), BF) for part in parts],
        compiler_params=big(16),
        name="first_turn",
    )(where, keep, got)


def second_turn_kernel(where_ref, a_ref, a_got, b_ref, b_got, a_keep, a_send, b_keep, b_send):
    y, x = where_ref[2] & 1, where_ref[2] >> 1
    for ref, got, own, keep, send in ((a_ref, a_got, x, a_keep, a_send), (b_ref, b_got, y, b_keep, b_send)):
        for z in range(keep.shape[0]):
            for out, at in ((keep, z * 2 + own), (send, z * 2 + 1 - own)):
                out[z] = (ref[at].astype(F32) + got[at].astype(F32)).astype(BF)


def second_turn(where, a_keep, a_got, b_keep, b_got):
    vmem = pl.BlockSpec(memory_space=pltpu.VMEM)
    shape = lambda block: jax.ShapeDtypeStruct((block.shape[0] // 2,) + block.shape[1:], BF)
    return pl.pallas_call(
        second_turn_kernel,
        in_specs=[pl.BlockSpec(memory_space=pltpu.SMEM)] + [vmem] * 4,
        out_shape=[shape(a_keep)] * 2 + [shape(b_keep)] * 2,
        compiler_params=big(16),
        name="second_turn",
    )(where, a_keep, a_got, b_keep, b_got)


def far_hop_kernel(where_ref, *refs):
    for r, out in enumerate(refs[4:]):
        at = where_ref[3] ^ r
        out[0] = sum(ref[at].astype(F32) for ref in refs[:4]).astype(BF)


def far_hop(where, parts):
    count, rows, width = parts[0].shape
    return pl.pallas_call(
        far_hop_kernel,
        in_specs=[pl.BlockSpec(memory_space=pltpu.SMEM)] + [pl.BlockSpec(memory_space=pltpu.VMEM)] * 4,
        out_shape=[jax.ShapeDtypeStruct((1, rows, width), BF)] * 4,
        compiler_params=big(16),
        cost_estimate=cost(4 * parts[0].size, 10 * parts[0].size),
        name="far_hop",
    )(where, *parts)


def gather_rows(block):
    return lax.all_gather(block, AXES, axis=0, tiled=False)


def scatter_rows(blocks):
    return lax.psum_scatter(blocks, AXES, scatter_dimension=0, tiled=False)


def xor_permute(block, mask, count):
    return lax.ppermute(block, AXES, [(d, d ^ mask) for d in range(count)])


def in_vmem(block):
    return pltpu.with_memory_space_constraint(block, pltpu.VMEM)


class Scatter:
    def __init__(self, where, count, space):
        self.where, self.count, self.space = where, count, space
        self.keep, self.got = [], []

    def add(self, keep, send):
        self.keep.append(keep)
        self.got.append(xor_permute(send, 1, self.count))

    def near(self, *after):
        got = tie(self.got, after)
        keep = [pltpu.with_memory_space_constraint(part, self.space) for part in self.keep]
        parts = near_hop(self.where, keep, [in_vmem(part) for part in got])
        self.keep, self.sent = parts[0], parts[1:]
        self.got = [xor_permute(part, 2 * r, self.count) for r, part in enumerate(self.sent, 1)]

    def far(self, *after):
        got = tie(self.got, after)
        parts = far_hop(self.where, [self.keep] + [in_vmem(part) for part in got])
        self.keep, self.sent = parts[0], parts[1:]
        self.got = [xor_permute(part, 8 * r, self.count) for r, part in enumerate(self.sent, 1)]

    def total(self):
        return sum(part[0].astype(F32) for part in [self.keep] + self.got)


def tie(value, other):
    if isinstance(other, tuple) and not other:
        return value
    return lax.optimization_barrier((value, other))[0]


def scatter_plain(keep, send, parts, count):
    blocks = jnp.stack([keep, send], axis=1).reshape((STRIPES,) + keep.shape[1:])
    sums, at = [], 0
    for part in parts:
        whole = blocks[:, at : at + part]
        rows = STRIPES * part
        flat = whole.reshape(count, rows // count, whole.shape[2])
        sums.append(lax.psum_scatter(flat.astype(F32), AXES, scatter_dimension=0, tiled=False))
        at += part
    return sums


def make_body(counts):
    count = counts[0] * counts[1]
    direct = counts == (8, 4)

    def body(
        tokens, lengths, buckets,
        query_weight, query_bias, key_weight, key_bias, value_weight, value_bias,
        output_weight, output_bias, relative_table, first_gain, first_shift,
        inner_weight, inner_bias, outer_weight, outer_bias, second_gain, second_shift,
        cotangent,
    ):
        rows, width = tokens.shape[1:]
        fan = inner_weight.shape[1] // width
        vectors = (
            query_bias, key_bias, value_bias, output_bias, first_gain, first_shift,
            outer_bias, second_gain, second_shift, inner_bias,
        )
        first_mats = (query_weight, key_weight, value_weight, relative_table)
        second_mats = [outer_weight]
        second_mats += [inner_weight[:, f * width : (f + 1) * width] for f in range(fan)]
        second_mats += [output_weight]

        def vector_rows(pieces):
            lead = pieces[0].shape[:-1]
            tile = jnp.zeros(lead + (8, width), BF)
            for i, piece in enumerate(pieces):
                lane = 0 if i < 8 else 128
                tile = tile.at[..., i % 8, lane : lane + piece.shape[-1]].set(piece)
            return tile

        me = lax.axis_index("wide") * counts[1] + lax.axis_index("narrow")
        if direct:
            first_pack, second_pack = pack(first_mats, vectors, outer_weight, inner_weight, output_weight, fan)
            second_all = gather_rows(second_pack)
            everyone = lambda block, step: jnp.concatenate(
                [block] + [xor_permute(block, step * r, count) for r in (1, 2, 3)]
            )
            near = everyone(everyone(first_pack[None], 8), 2)
            far = xor_permute(near, 1, count)
            where = jnp.stack([me, me & 1, (me >> 1) & 3, me >> 3]).astype(jnp.int32)
        else:
            whole = lambda block: lax.all_gather(block, AXES, axis=0, tiled=True)
            striped = lambda block: whole(block).reshape(STRIPES, -1, width)
            spread = [whole(v).reshape(STRIPES, -1) for v in vectors]
            first_all = jnp.concatenate(
                [striped(m) for m in first_mats] + [vector_rows(spread)], axis=1
            )
            second_all = jnp.concatenate([striped(m) for m in second_mats], axis=1)
            first_all = first_all.reshape((4, 4, 2) + first_all.shape[1:]).transpose(2, 1, 0, 3, 4)
            near, far = first_all.reshape((2, STRIPES // 2) + first_all.shape[3:])
            where = jnp.zeros((4,), jnp.int32)

        flat = tokens.reshape(rows, width)
        bucket_column = jnp.pad(buckets[::-1], (0, 1), constant_values=-1).reshape(-1, 1)
        q, k, v, kr, qr, vecs, mats, onehot, xt, tt = project_all(where, near, far, flat, bucket_column, fan)
        total = lengths[0, 0:1] + lengths[0, 1:2]
        context, probs = attend(total, q, k, v, kr, qr)
        cot = cotangent.reshape(rows, width)
        layer_out, outer_grad, slope, og, low, n1, inv, second, vg = feed_forward(
            vecs, context, flat, cot, second_all, fan
        )
        outer_blocks = outer_grad.reshape(count, -1, width)
        if direct:
            outer_sum = scatter_rows(outer_blocks)
        else:
            outer_out = scatter_rows(outer_blocks.astype(F32))
        inner_keep, inner_send, context_grad, fg, vg = feed_back(
            where, vecs, vg, og, low, slope, second, n1, inv, context, second_all, fan
        )
        vec = cut_vectors(vg, fan)
        if direct:
            inner = Scatter(where, count, pltpu.HBM)
            inner_got = tie(xor_permute(inner_send, 1, count), vec)
            inner_keep = in_vmem(inner_keep)
            a_keep, a_send, b_keep, b_send = first_turn(where, inner_keep, in_vmem(inner_got), 64)
            a_got, b_got = xor_permute(a_send, 2, count), xor_permute(b_send, 4, count)
            context_grad = tie(context_grad, (a_send, b_send))
        most = width // 128 // 2
        back = lambda dc, first, pairs, before: attend_back(
            q, k, v, kr, qr, dc, probs, onehot, first, pairs, before
        )
        grads = back(context_grad, 0, most, ())
        if direct:
            a_got, b_got = tie((a_got, b_got), grads[0])
            a_keep, a_send, b_keep, b_send = second_turn(where, a_keep, in_vmem(a_got), b_keep, in_vmem(b_got))
            a_got, b_got = xor_permute(a_send, 4, count), xor_permute(b_send, 2, count)
            context_grad = tie(context_grad, (a_send, b_send))
        d, pos = back(context_grad, most, width // 128 - most, grads)
        if direct:
            parts = [a_keep, in_vmem(a_got), b_keep, in_vmem(b_got)]
            last_keep, last_send, *parts = project_back(where, d, pos, mats, xt, tt, vec, fan, parts)
            inner.keep = parts[0]
            inner_sent = parts[1:]
        else:
            last_keep, last_send = project_back(where, d, pos, mats, xt, tt, vec, fan)

        part = width // STRIPES
        if direct:
            last = Scatter(where, count, pltpu.VMEM)
            last.add(last_keep, last_send)
            last.near()
            inner_sent[2] = tie(inner_sent[2], last.sent)
            inner.got = [xor_permute(part, 8 * r, count) for r, part in enumerate(inner_sent, 1)]
            tokens_grad = token_grads(fg, tie(d, last.sent), mats)
            last.far(tokens_grad)
            inner.got = tie(inner.got, tokens_grad)
            inner_sum = inner.total()
            inner_parts = [inner_sum[f * part : (f + 1) * part] for f in range(fan + 1)]
            output_out = inner_parts[fan]
            query_out, key_out, value_out, table_out, *pieces, outer_out = finish(
                [last.keep] + [in_vmem(got) for got in last.got],
                outer_sum[None], (part, part, part, 8), [piece.shape[0] for piece in vectors],
            )
        else:
            tokens_grad = token_grads(fg, d, mats)
            inner_parts = scatter_plain(inner_keep, inner_send, (part,) * (fan + 1), count)
            output_out = inner_parts[fan]
            query_out, key_out, value_out, table_out, _ = scatter_plain(
                last_keep, last_send, (part,) * 3 + (8, 8), count
            )
            blocks = jnp.stack([last_keep, last_send], axis=1).reshape(STRIPES, -1, width)
            tile = blocks[:, 3 * part + 8 : 3 * part + 16].astype(F32)
            pieces = []
            for i, piece in enumerate(vectors):
                lane = 0 if i < 8 else 128
                length = piece.shape[0] * count // STRIPES
                line = tile[:, i % 8, lane : lane + length].reshape(-1)
                pieces.append(lax.psum_scatter(line, AXES, scatter_dimension=0, tiled=True))
        inner_out = jnp.concatenate(inner_parts[:fan], axis=1)
        (qb, kb, vb, ob, g1, s1, outb, g2, s2, inb) = pieces
        return (
            layer_out.reshape(tokens.shape), tokens_grad.reshape(tokens.shape),
            query_out, qb, key_out, kb, value_out, vb, output_out, ob, table_out, g1, s1,
            inner_out, inb, outer_out, outb, g2, s2,
        )

    return body


def solution(mesh):
    counts = (mesh.shape["wide"], mesh.shape["narrow"])
    rows3, rows2, rows1 = P(AXES, None, None), P(AXES, None), P(AXES)
    params = (
        rows2, rows1, rows2, rows1, rows2, rows1, rows2, rows1, rows2, rows1, rows1,
        rows2, rows1, rows2, rows1, rows1, rows1,
    )
    return jax.shard_map(
        make_body(counts),
        mesh=mesh,
        in_specs=(rows3, rows2, P()) + params + (rows3,),
        out_specs=(rows3, rows3) + params,
        check_vma=False,
    )
```
